32 devices in a mesh: seq: 8 (over z, y), row: 4 (over x, core).
Axes of the slice: x: 2, y: 2, z: 4, core: 2. Of those that a mesh axis runs over, the one named last changes fastest.
Arguments:
- hidden_in: bfloat16 [8, 4096, 1024], P('row', 'seq'), may hold values from -6 to 6
- mixer_gain: bfloat16 [1024], replicated, may hold values from 0.099609375 to 1.8984375
- in_weight: bfloat16 [1024, 3072], replicated, may hold values from -0.1875 to 0.1875
- conv_kernel: bfloat16 [1024, 3], replicated, may hold values from -2.5 to 2.5
- out_weight: bfloat16 [1024, 1024], replicated, may hold values from -0.1875 to 0.1875
- feed_gain: bfloat16 [1024], replicated, may hold values from 0.099609375 to 1.8984375
- gate_weight: bfloat16 [1024, 4608], replicated, may hold values from -0.1875 to 0.1875
- up_weight: bfloat16 [1024, 4608], replicated, may hold values from -0.1875 to 0.1875
- down_weight: bfloat16 [4608, 1024], replicated, may hold values from -0.1875 to 0.1875
- document_lengths: int32 [8, 16], P('row'), may hold values from 1 to 1024, 4096 in all within a row
- valid_tokens: int32 [8], P('row'), may hold values from 3687 to 4096, as said below
- cotangent: bfloat16 [8, 4096, 1024], P('row', 'seq'), may hold values from -6 to 6
Outputs:
- output: bfloat16 [8, 4096, 1024], P('row', 'seq')
- input_grad: bfloat16 [8, 4096, 1024], P('row', 'seq')
- mixer_gain_grad: float32 [1024], P('seq')
- in_weight_grad: float32 [1024, 3072], P('seq', 'row')
- conv_kernel_grad: float32 [1024, 3], P('seq')
- out_weight_grad: float32 [1024, 1024], P('seq', 'row')
- feed_gain_grad: float32 [1024], P('seq')
- gate_weight_grad: float32 [1024, 4608], P('seq', 'row')
- up_weight_grad: float32 [1024, 4608], P('seq', 'row')
- down_weight_grad: float32 [4608, 1024], P('seq', 'row')
The draws below stay inside these ranges and needn't reach their ends.
Inputs may be any that keep to these rules, and one draw needn't show every extreme that they name: Positions from valid_tokens on are padding at the end of a row; some row is full and some row holds exactly 3687 valid positions.
All inputs are finite; a program needn't handle non-finite values.
Results may differ from the reference program's by a relative error of at most 0.015.
Values may be sent and summed in bfloat16 or wider, within the bound.
No kernel may reach another device: no remote copies, remote signals or barrier semaphores. Data moves between devices by JAX's collectives and lax.ppermute only.
A program may use at most 256 MiB of HBM per device.

```python
import math
import jax
import jax.numpy as jnp
import numpy as np
from jax import lax

D = 1024
FF = 4608
KS = 3
ROW_LEN = 4096
NDOC = 16
DOC_MOST = 1024
ROWS = 8


def draw_valid_tokens(key, part):
    least = ROW_LEN - ROW_LEN // 10
    drawn = jax.random.randint(key, (ROWS,), least, ROW_LEN + 1, dtype=jnp.int32)
    return drawn.at[0].set(ROW_LEN).at[1].set(least)


def shard_levels(key, dims, split, smallest, top_value):
    level, own = 1.0, jax.random.fold_in(key, 6)
    for axis_at, blocks in split:
        draws = jnp.exp(jax.random.uniform(jax.random.fold_in(own, axis_at), (blocks,), jnp.float32, smallest / len(split), top_value / len(split)))
        level = level * jnp.repeat(draws, dims[axis_at] // blocks).reshape([-1 if axis == axis_at else 1 for axis in range(len(dims))])
    return level


def profile(amount, total, most, skew):
    portions = [(1 << 20) // math.isqrt(standing ** skew) + 1 for standing in range(2, amount + 1)]
    rest, given = total - most - (amount - 1), [1] * (amount - 1)
    while rest > 0:
        candidates = [i for i in range(amount - 1) if given[i] < most]
        mass, budget = sum([portions[i] for i in candidates]), rest
        for i in candidates:
            more = min(most - given[i], max(1, budget * portions[i] // mass), rest)
            given[i] = given[i] + more
            rest = rest - more
    return np.array([most] + given)


def uneven_parts(rng, amount, total, limit, slope):
    if amount == 2:
        one = jax.random.randint(rng, (), max(1, total - limit), min(limit, total - 1) + 1)
        return jnp.stack([one, total - one])
    tallies = jnp.asarray(profile(amount, total, limit, slope), jnp.int32)
    twos = (amount - 1) // 2
    source_of, sink = tallies[1:1 + 2 * twos:2], tallies[2:2 + 2 * twos:2]
    slack = jnp.minimum(source_of - 1, limit - sink)
    shifted = jax.random.randint(jax.random.fold_in(rng, 1), (twos,), 0, 1 << 20) % (slack + 1)
    tallies = tallies.at[1:1 + 2 * twos:2].set(source_of - shifted).at[2:2 + 2 * twos:2].set(sink + shifted)
    return tallies[jax.random.permutation(jax.random.fold_in(rng, 2), amount)]


def normal_values(rng, extent, spread, reach, shards=(), held_as=jnp.bfloat16):
    factor_of = shard_levels(rng, extent, shards, -0.22, 0.18) if shards else 1.0
    values = jax.random.normal(rng, extent, jnp.float32) * spread * factor_of
    return jnp.minimum(jnp.maximum(values, -reach), reach).astype(held_as)


def setup_inputs(seed: int = 0) -> dict:
    arg_keys = jax.random.split(jax.random.key(seed), 13)
    return {
        "hidden_in": normal_values(arg_keys[0], (ROWS, ROW_LEN, D), 1.0, 6.0, ((0, 4), (1, 8))),
        "mixer_gain": jnp.clip(1.0 + 0.18 * jax.random.normal(arg_keys[1], (D,), jnp.float32), 0.099609375, 1.8984375).astype(jnp.bfloat16),
        "in_weight": normal_values(arg_keys[2], (D, 3 * D), D ** -0.5, 0.1875),
        "conv_kernel": normal_values(arg_keys[3], (D, KS), 0.5, 2.5),
        "out_weight": normal_values(arg_keys[4], (D, D), D ** -0.5, 0.1875),
        "feed_gain": jnp.clip(1.0 + 0.18 * jax.random.normal(arg_keys[5], (D,), jnp.float32), 0.099609375, 1.8984375).astype(jnp.bfloat16),
        "gate_weight": normal_values(arg_keys[6], (D, FF), D ** -0.5, 0.1875),
        "up_weight": normal_values(arg_keys[7], (D, FF), D ** -0.5, 0.1875),
        "down_weight": normal_values(arg_keys[8], (FF, D), (FF // 4) ** -0.5, 0.1875),
        "document_lengths": jax.vmap(lambda own: uneven_parts(own, NDOC, ROW_LEN, DOC_MOST, 1))(jax.random.split(arg_keys[9], ROWS)).reshape((ROWS, NDOC)).astype(jnp.int32),
        "valid_tokens": draw_valid_tokens(jax.random.fold_in(arg_keys[12], 71), 0),
        "cotangent": normal_values(arg_keys[11], (ROWS, ROW_LEN, D), 1.0, 6.0, ((0, 4), (1, 8))),
    }


EPS = 1e-05

@jax.custom_vjp
def low(v):
    return lax.optimization_barrier(v.astype(jnp.bfloat16)).astype(jnp.float32)

@jax.custom_vjp
def low_back(v):
    return v

def low_keep(v):
    return (low(v), None)

def low_pass(kept, grad):
    return (grad,)

def back_keep(v):
    return (v, None)

def back_low(kept, grad):
    return (low(grad),)
low.defvjp(low_keep, low_pass)
low_back.defvjp(back_keep, back_low)

def matmul(left, right):
    return jnp.dot(left, right, precision=lax.Precision.HIGHEST)

def forward(hidden, weight_set, keep_one, keep_two, valid_mask):
    mixer_gain, in_weight, conv_kernel, out_weight, feed_gain, gate_weight, up_weight, down_weight = weight_set
    width = hidden.shape[1]
    inverse_one = lax.rsqrt(lax.optimization_barrier(jnp.mean(hidden * hidden, axis=1, keepdims=True)) + EPS)
    normed = low(hidden * inverse_one * mixer_gain)
    project = low_back(matmul(normed, in_weight))
    input_gate = project[:, :width]
    output_gate = project[:, width:2 * width]
    values = project[:, 2 * width:]
    product = low(input_gate * values)
    padded = jnp.pad(product, ((2, 0), (0, 0)))
    conv_out = conv_kernel[:, 0] * padded[2:] + keep_one * conv_kernel[:, 1] * padded[1:-1] + keep_two * conv_kernel[:, 2] * padded[:-2]
    mixed_in = low(output_gate * conv_out)
    mixer_out = low_back(matmul(mixed_in, out_weight))
    residual = hidden + valid_mask * mixer_out
    inverse_two = lax.rsqrt(lax.optimization_barrier(jnp.mean(residual * residual, axis=1, keepdims=True)) + EPS)
    normed_two = low(residual * inverse_two * feed_gain)
    gate_pre = low_back(matmul(normed_two, gate_weight))
    up_pre = low_back(matmul(normed_two, up_weight))
    activation = low(jax.nn.silu(gate_pre) * up_pre)
    feed_out = low_back(matmul(activation, down_weight))
    return residual + valid_mask * feed_out

def reference(hidden_in, mixer_gain, in_weight, conv_kernel, out_weight, feed_gain, gate_weight, up_weight, down_weight, document_lengths, valid_tokens, cotangent):
    weights = tuple((weight_item.astype(jnp.float32) for weight_item in (mixer_gain, in_weight, conv_kernel, out_weight, feed_gain, gate_weight, up_weight, down_weight)))
    positions = jnp.arange(ROW_LEN, dtype=jnp.int32)

    def row_step(totals, row_items):
        row_hidden, row_lengths, row_valid, row_cotangent = row_items
        starts = (jnp.cumsum(row_lengths) - row_lengths).astype(jnp.int32)
        is_start = jnp.any(positions[:, None] == starts[None, :], axis=1)
        before = jnp.any((positions - 1)[:, None] == starts[None, :], axis=1)
        keep_one = (1.0 - is_start.astype(jnp.float32))[:, None]
        keep_two = keep_one * (1.0 - before.astype(jnp.float32))[:, None]
        valid_mask = (positions < row_valid).astype(jnp.float32)[:, None]

        def closure(hidden, weight_set):
            return forward(hidden, weight_set, keep_one, keep_two, valid_mask)
        result, pullback = jax.vjp(closure, row_hidden.astype(jnp.float32), weights)
        hidden_grad, weight_grads = pullback(row_cotangent.astype(jnp.float32))
        totals = jax.tree.map(jnp.add, totals, weight_grads)
        return (totals, (result.astype(jnp.bfloat16), hidden_grad.astype(jnp.bfloat16)))
    initial = tuple((jnp.zeros(weight_item.shape, jnp.float32) for weight_item in weights))
    totals, (output, input_grad) = lax.scan(row_step, initial, (hidden_in, document_lengths, valid_tokens, cotangent))
    return (output, input_grad, totals[0], totals[1], totals[2], totals[3], totals[4], totals[5], totals[6], totals[7])
```

```python
import jax
import jax.numpy as jnp
from jax import lax
from jax.experimental import pallas as pl
from jax.experimental.pallas import tpu as pltpu
from jax.sharding import PartitionSpec as P

EPS = 1e-05


def passed_along(value, axis, by):
    length = lax.axis_size(axis)
    pairs = [(i, i + by) for i in range(length) if 0 <= i + by < length]
    return lax.ppermute(value, axis, pairs)


def contract_rows(left, right):
    return lax.dot_general(
        left, right, (((0,), (0,)), ((), ())), preferred_element_type=jnp.float32
    )


def contract_cols(left, right):
    return lax.dot_general(
        left, right, (((1,), (1,)), ((), ())), preferred_element_type=jnp.float32
    )


def swapped(value, axis, bit):
    length = lax.axis_size(axis)
    return lax.ppermute(value, axis, [(i, i ^ bit) for i in range(length)])


def wide(left, right):
    return left.astype(jnp.float32) + right.astype(jnp.float32)


def narrow(value):
    return value.astype(jnp.bfloat16)


def feed_chunk(place, own_in, other_in, own_grad, other_grad, gate_weight, up_weight, down_weight, chunk, chunks):
    tokens, width = own_in.shape
    hidden = gate_weight.shape[1]
    rows = 2
    block = hidden // 4
    part = block // chunks
    span = rows * part
    tile = min(512, tokens)
    tiles = 2 * tokens // tile
    half_tiles = tokens // tile
    eighth = width // 8
    step = 256

    def kernel(
        place_ref, own_ref, other_ref, own_grad_ref, other_grad_ref, gate_ref, up_ref, down_ref,
        act_out, gate_out, up_out, gate_send, gate_keep, up_send, up_keep, down_send, down_keep,
        tok, grd, wg, wu, wd, act, gg, ug, gw, uw, dw, in_sem, w_sem, out_sem, grad_sem,
    ):
        def token_copy(t, which):
            buf = (tok, grd)[which]
            src = ((own_ref, other_ref), (own_grad_ref, other_grad_ref))[which][0 if t < half_tiles else 1]
            return pltpu.make_async_copy(
                src.at[pl.ds((t % half_tiles) * tile, tile)],
                buf.at[pl.ds(t * tile, tile)],
                in_sem.at[which, t],
            )

        weight_copies = []
        for n, (ref, buf) in enumerate(((gate_ref, wg), (up_ref, wu))):
            weight_copies.append([
                pltpu.make_async_copy(
                    ref.at[:, pl.ds(pl.multiple_of(place_ref[j] * block + chunk * part, 128), part)],
                    buf.at[:, pl.ds(j * part, part)],
                    w_sem.at[n, j],
                )
                for j in range(2)
            ])
        weight_copies.append([
            pltpu.make_async_copy(
                down_ref.at[pl.ds(pl.multiple_of(place_ref[j] * block + chunk * part, 128), part), :],
                wd.at[pl.ds(j * part, part), :],
                w_sem.at[2, j],
            )
            for j in range(2)
        ])
        token_copy(0, 0).start()
        for copy in weight_copies[0]:
            copy.start()
        for copy in weight_copies[1]:
            copy.start()
        token_copy(0, 1).start()
        for copy in weight_copies[2]:
            copy.start()
        outs = []
        for t in range(tiles):
            at = pl.ds(t * tile, tile)
            token_copy(t, 0).wait()
            if t == 0:
                for copy in weight_copies[0] + weight_copies[1]:
                    copy.wait()
            if t + 1 < tiles:
                token_copy(t + 1, 0).start()
                token_copy(t + 1, 1).start()
            token_copy(t, 1).wait()
            if t == 0:
                for copy in weight_copies[2]:
                    copy.wait()
            for n in range(span // step):
                cols = pl.ds(n * step, step)
                gate = jnp.dot(tok[at, :], wg[:, cols], preferred_element_type=jnp.float32)
                up = jnp.dot(tok[at, :], wu[:, cols], preferred_element_type=jnp.float32)
                grad = contract_cols(grd[at, :], wd[cols, :])
                sig = jax.nn.sigmoid(gate)
                gate_sig = gate * sig
                act[at, cols] = narrow(gate_sig * up)
                ug[at, cols] = narrow(grad * gate_sig)
                gg[at, cols] = narrow(grad * up * (sig + gate_sig * (1.0 - sig)))
            for n, (buf, out) in enumerate(((act, act_out), (gg, gate_out), (ug, up_out))):
                copy = pltpu.make_async_copy(buf.at[at], out.at[at], out_sem.at[n, t])
                copy.start()
                outs.append(copy)

        for buf, grad in ((gw, gg), (uw, ug)):
            for n in range(span // step):
                cols = pl.ds(n * step, step)
                total = narrow(contract_rows(tok[...], grad[:, cols]))
                for i in range(8):
                    spot = place_ref[2 + i]
                    rows_i = total[i * eighth : (i + 1) * eighth]
                    for c in range(step // 128):
                        col = n * step + c * 128
                        buf[col // part, spot, :, pl.ds(col % part, 128)] = rows_i[:, c * 128 : (c + 1) * 128]
            if buf is gw:
                pairs = [
                    (gw.at[j, pl.ds(4 * h + 2 * z, 2)], out.at[j, h], grad_sem.at[8 + 4 * z + 2 * j + h])
                    for z, out in enumerate((gate_send, gate_keep))
                    for j in range(2)
                    for h in range(2)
                ]
            else:
                pairs = [
                    (uw.at[j, 2 * h + y], out.at[j, h], grad_sem.at[16 + 8 * y + 4 * j + h])
                    for y, out in enumerate((up_send, up_keep))
                    for j in range(2)
                    for h in range(4)
                ]
            for src, out, sem in pairs:
                copy = pltpu.make_async_copy(src, out, sem)
                copy.start()
                outs.append(copy)
        for side in range(2):
            for n in range(2):
                cols = pl.ds(pl.multiple_of(place_ref[10 + side] * (width // 2) + n * (width // 4), 128), width // 4)
                total = narrow(contract_rows(act[...], grd[:, cols]))
                for j in range(2):
                    dw[side, place_ref[12 + j], :, pl.ds(n * (width // 4), width // 4)] = total[j * part : (j + 1) * part]
            copy = pltpu.make_async_copy(dw.at[side], (down_send, down_keep)[side], grad_sem.at[side])
            copy.start()
            outs.append(copy)
        for copy in outs:
            copy.wait()

    any_spec = pl.BlockSpec(memory_space=pl.ANY)
    low = jnp.bfloat16
    both = 2 * tokens
    flops = 6 * 2 * both * width * span
    return pl.pallas_call(
        kernel,
        out_shape=[jax.ShapeDtypeStruct((both, span), low)] * 3
        + [jax.ShapeDtypeStruct((2, 2, 2, eighth, part), low)] * 2
        + [jax.ShapeDtypeStruct((2, 4, eighth, part), low)] * 2
        + [jax.ShapeDtypeStruct((2, part, width // 2), low)] * 2,
        grid_spec=pltpu.PrefetchScalarGridSpec(
            num_scalar_prefetch=1,
            grid=(1,),
            in_specs=[any_spec] * 7,
            out_specs=[any_spec] * 9,
            scratch_shapes=[
                pltpu.VMEM((both, width), low),
                pltpu.VMEM((both, width), low),
                pltpu.VMEM((width, span), low),
                pltpu.VMEM((width, span), low),
                pltpu.VMEM((span, width), low),
                pltpu.VMEM((both, span), low),
                pltpu.VMEM((both, span), low),
                pltpu.VMEM((both, span), low),
                pltpu.VMEM((2, 8, eighth, part), low),
                pltpu.VMEM((2, 8, eighth, part), low),
                pltpu.VMEM((2, 2, part, width // 2), low),
                pltpu.SemaphoreType.DMA((2, tiles)),
                pltpu.SemaphoreType.DMA((3, 2)),
                pltpu.SemaphoreType.DMA((3, tiles)),
                pltpu.SemaphoreType.DMA((32,)),
            ],
        ),
        compiler_params=pltpu.CompilerParams(vmem_limit_bytes=56 << 20),
        cost_estimate=pl.CostEstimate(flops=flops, bytes_accessed=24 << 20, transcendentals=both * span),
        name=f"feed_{chunk}",
    )(place, own_in, other_in, own_grad, other_grad, gate_weight, up_weight, down_weight)


def feed_sum(place, groups, weights, across, block, name):
    chunks = len(groups[0])
    both, span = groups[0][0].shape
    part = span // 2
    width = weights[0].shape[0] if across else weights[0].shape[1]
    tokens = both // 2
    tile = min(512, tokens)
    tiles = both // tile
    half_tiles = tiles // 2
    kinds = len(groups)

    def kernel(place_ref, *refs):
        lefts = [refs[g * chunks : (g + 1) * chunks] for g in range(kinds)]
        rights = refs[kinds * chunks : kinds * chunks + kinds]
        own_out, other_out, lbuf, wbuf, total, obuf, l_sem, w_sem, o_sem = refs[kinds * chunks + kinds :]

        def weight_copies(k):
            slot = k % 2
            copies = []
            for g in range(kinds):
                for j in range(2):
                    rows = pl.ds(pl.multiple_of(place_ref[j] * block + k * part, 128), part)
                    if across:
                        src, dst = rights[g].at[:, rows], wbuf.at[slot, g, :, pl.ds(j * part, part)]
                    else:
                        src, dst = rights[g].at[rows, :], wbuf.at[slot, g, pl.ds(j * part, part), :]
                    copies.append(pltpu.make_async_copy(src, dst, w_sem.at[slot, g, j]))
            return copies

        def left_copies(k, t, slot):
            return [
                pltpu.make_async_copy(lefts[g][k].at[pl.ds(t * tile, tile)], lbuf.at[slot, g], l_sem.at[slot, g])
                for g in range(kinds)
            ]

        def out_copy(t, slot):
            ref = own_out if t < half_tiles else other_out
            return pltpu.make_async_copy(
                obuf.at[slot], ref.at[pl.ds((t % half_tiles) * tile, tile)], o_sem.at[slot]
            )

        for copy in left_copies(0, 0, 0) + weight_copies(0):
            copy.start()
        for k in range(chunks):
            for t in range(tiles):
                n = k * tiles + t
                for copy in left_copies(k, t, n % 2):
                    copy.wait()
                if t == 0:
                    for copy in weight_copies(k):
                        copy.wait()
                if n + 1 < chunks * tiles:
                    for copy in left_copies((n + 1) // tiles, (n + 1) % tiles, (n + 1) % 2):
                        copy.start()
                if t == 0 and k + 1 < chunks:
                    for copy in weight_copies(k + 1):
                        copy.start()
                value = None
                for g in range(kinds):
                    left, right = lbuf[n % 2, g], wbuf[k % 2, g]
                    term = contract_cols(left, right) if across else jnp.dot(left, right, preferred_element_type=jnp.float32)
                    value = term if value is None else value + term
                if k > 0:
                    value = value + total[t]
                if k + 1 < chunks:
                    total[t] = value
                else:
                    if t >= 2:
                        out_copy(t - 2, t % 2).wait()
                    obuf[t % 2] = narrow(value)
                    out_copy(t, t % 2).start()
        for t in range(max(0, tiles - 2), tiles):
            out_copy(t, t % 2).wait()

    any_spec = pl.BlockSpec(memory_space=pl.ANY)
    low = jnp.bfloat16
    wshape = (width, span) if across else (span, width)
    return pl.pallas_call(
        kernel,
        out_shape=[jax.ShapeDtypeStruct((tokens, width), low)] * 2,
        grid_spec=pltpu.PrefetchScalarGridSpec(
            num_scalar_prefetch=1,
            grid=(1,),
            in_specs=[any_spec] * (kinds * chunks + kinds),
            out_specs=[any_spec] * 2,
            scratch_shapes=[
                pltpu.VMEM((2, kinds, tile, span), low),
                pltpu.VMEM((2, kinds) + wshape, low),
                pltpu.VMEM((tiles, tile, width), jnp.float32),
                pltpu.VMEM((2, tile, width), low),
                pltpu.SemaphoreType.DMA((2, kinds)),
                pltpu.SemaphoreType.DMA((2, kinds, 2)),
                pltpu.SemaphoreType.DMA((2,)),
            ],
        ),
        compiler_params=pltpu.CompilerParams(vmem_limit_bytes=48 << 20),
        cost_estimate=pl.CostEstimate(
            flops=kinds * chunks * 2 * both * width * span, bytes_accessed=24 << 20, transcendentals=0
        ),
        name=name,
    )(place, *[item for group in groups for item in group], *weights)


def plain(
    hidden_in,
    mixer_gain,
    in_weight,
    conv_kernel,
    out_weight,
    feed_gain,
    gate_weight,
    up_weight,
    down_weight,
    document_lengths,
    valid_tokens,
    cotangent,
):
    row_count, span_length, model_width = hidden_in.shape
    token_count = row_count * span_length
    offset = lax.axis_index("seq") * span_length
    positions = offset + jnp.arange(span_length, dtype=jnp.int32)
    starts = jnp.cumsum(document_lengths, axis=1) - document_lengths
    is_start = jnp.any(positions[None, :, None] == starts[:, None, :], axis=2)
    before = jnp.any((positions - 1)[None, :, None] == starts[:, None, :], axis=2)
    keep_one = (1.0 - is_start.astype(jnp.float32))[:, :, None]
    keep_two = keep_one * (1.0 - before.astype(jnp.float32))[:, :, None]
    valid_mask = (
        (positions[None, :] < valid_tokens[:, None]).astype(jnp.float32).reshape(token_count, 1)
    )
    mixer_scale = mixer_gain.astype(jnp.float32)
    feed_scale = feed_gain.astype(jnp.float32)
    kernel = conv_kernel.astype(jnp.float32)
    source = hidden_in.astype(jnp.float32).reshape(token_count, model_width)
    inverse_one = lax.rsqrt(jnp.mean(source * source, axis=1, keepdims=True) + EPS)
    normed = (source * inverse_one * mixer_scale).astype(jnp.bfloat16)
    project = jnp.dot(normed, in_weight, preferred_element_type=jnp.float32)
    input_gate = project[:, :model_width]
    output_gate = project[:, model_width : 2 * model_width]
    values = project[:, 2 * model_width :]
    product = (
        (input_gate * values).astype(jnp.bfloat16).reshape(row_count, span_length, model_width)
    )
    rim_values = passed_along(product[:, span_length - 2 :, :], "seq", 1)
    extended = jnp.concatenate([rim_values, product], axis=1).astype(jnp.float32)
    tap_zero = extended[:, 2:, :]
    tap_one = keep_one * extended[:, 1:-1, :]
    tap_two = keep_two * extended[:, :-2, :]
    conv_out = (kernel[:, 0] * tap_zero + kernel[:, 1] * tap_one + kernel[:, 2] * tap_two).reshape(
        token_count, model_width
    )
    mixed_in = (output_gate * conv_out).astype(jnp.bfloat16)
    mixer_out = jnp.dot(mixed_in, out_weight, preferred_element_type=jnp.float32)
    residual = source + valid_mask * mixer_out
    inverse_two = lax.rsqrt(jnp.mean(residual * residual, axis=1, keepdims=True) + EPS)
    normed_two = (residual * inverse_two * feed_scale).astype(jnp.bfloat16)
    gate_pre = jnp.dot(normed_two, gate_weight, preferred_element_type=jnp.float32)
    up_pre = jnp.dot(normed_two, up_weight, preferred_element_type=jnp.float32)
    sigmoid_gate = jax.nn.sigmoid(gate_pre)
    activation = (gate_pre * sigmoid_gate * up_pre).astype(jnp.bfloat16)
    feed_out = jnp.dot(activation, down_weight, preferred_element_type=jnp.float32)
    output = (
        (residual + valid_mask * feed_out)
        .astype(jnp.bfloat16)
        .reshape(row_count, span_length, model_width)
    )
    upstream = cotangent.astype(jnp.float32).reshape(token_count, model_width)
    feed_grad = (valid_mask * upstream).astype(jnp.bfloat16)
    down_grad = contract_rows(activation, feed_grad)
    activation_grad = contract_cols(feed_grad, down_weight)
    up_grad = (activation_grad * gate_pre * sigmoid_gate).astype(jnp.bfloat16)
    gate_grad = (
        activation_grad * up_pre * sigmoid_gate * (1.0 + gate_pre * (1.0 - sigmoid_gate))
    ).astype(jnp.bfloat16)
    gate_wgrad = contract_rows(normed_two, gate_grad)
    up_wgrad = contract_rows(normed_two, up_grad)
    normed_two_grad = contract_cols(gate_grad, gate_weight) + contract_cols(up_grad, up_weight)
    feed_gain_grad = jnp.sum(normed_two_grad * residual * inverse_two, axis=0)
    scaled_two = feed_scale * normed_two_grad
    residual_grad = (
        upstream
        + inverse_two * scaled_two
        - residual
        * (inverse_two * inverse_two * inverse_two)
        * jnp.mean(scaled_two * residual, axis=1, keepdims=True)
    )
    feed_gain_part, gate_part, up_part, down_part = (
        lax.psum_scatter(
            feed_gain_grad.astype(jnp.bfloat16), "seq", scatter_dimension=0, tiled=True
        ).astype(jnp.float32),
        lax.psum_scatter(
            gate_wgrad.astype(jnp.bfloat16), "seq", scatter_dimension=0, tiled=True
        ).astype(jnp.float32),
        lax.psum_scatter(
            up_wgrad.astype(jnp.bfloat16), "seq", scatter_dimension=0, tiled=True
        ).astype(jnp.float32),
        lax.psum_scatter(
            down_grad.astype(jnp.bfloat16), "seq", scatter_dimension=0, tiled=True
        ).astype(jnp.float32),
    )
    gate_part, up_part, down_part = (
        lax.psum_scatter(
            gate_part.astype(jnp.bfloat16), "row", scatter_dimension=1, tiled=True
        ).astype(jnp.float32),
        lax.psum_scatter(
            up_part.astype(jnp.bfloat16), "row", scatter_dimension=1, tiled=True
        ).astype(jnp.float32),
        lax.psum_scatter(
            down_part.astype(jnp.bfloat16), "row", scatter_dimension=1, tiled=True
        ).astype(jnp.float32),
    )
    mixer_grad = (valid_mask * residual_grad).astype(jnp.bfloat16)
    out_wgrad = contract_rows(mixed_in, mixer_grad)
    mixed_grad = contract_cols(mixer_grad, out_weight)
    output_gate_grad = mixed_grad * conv_out
    conv_grad = (mixed_grad * output_gate).reshape(row_count, span_length, model_width)
    kernel_grad = jnp.stack(
        [
            jnp.sum(conv_grad * tap_zero, axis=(0, 1)),
            jnp.sum(conv_grad * tap_one, axis=(0, 1)),
            jnp.sum(conv_grad * tap_two, axis=(0, 1)),
        ],
        axis=1,
    )
    grad_zero = kernel[:, 0] * conv_grad
    grad_one = keep_one * kernel[:, 1] * conv_grad
    grad_two = keep_two * kernel[:, 2] * conv_grad
    extended_grad = (
        jnp.pad(grad_zero, ((0, 0), (2, 0), (0, 0)))
        + jnp.pad(grad_one, ((0, 0), (1, 1), (0, 0)))
        + jnp.pad(grad_two, ((0, 0), (0, 2), (0, 0)))
    )
    returned = passed_along(extended_grad[:, :2, :], "seq", -1)
    product_grad = extended_grad[:, 2:, :] + jnp.pad(
        returned, ((0, 0), (span_length - 2, 0), (0, 0))
    )
    flat_grad = product_grad.reshape(token_count, model_width)
    project_grad = jnp.concatenate(
        [flat_grad * values, output_gate_grad, flat_grad * input_gate], axis=1
    ).astype(jnp.bfloat16)
    in_wgrad = contract_rows(normed, project_grad)
    normed_grad = contract_cols(project_grad, in_weight)
    mixer_gain_grad = jnp.sum(normed_grad * source * inverse_one, axis=0)
    scaled_one = mixer_scale * normed_grad
    input_grad = (
        residual_grad
        + inverse_one * scaled_one
        - source
        * (inverse_one * inverse_one * inverse_one)
        * jnp.mean(scaled_one * source, axis=1, keepdims=True)
    )
    input_grad = input_grad.astype(jnp.bfloat16).reshape(row_count, span_length, model_width)
    mixer_gain_part, in_part, kernel_part, out_part = (
        lax.psum_scatter(
            mixer_gain_grad.astype(jnp.bfloat16), "seq", scatter_dimension=0, tiled=True
        ).astype(jnp.float32),
        lax.psum_scatter(
            in_wgrad.astype(jnp.bfloat16), "seq", scatter_dimension=0, tiled=True
        ).astype(jnp.float32),
        lax.psum_scatter(
            kernel_grad.astype(jnp.bfloat16), "seq", scatter_dimension=0, tiled=True
        ).astype(jnp.float32),
        lax.psum_scatter(
            out_wgrad.astype(jnp.bfloat16), "seq", scatter_dimension=0, tiled=True
        ).astype(jnp.float32),
    )
    in_part, out_part = (
        lax.psum_scatter(
            in_part.astype(jnp.bfloat16), "row", scatter_dimension=1, tiled=True
        ).astype(jnp.float32),
        lax.psum_scatter(
            out_part.astype(jnp.bfloat16), "row", scatter_dimension=1, tiled=True
        ).astype(jnp.float32),
    )
    mixer_gain_part, feed_gain_part, kernel_part = lax.psum(
        (mixer_gain_part, feed_gain_part, kernel_part), "row"
    )
    return (
        output,
        input_grad,
        mixer_gain_part,
        in_part,
        kernel_part,
        out_part,
        feed_gain_part,
        gate_part,
        up_part,
        down_part,
    )


def settle(value, order):
    names = ["x", "z1", "z0", "y"]
    links = {"x": ("row", 2), "y": ("seq", 1), "z0": ("seq", 2), "z1": ("seq", 4)}
    for name in order:
        at = names.index(name)
        names.remove(name)
        give = lax.index_in_dim(value, 0, at, keepdims=False)
        keep = lax.index_in_dim(value, 1, at, keepdims=False)
        value = wide(keep, swapped(narrow(give), *links[name]))
        if names:
            value = narrow(value)
    return value


def fast(
    hidden_in,
    mixer_gain,
    in_weight,
    conv_kernel,
    out_weight,
    feed_gain,
    gate_weight,
    up_weight,
    down_weight,
    document_lengths,
    valid_tokens,
    cotangent,
):
    row_count, span_length, model_width = hidden_in.shape
    token_count = row_count * span_length
    hidden_width = gate_weight.shape[1]
    block = hidden_width // 4
    chunks = 3
    part = block // chunks
    seq = lax.axis_index("seq")
    row = lax.axis_index("row")
    row_x, core = row // 2, row % 2
    seq_y, seq_z0, seq_z1 = seq % 2, (seq // 2) % 2, seq // 4
    place = jnp.stack(
        [row ^ 2, row]
        + [i ^ seq ^ 7 for i in range(8)]
        + [1 - row_x, row_x, 1 - ((1 - row_x) ^ seq_z1), 1 - (row_x ^ seq_z1)]
    ).astype(jnp.int32)
    offset = seq * span_length
    positions = offset + jnp.arange(span_length, dtype=jnp.int32)
    starts = jnp.cumsum(document_lengths, axis=1) - document_lengths
    is_start = jnp.any(positions[None, :, None] == starts[:, None, :], axis=2)
    before = jnp.any((positions - 1)[None, :, None] == starts[:, None, :], axis=2)
    keep_one = (1.0 - is_start.astype(jnp.float32))[:, :, None]
    keep_two = keep_one * (1.0 - before.astype(jnp.float32))[:, :, None]
    valid_mask = (
        (positions[None, :] < valid_tokens[:, None]).astype(jnp.float32).reshape(token_count, 1)
    )
    mixer_scale = mixer_gain.astype(jnp.float32)
    feed_scale = feed_gain.astype(jnp.float32)
    kernel = conv_kernel.astype(jnp.float32)
    upstream = cotangent.astype(jnp.float32).reshape(token_count, model_width)
    feed_grad = narrow(valid_mask * upstream)
    other_grad = swapped(feed_grad, "row", 1)

    source = hidden_in.astype(jnp.float32).reshape(token_count, model_width)
    inverse_one = lax.rsqrt(jnp.mean(source * source, axis=1, keepdims=True) + EPS)
    normed = (source * inverse_one * mixer_scale).astype(jnp.bfloat16)
    project = jnp.dot(normed, in_weight, preferred_element_type=jnp.float32)
    input_gate = project[:, :model_width]
    output_gate = project[:, model_width : 2 * model_width]
    values = project[:, 2 * model_width :]
    product = (
        (input_gate * values).astype(jnp.bfloat16).reshape(row_count, span_length, model_width)
    )
    rim_values = passed_along(product[:, span_length - 2 :, :], "seq", 1)
    extended = jnp.concatenate([rim_values, product], axis=1).astype(jnp.float32)
    tap_zero = extended[:, 2:, :]
    tap_one = keep_one * extended[:, 1:-1, :]
    tap_two = keep_two * extended[:, :-2, :]
    conv_out = (kernel[:, 0] * tap_zero + kernel[:, 1] * tap_one + kernel[:, 2] * tap_two).reshape(
        token_count, model_width
    )
    mixed_in = (output_gate * conv_out).astype(jnp.bfloat16)
    mixer_out = jnp.dot(mixed_in, out_weight, preferred_element_type=jnp.float32)
    residual = source + valid_mask * mixer_out
    inverse_two = lax.rsqrt(jnp.mean(residual * residual, axis=1, keepdims=True) + EPS)
    normed_two = (residual * inverse_two * feed_scale).astype(jnp.bfloat16)
    other_normed = swapped(normed_two, "row", 1)

    acts, gates, ups, gate_parts, up_parts, down_parts = [], [], [], [], [], []
    for chunk in range(chunks):
        act, gate_grad, up_grad, gs, gk, us, uk, ds, dk = feed_chunk(
            place, normed_two, other_normed, feed_grad, other_grad, gate_weight, up_weight, down_weight, chunk, chunks
        )
        acts.append(act)
        gates.append(gate_grad)
        ups.append(up_grad)
        gate = narrow(wide(gk, swapped(gs, "seq", 2)))
        gate = narrow(wide(gate[1], swapped(gate[0], "row", 2)))
        gate_parts.append(gate)
        up = narrow(wide(uk, swapped(us, "seq", 1)))
        up = narrow(wide(up[1], swapped(up[0], "row", 2)))
        up_parts.append(up)
        down_parts.append(narrow(wide(dk, swapped(ds, "row", 2))))
    own_ntg, give_ntg = feed_sum(place, [gates, ups], [gate_weight, up_weight], True, block, "normed_two_grad")
    take_ntg = swapped(give_ntg, "row", 1)
    own_feed, give_feed = feed_sum(place, [acts], [down_weight], False, block, "feed_out")
    take_feed = swapped(give_feed, "row", 1)
    output = narrow(residual + valid_mask * wide(own_feed, take_feed)).reshape(row_count, span_length, model_width)

    gate = jnp.stack(gate_parts)
    gate = narrow(wide(gate[:, :, 1], swapped(gate[:, :, 0], "seq", 1)))
    gate = wide(gate[:, 1], swapped(gate[:, 0], "seq", 4))
    gate_part = jnp.concatenate([gate[i] for i in range(chunks)], axis=1)
    up = jnp.stack(up_parts).reshape(chunks, 2, 2, model_width // 8, part)
    up = narrow(wide(up[:, :, 1], swapped(up[:, :, 0], "seq", 2)))
    up = wide(up[:, 1], swapped(up[:, 0], "seq", 4))
    up_part = jnp.concatenate([up[i] for i in range(chunks)], axis=1)
    down = jnp.concatenate(down_parts, axis=1)
    low_half, high_half = down[:, : block // 2], down[:, block // 2 :]
    down = narrow(
        wide(
            jnp.where(seq_y == 0, low_half, high_half),
            swapped(jnp.where(seq_y == 0, high_half, low_half), "seq", 1),
        )
    )
    down = narrow(wide(down[1], swapped(down[0], "seq", 4)))
    holder = [[(r & 1) == ((s >> 1) & 1) for r in range(4)] for s in range(8)]
    down = wide(
        down,
        lax.ppermute(
            down,
            ("seq", "row"),
            [(s * 4 + r, (s ^ 2) * 4 + r) for s in range(8) for r in range(4) if not holder[s][r]],
        ),
    )
    quarter = model_width // 4
    down_own = jnp.where(core == 0, down[:, :quarter], down[:, quarter:])
    down_other = narrow(jnp.where(core == 0, down[:, quarter:], down[:, :quarter]))
    down_other = lax.ppermute(
        down_other,
        ("seq", "row"),
        [(s * 4 + r, s * 4 + (r ^ 1)) for s in range(8) for r in range(4) if holder[s][r]],
    )
    down_part = jnp.where(core == seq_z0, down_own, down_other.astype(jnp.float32))

    normed_two_grad = wide(own_ntg, take_ntg)
    feed_gain_grad = jnp.sum(normed_two_grad * residual * inverse_two, axis=0)
    scaled_two = feed_scale * normed_two_grad
    residual_grad = (
        upstream
        + inverse_two * scaled_two
        - residual
        * (inverse_two * inverse_two * inverse_two)
        * jnp.mean(scaled_two * residual, axis=1, keepdims=True)
    )
    mixer_grad = (valid_mask * residual_grad).astype(jnp.bfloat16)

    def by_seq(value):
        width = value.shape[1] // 8
        return jnp.concatenate(
            [lax.dynamic_slice_in_dim(value, (p ^ seq ^ 7) * width, width, 1) for p in range(8)], axis=1
        )

    def by_row(value, core_at):
        width = value.shape[1] // 4
        return jnp.concatenate(
            [
                lax.dynamic_slice_in_dim(value, ((row ^ 3) ^ (2 * x + core_at)) * width, width, 1)
                for x in range(2)
            ],
            axis=1,
        )

    def pair_summed(left, right):
        give = contract_rows(left, by_row(right, 0))
        keep = contract_rows(left, by_row(right, 1))
        both = narrow(keep + swapped(narrow(give), "row", 1).astype(jnp.float32))
        width = both.shape[1] // 2
        return jnp.stack(
            [both[:, i * width : (i + 1) * width].reshape(2, 2, 2, model_width // 8, width) for i in range(2)]
        )

    out_sum = pair_summed(by_seq(mixed_in), mixer_grad)
    mixed_grad = contract_cols(mixer_grad, out_weight)
    output_gate_grad = mixed_grad * conv_out
    conv_grad = (mixed_grad * output_gate).reshape(row_count, span_length, model_width)
    kernel_grad = [
        jnp.sum(conv_grad * tap_zero, axis=(0, 1)),
        jnp.sum(conv_grad * tap_one, axis=(0, 1)),
        jnp.sum(conv_grad * tap_two, axis=(0, 1)),
    ]
    grad_zero = kernel[:, 0] * conv_grad
    grad_one = keep_one * kernel[:, 1] * conv_grad
    grad_two = keep_two * kernel[:, 2] * conv_grad
    extended_grad = (
        jnp.pad(grad_zero, ((0, 0), (2, 0), (0, 0)))
        + jnp.pad(grad_one, ((0, 0), (1, 1), (0, 0)))
        + jnp.pad(grad_two, ((0, 0), (0, 2), (0, 0)))
    )
    returned = passed_along(extended_grad[:, :2, :], "seq", -1)
    product_grad = extended_grad[:, 2:, :] + jnp.pad(
        returned, ((0, 0), (span_length - 2, 0), (0, 0))
    )
    flat_grad = product_grad.reshape(token_count, model_width)
    project_grad = jnp.concatenate(
        [flat_grad * values, output_gate_grad, flat_grad * input_gate], axis=1
    ).astype(jnp.bfloat16)
    in_sum = pair_summed(by_seq(normed), project_grad)
    third = in_sum.shape[-1] // 3
    in_part = jnp.concatenate(
        [
            settle(in_sum[..., i * third : (i + 1) * third], order)
            for i, order in enumerate((("x", "y", "z0", "z1"), ("y", "x", "z0", "z1"), ("z0", "x", "y", "z1")))
        ],
        axis=1,
    )
    out_part = settle(out_sum, ("y", "z0", "x", "z1"))
    normed_grad = contract_cols(project_grad, in_weight)
    mixer_gain_grad = jnp.sum(normed_grad * source * inverse_one, axis=0)
    scaled_one = mixer_scale * normed_grad
    input_grad = (
        residual_grad
        + inverse_one * scaled_one
        - source
        * (inverse_one * inverse_one * inverse_one)
        * jnp.mean(scaled_one * source, axis=1, keepdims=True)
    )
    input_grad = input_grad.astype(jnp.bfloat16).reshape(row_count, span_length, model_width)
    small = jnp.stack([mixer_gain_grad, feed_gain_grad] + kernel_grad)
    for axis, bit in (("row", 1), ("row", 2), ("seq", 1), ("seq", 2), ("seq", 4)):
        small = small + swapped(small, axis, bit)
    small = lax.dynamic_slice_in_dim(small, seq * (model_width // 8), model_width // 8, 1)
    return (
        output,
        input_grad,
        small[0],
        in_part,
        small[2:].T,
        out_part,
        small[1],
        gate_part,
        up_part,
        down_part,
    )


def local(*args):
    hidden_in, gate_weight = args[0], args[6]
    tokens = hidden_in.shape[0] * hidden_in.shape[1]
    width, hidden = gate_weight.shape
    tiled = lax.axis_size("seq") == 8 and lax.axis_size("row") == 4 and hidden % (4 * 3 * 128) == 0
    if tiled and width % 1024 == 0 and tokens % 512 == 0:
        return fast(*args)
    return plain(*args)


def solution(mesh):
    in_specs = (
        P("row", "seq", None),
        P(),
        P(),
        P(),
        P(),
        P(),
        P(),
        P(),
        P(),
        P("row", None),
        P("row"),
        P("row", "seq", None),
    )
    out_specs = (
        P("row", "seq", None),
        P("row", "seq", None),
        P("seq"),
        P("seq", "row"),
        P("seq", None),
        P("seq", "row"),
        P("seq"),
        P("seq", "row"),
        P("seq", "row"),
        P("seq", "row"),
    )
    return jax.shard_map(local, mesh=mesh, in_specs=in_specs, out_specs=out_specs, check_vma=False)
```

```python
import jax
import jax.numpy as jnp
from jax import lax
from jax.experimental import pallas as pl
from jax.experimental.pallas import tpu as pltpu
from jax.sharding import PartitionSpec as P

EPS = 1e-05


def passed_along(value, axis, by):
    length = lax.axis_size(axis)
    pairs = [(i, i + by) for i in range(length) if 0 <= i + by < length]
    return lax.ppermute(value, axis, pairs)


def contract_rows(left, right):
    return lax.dot_general(
        left, right, (((0,), (0,)), ((), ())), preferred_element_type=jnp.float32
    )


def contract_cols(left, right):
    return lax.dot_general(
        left, right, (((1,), (1,)), ((), ())), preferred_element_type=jnp.float32
    )


def swapped(value, axis, bit):
    length = lax.axis_size(axis)
    return lax.ppermute(value, axis, [(i, i ^ bit) for i in range(length)])


def wide(left, right):
    return left.astype(jnp.float32) + right.astype(jnp.float32)


def narrow(value):
    return value.astype(jnp.bfloat16)


def feed_chunk(place, own_in, other_in, own_grad, other_grad, gate_weight, up_weight, down_weight, chunk, chunks):
    tokens, width = own_in.shape
    hidden = gate_weight.shape[1]
    rows = 2
    block = hidden // 4
    part = block // chunks
    span = rows * part
    tile = min(512, tokens)
    tiles = 2 * tokens // tile
    half_tiles = tokens // tile
    eighth = width // 8
    step = 256

    def kernel(
        place_ref, own_ref, other_ref, own_grad_ref, other_grad_ref, gate_ref, up_ref, down_ref,
        act_out, gate_out, up_out, gate_send, gate_keep, up_send, up_keep, down_send, down_keep,
        tok, grd, wg, wu, wd, act, gg, ug, gw, uw, dw, in_sem, w_sem, out_sem, grad_sem,
    ):
        def token_copy(t, which):
            buf = (tok, grd)[which]
            src = ((own_ref, other_ref), (own_grad_ref, other_grad_ref))[which][0 if t < half_tiles else 1]
            return pltpu.make_async_copy(
                src.at[pl.ds((t % half_tiles) * tile, tile)],
                buf.at[pl.ds(t * tile, tile)],
                in_sem.at[which, t],
            )

        weight_copies = []
        for n, (ref, buf) in enumerate(((gate_ref, wg), (up_ref, wu))):
            weight_copies.append([
                pltpu.make_async_copy(
                    ref.at[:, pl.ds(pl.multiple_of(place_ref[j] * block + chunk * part, 128), part)],
                    buf.at[:, pl.ds(j * part, part)],
                    w_sem.at[n, j],
                )
                for j in range(2)
            ])
        weight_copies.append([
            pltpu.make_async_copy(
                down_ref.at[pl.ds(pl.multiple_of(place_ref[j] * block + chunk * part, 128), part), :],
                wd.at[pl.ds(j * part, part), :],
                w_sem.at[2, j],
            )
            for j in range(2)
        ])
        token_copy(0, 0).start()
        for copy in weight_copies[0]:
            copy.start()
        for copy in weight_copies[1]:
            copy.start()
        token_copy(0, 1).start()
        for copy in weight_copies[2]:
            copy.start()
        outs = []
        for t in range(tiles):
            at = pl.ds(t * tile, tile)
            token_copy(t, 0).wait()
            if t == 0:
                for copy in weight_copies[0] + weight_copies[1]:
                    copy.wait()
            if t + 1 < tiles:
                token_copy(t + 1, 0).start()
                token_copy(t + 1, 1).start()
            token_copy(t, 1).wait()
            if t == 0:
                for copy in weight_copies[2]:
                    copy.wait()
            for n in range(span // step):
                cols = pl.ds(n * step, step)
                gate = jnp.dot(tok[at, :], wg[:, cols], preferred_element_type=jnp.float32)
                up = jnp.dot(tok[at, :], wu[:, cols], preferred_element_type=jnp.float32)
                grad = contract_cols(grd[at, :], wd[cols, :])
                sig = jax.nn.sigmoid(gate)
                gate_sig = gate * sig
                act[at, cols] = narrow(gate_sig * up)
                ug[at, cols] = narrow(grad * gate_sig)
                gg[at, cols] = narrow(grad * up * (sig + gate_sig * (1.0 - sig)))
            for n, (buf, out) in enumerate(((act, act_out), (gg, gate_out), (ug, up_out))):
                copy = pltpu.make_async_copy(buf.at[at], out.at[at], out_sem.at[n, t])
                copy.start()
                outs.append(copy)

        for buf, grad in ((gw, gg), (uw, ug)):
            for n in range(span // step):
                cols = pl.ds(n * step, step)
                total = narrow(contract_rows(tok[...], grad[:, cols]))
                for i in range(8):
                    spot = place_ref[2 + i]
                    rows_i = total[i * eighth : (i + 1) * eighth]
                    for c in range(step // 128):
                        col = n * step + c * 128
                        buf[col // part, spot, :, pl.ds(col % part, 128)] = rows_i[:, c * 128 : (c + 1) * 128]
            if buf is gw:
                pairs = [
                    (gw.at[j, pl.ds(4 * h + 2 * z, 2)], out.at[j, h], grad_sem.at[8 + 4 * z + 2 * j + h])
                    for z, out in enumerate((gate_send, gate_keep))
                    for j in range(2)
                    for h in range(2)
                ]
            else:
                pairs = [
                    (uw.at[j, 2 * h + y], out.at[j, h], grad_sem.at[16 + 8 * y + 4 * j + h])
                    for y, out in enumerate((up_send, up_keep))
                    for j in range(2)
                    for h in range(4)
                ]
            for src, out, sem in pairs:
                copy = pltpu.make_async_copy(src, out, sem)
                copy.start()
                outs.append(copy)
        for side in range(2):
            for n in range(2):
                cols = pl.ds(pl.multiple_of(place_ref[10 + side] * (width // 2) + n * (width // 4), 128), width // 4)
                total = narrow(contract_rows(act[...], grd[:, cols]))
                for j in range(2):
                    dw[side, place_ref[12 + j], :, pl.ds(n * (width // 4), width // 4)] = total[j * part : (j + 1) * part]
            copy = pltpu.make_async_copy(dw.at[side], (down_send, down_keep)[side], grad_sem.at[side])
            copy.start()
            outs.append(copy)
        for copy in outs:
            copy.wait()

    any_spec = pl.BlockSpec(memory_space=pltpu.HBM)
    low = jnp.bfloat16
    both = 2 * tokens
    flops = 6 * 2 * both * width * span
    return pl.pallas_call(
        kernel,
        out_shape=[jax.ShapeDtypeStruct((both, span), low)] * 3
        + [jax.ShapeDtypeStruct((2, 2, 2, eighth, part), low)] * 2
        + [jax.ShapeDtypeStruct((2, 4, eighth, part), low)] * 2
        + [jax.ShapeDtypeStruct((2, part, width // 2), low)] * 2,
        grid_spec=pltpu.PrefetchScalarGridSpec(
            num_scalar_prefetch=1,
            grid=(1,),
            in_specs=[any_spec] * 7,
            out_specs=[any_spec] * 9,
            scratch_shapes=[
                pltpu.VMEM((both, width), low),
                pltpu.VMEM((both, width), low),
                pltpu.VMEM((width, span), low),
                pltpu.VMEM((width, span), low),
                pltpu.VMEM((span, width), low),
                pltpu.VMEM((both, span), low),
                pltpu.VMEM((both, span), low),
                pltpu.VMEM((both, span), low),
                pltpu.VMEM((2, 8, eighth, part), low),
                pltpu.VMEM((2, 8, eighth, part), low),
                pltpu.VMEM((2, 2, part, width // 2), low),
                pltpu.SemaphoreType.DMA((2, tiles)),
                pltpu.SemaphoreType.DMA((3, 2)),
                pltpu.SemaphoreType.DMA((3, tiles)),
                pltpu.SemaphoreType.DMA((32,)),
            ],
        ),
        compiler_params=pltpu.CompilerParams(vmem_limit_bytes=56 << 20),
        cost_estimate=pl.CostEstimate(flops=flops, bytes_accessed=24 << 20, transcendentals=both * span),
        name=f"feed_{chunk}",
    )(place, own_in, other_in, own_grad, other_grad, gate_weight, up_weight, down_weight)


def feed_sum(place, groups, weights, across, block, name):
    chunks = len(groups[0])
    both, span = groups[0][0].shape
    part = span // 2
    width = weights[0].shape[0] if across else weights[0].shape[1]
    tokens = both // 2
    tile = min(512, tokens)
    tiles = both // tile
    half_tiles = tiles // 2
    kinds = len(groups)

    def kernel(place_ref, *refs):
        lefts = [refs[g * chunks : (g + 1) * chunks] for g in range(kinds)]
        rights = refs[kinds * chunks : kinds * chunks + kinds]
        own_out, other_out, lbuf, wbuf, total, obuf, l_sem, w_sem, o_sem = refs[kinds * chunks + kinds :]

        def weight_copies(k):
            slot = k % 2
            copies = []
            for g in range(kinds):
                for j in range(2):
                    rows = pl.ds(pl.multiple_of(place_ref[j] * block + k * part, 128), part)
                    if across:
                        src, dst = rights[g].at[:, rows], wbuf.at[slot, g, :, pl.ds(j * part, part)]
                    else:
                        src, dst = rights[g].at[rows, :], wbuf.at[slot, g, pl.ds(j * part, part), :]
                    copies.append(pltpu.make_async_copy(src, dst, w_sem.at[slot, g, j]))
            return copies

        def left_copies(k, t, slot):
            return [
                pltpu.make_async_copy(lefts[g][k].at[pl.ds(t * tile, tile)], lbuf.at[slot, g], l_sem.at[slot, g])
                for g in range(kinds)
            ]

        def out_copy(t, slot):
            ref = own_out if t < half_tiles else other_out
            return pltpu.make_async_copy(
                obuf.at[slot], ref.at[pl.ds((t % half_tiles) * tile, tile)], o_sem.at[slot]
            )

        for copy in left_copies(0, 0, 0) + weight_copies(0):
            copy.start()
        for k in range(chunks):
            for t in range(tiles):
                n = k * tiles + t
                for copy in left_copies(k, t, n % 2):
                    copy.wait()
                if t == 0:
                    for copy in weight_copies(k):
                        copy.wait()
                if n + 1 < chunks * tiles:
                    for copy in left_copies((n + 1) // tiles, (n + 1) % tiles, (n + 1) % 2):
                        copy.start()
                if t == 0 and k + 1 < chunks:
                    for copy in weight_copies(k + 1):
                        copy.start()
                value = None
                for g in range(kinds):
                    left, right = lbuf[n % 2, g], wbuf[k % 2, g]
                    term = contract_cols(left, right) if across else jnp.dot(left, right, preferred_element_type=jnp.float32)
                    value = term if value is None else value + term
                if k > 0:
                    value = value + total[t]
                if k + 1 < chunks:
                    total[t] = value
                else:
                    if t >= 2:
                        out_copy(t - 2, t % 2).wait()
                    obuf[t % 2] = narrow(value)
                    out_copy(t, t % 2).start()
        for t in range(max(0, tiles - 2), tiles):
            out_copy(t, t % 2).wait()

    any_spec = pl.BlockSpec(memory_space=pltpu.HBM)
    low = jnp.bfloat16
    wshape = (width, span) if across else (span, width)
    return pl.pallas_call(
        kernel,
        out_shape=[jax.ShapeDtypeStruct((tokens, width), low)] * 2,
        grid_spec=pltpu.PrefetchScalarGridSpec(
            num_scalar_prefetch=1,
            grid=(1,),
            in_specs=[any_spec] * (kinds * chunks + kinds),
            out_specs=[any_spec] * 2,
            scratch_shapes=[
                pltpu.VMEM((2, kinds, tile, span), low),
                pltpu.VMEM((2, kinds) + wshape, low),
                pltpu.VMEM((tiles, tile, width), jnp.float32),
                pltpu.VMEM((2, tile, width), low),
                pltpu.SemaphoreType.DMA((2, kinds)),
                pltpu.SemaphoreType.DMA((2, kinds, 2)),
                pltpu.SemaphoreType.DMA((2,)),
            ],
        ),
        compiler_params=pltpu.CompilerParams(vmem_limit_bytes=48 << 20),
        cost_estimate=pl.CostEstimate(
            flops=kinds * chunks * 2 * both * width * span, bytes_accessed=24 << 20, transcendentals=0
        ),
        name=name,
    )(place, *[item for group in groups for item in group], *weights)


LOW = jnp.bfloat16
FULL = jnp.float32
MARGIN = 16


def whole(shape):
    return pl.BlockSpec(shape, lambda *_: (0,) * len(shape), pipeline_mode=pl.Buffered(1))


def mixer_forward(marks, hidden, rim, in_weight, out_weight, scales):
    tokens, width = hidden.shape
    tile = 256
    per_row = tokens // 2 // tile
    steps = tokens // tile

    def kernel(
        marks_ref, hidden_ref, rim_ref, in_ref, out_ref, scale_ref,
        normed_out, gate_out, open_out, value_out, product_out, mixed_out, residual_out, next_out, before_out,
        ext, carry,
    ):
        at = pl.program_id(0) % per_row
        tile_in = hidden_ref[...].astype(FULL)

        @pl.when(at == 0)
        def _():
            carry[...] = rim_ref[...].astype(FULL)

        source = jnp.concatenate([carry[...], tile_in], axis=0)
        carry[...] = tile_in[tile - MARGIN :]
        inverse = lax.rsqrt(jnp.mean(source * source, axis=1, keepdims=True) + EPS)
        normed = narrow(source * inverse * scale_ref[0:1, :])
        gate = jnp.dot(normed, in_ref[:, :width], preferred_element_type=FULL)
        value = jnp.dot(normed, in_ref[:, 2 * width :], preferred_element_type=FULL)
        product = narrow(gate * value)
        ext[...] = product.astype(FULL)
        opened = jnp.dot(normed[MARGIN:], in_ref[:, width : 2 * width], preferred_element_type=FULL)
        conv = (
            scale_ref[2:3, :] * ext[MARGIN:, :]
            + marks_ref[:, 0:1] * scale_ref[3:4, :] * ext[MARGIN - 1 : MARGIN - 1 + tile, :]
            + marks_ref[:, 1:2] * scale_ref[4:5, :] * ext[MARGIN - 2 : MARGIN - 2 + tile, :]
        )
        mixed = narrow(opened * conv)
        residual = tile_in + marks_ref[:, 2:3] * jnp.dot(mixed, out_ref[...], preferred_element_type=FULL)
        inverse_two = lax.rsqrt(jnp.mean(residual * residual, axis=1, keepdims=True) + EPS)
        next_out[...] = narrow(residual * inverse_two * scale_ref[1:2, :])
        normed_out[...] = normed[MARGIN:]
        gate_out[...] = narrow(gate[MARGIN:])
        open_out[...] = narrow(opened)
        value_out[...] = narrow(value[MARGIN:])
        product_out[...] = product[MARGIN:]
        mixed_out[...] = mixed
        residual_out[...] = residual

        @pl.when(at == 0)
        def _():
            before_out[...] = product[:MARGIN]

    def rows(last, size=tile):
        return pl.BlockSpec((size, last), lambda i: (i, 0))

    row_spec = pl.BlockSpec((MARGIN, width), lambda i: (i // per_row, 0))
    return pl.pallas_call(
        kernel,
        grid=(steps,),
        in_specs=[rows(8), rows(width), row_spec, whole(in_weight.shape), whole(out_weight.shape), whole(scales.shape)],
        out_specs=[rows(width)] * 8 + [row_spec],
        out_shape=[jax.ShapeDtypeStruct((tokens, width), LOW)] * 6
        + [jax.ShapeDtypeStruct((tokens, width), FULL), jax.ShapeDtypeStruct((tokens, width), LOW)]
        + [jax.ShapeDtypeStruct((2 * MARGIN, width), LOW)],
        scratch_shapes=[pltpu.VMEM((tile + MARGIN, width), FULL), pltpu.VMEM((MARGIN, width), FULL)],
        compiler_params=pltpu.CompilerParams(vmem_limit_bytes=44 << 20),
        cost_estimate=pl.CostEstimate(flops=8 * tokens * width * width, bytes_accessed=28 << 20, transcendentals=0),
        name="mixer_forward",
    )(marks, hidden, rim, in_weight, out_weight, scales)


def mixer_middle(marks, own, other, residual, cotangent, product, before, opened, out_weight, scales):
    tokens, width = own.shape
    tile = 256
    per_row = tokens // 2 // tile
    steps = tokens // tile

    def kernel(
        marks_ref, own_ref, other_ref, residual_ref, cot_ref, product_ref, before_ref, open_ref, out_ref, scale_ref,
        grad_out, mixer_out, open_grad_out, conv_out, sums_out,
        ext, carry,
    ):
        step = pl.program_id(0)
        at = step % per_row

        @pl.when(at == 0)
        def _():
            carry[...] = before_ref[...].astype(FULL)

        @pl.when(step == 0)
        def _():
            sums_out[...] = jnp.zeros_like(sums_out)

        grad = own_ref[...].astype(FULL) + other_ref[...].astype(FULL)
        residual = residual_ref[...]
        inverse = lax.rsqrt(jnp.mean(residual * residual, axis=1, keepdims=True) + EPS)
        sums_out[1:2, :] += jnp.sum(grad * (residual * inverse), axis=0, keepdims=True)
        scaled = scale_ref[1:2, :] * grad
        lean = (inverse * inverse * inverse) * jnp.mean(scaled * residual, axis=1, keepdims=True)
        residual_grad = cot_ref[...].astype(FULL) + inverse * scaled - residual * lean
        grad_out[...] = residual_grad
        mixer = narrow(marks_ref[:, 2:3] * residual_grad)
        mixer_out[...] = mixer
        mixed = contract_cols(mixer, out_ref[...])
        product = product_ref[...].astype(FULL)
        ext[:MARGIN, :] = carry[...]
        ext[MARGIN:, :] = product
        carry[...] = product[tile - MARGIN :]
        one = marks_ref[:, 0:1] * ext[MARGIN - 1 : MARGIN - 1 + tile, :]
        two = marks_ref[:, 1:2] * ext[MARGIN - 2 : MARGIN - 2 + tile, :]
        conv = scale_ref[2:3, :] * product + scale_ref[3:4, :] * one + scale_ref[4:5, :] * two
        open_grad_out[...] = narrow(mixed * conv)
        conv_grad = mixed * open_ref[...].astype(FULL)
        conv_out[...] = conv_grad
        sums_out[2:3, :] += jnp.sum(conv_grad * product, axis=0, keepdims=True)
        sums_out[3:4, :] += jnp.sum(conv_grad * one, axis=0, keepdims=True)
        sums_out[4:5, :] += jnp.sum(conv_grad * two, axis=0, keepdims=True)

    def rows(last):
        return pl.BlockSpec((tile, last), lambda i: (i, 0))

    row_spec = pl.BlockSpec((MARGIN, width), lambda i: (i // per_row, 0))
    return pl.pallas_call(
        kernel,
        grid=(steps,),
        in_specs=[rows(8)] + [rows(width)] * 5 + [row_spec, rows(width), whole(out_weight.shape), whole(scales.shape)],
        out_specs=[rows(width)] * 4 + [pl.BlockSpec((8, width), lambda i: (0, 0))],
        out_shape=[jax.ShapeDtypeStruct((tokens, width), kind) for kind in (FULL, LOW, LOW, FULL)]
        + [jax.ShapeDtypeStruct((8, width), FULL)],
        scratch_shapes=[pltpu.VMEM((tile + MARGIN, width), FULL), pltpu.VMEM((MARGIN, width), FULL)],
        compiler_params=pltpu.CompilerParams(vmem_limit_bytes=44 << 20),
        cost_estimate=pl.CostEstimate(flops=2 * tokens * width * width, bytes_accessed=32 << 20, transcendentals=0),
        name="mixer_middle",
    )(marks, own, other, residual, cotangent, product, before, opened, out_weight, scales)


def project_grads(marks, conv_grad, after, gate, value, open_grad, scales):
    tokens, width = conv_grad.shape
    tile = 256
    per_row = tokens // 2 // tile
    steps = tokens // tile

    def kernel(marks_ref, conv_ref, after_ref, gate_ref, value_ref, open_ref, scale_ref, grad_out, ext, carry):
        at = (steps - 1 - pl.program_id(0)) % per_row

        @pl.when(at == per_row - 1)
        def _():
            carry[...] = after_ref[...]

        grad = conv_ref[...]
        ext[:tile, :] = grad
        ext[tile:, :] = carry[...]
        carry[...] = grad[:8]
        product_grad = (
            scale_ref[2:3, :] * grad
            + marks_ref[:, 3:4] * scale_ref[3:4, :] * ext[1 : 1 + tile, :]
            + marks_ref[:, 4:5] * scale_ref[4:5, :] * ext[2 : 2 + tile, :]
        )
        grad_out[:, :width] = narrow(product_grad * value_ref[...].astype(FULL))
        grad_out[:, width : 2 * width] = open_ref[...]
        grad_out[:, 2 * width :] = narrow(product_grad * gate_ref[...].astype(FULL))

    def rows(last):
        return pl.BlockSpec((tile, last), lambda i: (steps - 1 - i, 0))

    row_spec = pl.BlockSpec((8, width), lambda i: ((steps - 1 - i) // per_row, 0))
    return pl.pallas_call(
        kernel,
        grid=(steps,),
        in_specs=[rows(8), rows(width), row_spec, rows(width), rows(width), rows(width), whole(scales.shape)],
        out_specs=rows(3 * width),
        out_shape=jax.ShapeDtypeStruct((tokens, 3 * width), LOW),
        scratch_shapes=[pltpu.VMEM((tile + 8, width), FULL), pltpu.VMEM((8, width), FULL)],
        compiler_params=pltpu.CompilerParams(vmem_limit_bytes=32 << 20),
        cost_estimate=pl.CostEstimate(flops=10 * tokens * width, bytes_accessed=16 << 20, transcendentals=0),
        name="project_grads",
    )(marks, conv_grad, after, gate, value, open_grad, scales)


def pair_grads(place, left, right, cores, name):
    tokens, width = left.shape
    block = right.shape[1] // 4
    eighth = width // 8
    count = len(cores)
    step = 256

    def kernel(place_ref, left_ref, right_ref, *outs):
        at = pl.program_id(0)
        for n in range(block // step):
            total = narrow(contract_rows(left_ref[...], right_ref[:, n * step : (n + 1) * step]))
            for c in range(count):
                @pl.when(at // 2 == c)
                def _():
                    for i in range(8):
                        outs[c][0, place_ref[2 + i], :, n * step : (n + 1) * step] = total[i * eighth : (i + 1) * eighth]

    def column(i, place_ref):
        return (0, place_ref[14 + 2 * cores[0] + i])

    def out_spec(c):
        return pl.BlockSpec(
            (1, 8, eighth, block), lambda i, place_ref: (jnp.clip(i - 2 * c, 0, 1), 0, 0, 0)
        )

    return pl.pallas_call(
        kernel,
        grid_spec=pltpu.PrefetchScalarGridSpec(
            num_scalar_prefetch=1,
            grid=(2 * count,),
            in_specs=[
                pl.BlockSpec((tokens, width), lambda i, place_ref: (0, 0), pipeline_mode=pl.Buffered(1)),
                pl.BlockSpec((tokens, block), column),
            ],
            out_specs=[out_spec(c) for c in range(count)],
        ),
        out_shape=[jax.ShapeDtypeStruct((2, 8, eighth, block), LOW)] * count,
        compiler_params=pltpu.CompilerParams(vmem_limit_bytes=32 << 20),
        cost_estimate=pl.CostEstimate(
            flops=count * 4 * tokens * width * block, bytes_accessed=8 << 20, transcendentals=0
        ),
        name=name,
    )(place, left, right)


def mixer_backward(project_grad, in_weight, hidden, residual_grad, sums, scales):
    tokens, width = hidden.shape
    tile = 256
    steps = tokens // tile

    def kernel(grad_ref, in_ref, hidden_ref, residual_ref, sums_ref, scale_ref, input_out, sums_out):
        @pl.when(pl.program_id(0) == 0)
        def _():
            sums_out[...] = sums_ref[...]

        normed_grad = contract_cols(grad_ref[...], in_ref[...])
        source = hidden_ref[...].astype(FULL)
        inverse = lax.rsqrt(jnp.mean(source * source, axis=1, keepdims=True) + EPS)
        sums_out[0:1, :] += jnp.sum(normed_grad * (source * inverse), axis=0, keepdims=True)
        scaled = scale_ref[0:1, :] * normed_grad
        lean = (inverse * inverse * inverse) * jnp.mean(scaled * source, axis=1, keepdims=True)
        input_out[...] = narrow(residual_ref[...] + inverse * scaled - source * lean)

    def rows(last):
        return pl.BlockSpec((tile, last), lambda i: (i, 0))

    small = pl.BlockSpec((8, width), lambda i: (0, 0))
    return pl.pallas_call(
        kernel,
        grid=(steps,),
        in_specs=[rows(3 * width), whole(in_weight.shape), rows(width), rows(width), small, whole(scales.shape)],
        out_specs=[rows(width), small],
        out_shape=[jax.ShapeDtypeStruct((tokens, width), LOW), jax.ShapeDtypeStruct((8, width), FULL)],
        compiler_params=pltpu.CompilerParams(vmem_limit_bytes=32 << 20),
        cost_estimate=pl.CostEstimate(flops=6 * tokens * width * width, bytes_accessed=20 << 20, transcendentals=0),
        name="mixer_backward",
    )(project_grad, in_weight, hidden, residual_grad, sums, scales)


def plain(
    hidden_in,
    mixer_gain,
    in_weight,
    conv_kernel,
    out_weight,
    feed_gain,
    gate_weight,
    up_weight,
    down_weight,
    document_lengths,
    valid_tokens,
    cotangent,
):
    row_count, span_length, model_width = hidden_in.shape
    token_count = row_count * span_length
    offset = lax.axis_index("seq") * span_length
    positions = offset + jnp.arange(span_length, dtype=jnp.int32)
    starts = jnp.cumsum(document_lengths, axis=1) - document_lengths
    is_start = jnp.any(positions[None, :, None] == starts[:, None, :], axis=2)
    before = jnp.any((positions - 1)[None, :, None] == starts[:, None, :], axis=2)
    keep_one = (1.0 - is_start.astype(jnp.float32))[:, :, None]
    keep_two = keep_one * (1.0 - before.astype(jnp.float32))[:, :, None]
    valid_mask = (
        (positions[None, :] < valid_tokens[:, None]).astype(jnp.float32).reshape(token_count, 1)
    )
    mixer_scale = mixer_gain.astype(jnp.float32)
    feed_scale = feed_gain.astype(jnp.float32)
    kernel = conv_kernel.astype(jnp.float32)
    source = hidden_in.astype(jnp.float32).reshape(token_count, model_width)
    inverse_one = lax.rsqrt(jnp.mean(source * source, axis=1, keepdims=True) + EPS)
    normed = (source * inverse_one * mixer_scale).astype(jnp.bfloat16)
    project = jnp.dot(normed, in_weight, preferred_element_type=jnp.float32)
    input_gate = project[:, :model_width]
    output_gate = project[:, model_width : 2 * model_width]
    values = project[:, 2 * model_width :]
    product = (
        (input_gate * values).astype(jnp.bfloat16).reshape(row_count, span_length, model_width)
    )
    rim_values = passed_along(product[:, span_length - 2 :, :], "seq", 1)
    extended = jnp.concatenate([rim_values, product], axis=1).astype(jnp.float32)
    tap_zero = extended[:, 2:, :]
    tap_one = keep_one * extended[:, 1:-1, :]
    tap_two = keep_two * extended[:, :-2, :]
    conv_out = (kernel[:, 0] * tap_zero + kernel[:, 1] * tap_one + kernel[:, 2] * tap_two).reshape(
        token_count, model_width
    )
    mixed_in = (output_gate * conv_out).astype(jnp.bfloat16)
    mixer_out = jnp.dot(mixed_in, out_weight, preferred_element_type=jnp.float32)
    residual = source + valid_mask * mixer_out
    inverse_two = lax.rsqrt(jnp.mean(residual * residual, axis=1, keepdims=True) + EPS)
    normed_two = (residual * inverse_two * feed_scale).astype(jnp.bfloat16)
    gate_pre = jnp.dot(normed_two, gate_weight, preferred_element_type=jnp.float32)
    up_pre = jnp.dot(normed_two, up_weight, preferred_element_type=jnp.float32)
    sigmoid_gate = jax.nn.sigmoid(gate_pre)
    activation = (gate_pre * sigmoid_gate * up_pre).astype(jnp.bfloat16)
    feed_out = jnp.dot(activation, down_weight, preferred_element_type=jnp.float32)
    output = (
        (residual + valid_mask * feed_out)
        .astype(jnp.bfloat16)
        .reshape(row_count, span_length, model_width)
    )
    upstream = cotangent.astype(jnp.float32).reshape(token_count, model_width)
    feed_grad = (valid_mask * upstream).astype(jnp.bfloat16)
    down_grad = contract_rows(activation, feed_grad)
    activation_grad = contract_cols(feed_grad, down_weight)
    up_grad = (activation_grad * gate_pre * sigmoid_gate).astype(jnp.bfloat16)
    gate_grad = (
        activation_grad * up_pre * sigmoid_gate * (1.0 + gate_pre * (1.0 - sigmoid_gate))
    ).astype(jnp.bfloat16)
    gate_wgrad = contract_rows(normed_two, gate_grad)
    up_wgrad = contract_rows(normed_two, up_grad)
    normed_two_grad = contract_cols(gate_grad, gate_weight) + contract_cols(up_grad, up_weight)
    feed_gain_grad = jnp.sum(normed_two_grad * residual * inverse_two, axis=0)
    scaled_two = feed_scale * normed_two_grad
    residual_grad = (
        upstream
        + inverse_two * scaled_two
        - residual
        * (inverse_two * inverse_two * inverse_two)
        * jnp.mean(scaled_two * residual, axis=1, keepdims=True)
    )
    feed_gain_part, gate_part, up_part, down_part = (
        lax.psum_scatter(
            feed_gain_grad.astype(jnp.bfloat16), "seq", scatter_dimension=0, tiled=True
        ).astype(jnp.float32),
        lax.psum_scatter(
            gate_wgrad.astype(jnp.bfloat16), "seq", scatter_dimension=0, tiled=True
        ).astype(jnp.float32),
        lax.psum_scatter(
            up_wgrad.astype(jnp.bfloat16), "seq", scatter_dimension=0, tiled=True
        ).astype(jnp.float32),
        lax.psum_scatter(
            down_grad.astype(jnp.bfloat16), "seq", scatter_dimension=0, tiled=True
        ).astype(jnp.float32),
    )
    gate_part, up_part, down_part = (
        lax.psum_scatter(
            gate_part.astype(jnp.bfloat16), "row", scatter_dimension=1, tiled=True
        ).astype(jnp.float32),
        lax.psum_scatter(
            up_part.astype(jnp.bfloat16), "row", scatter_dimension=1, tiled=True
        ).astype(jnp.float32),
        lax.psum_scatter(
            down_part.astype(jnp.bfloat16), "row", scatter_dimension=1, tiled=True
        ).astype(jnp.float32),
    )
    mixer_grad = (valid_mask * residual_grad).astype(jnp.bfloat16)
    out_wgrad = contract_rows(mixed_in, mixer_grad)
    mixed_grad = contract_cols(mixer_grad, out_weight)
    output_gate_grad = mixed_grad * conv_out
    conv_grad = (mixed_grad * output_gate).reshape(row_count, span_length, model_width)
    kernel_grad = jnp.stack(
        [
            jnp.sum(conv_grad * tap_zero, axis=(0, 1)),
            jnp.sum(conv_grad * tap_one, axis=(0, 1)),
            jnp.sum(conv_grad * tap_two, axis=(0, 1)),
        ],
        axis=1,
    )
    grad_zero = kernel[:, 0] * conv_grad
    grad_one = keep_one * kernel[:, 1] * conv_grad
    grad_two = keep_two * kernel[:, 2] * conv_grad
    extended_grad = (
        jnp.pad(grad_zero, ((0, 0), (2, 0), (0, 0)))
        + jnp.pad(grad_one, ((0, 0), (1, 1), (0, 0)))
        + jnp.pad(grad_two, ((0, 0), (0, 2), (0, 0)))
    )
    returned = passed_along(extended_grad[:, :2, :], "seq", -1)
    product_grad = extended_grad[:, 2:, :] + jnp.pad(
        returned, ((0, 0), (span_length - 2, 0), (0, 0))
    )
    flat_grad = product_grad.reshape(token_count, model_width)
    project_grad = jnp.concatenate(
        [flat_grad * values, output_gate_grad, flat_grad * input_gate], axis=1
    ).astype(jnp.bfloat16)
    in_wgrad = contract_rows(normed, project_grad)
    normed_grad = contract_cols(project_grad, in_weight)
    mixer_gain_grad = jnp.sum(normed_grad * source * inverse_one, axis=0)
    scaled_one = mixer_scale * normed_grad
    input_grad = (
        residual_grad
        + inverse_one * scaled_one
        - source
        * (inverse_one * inverse_one * inverse_one)
        * jnp.mean(scaled_one * source, axis=1, keepdims=True)
    )
    input_grad = input_grad.astype(jnp.bfloat16).reshape(row_count, span_length, model_width)
    mixer_gain_part, in_part, kernel_part, out_part = (
        lax.psum_scatter(
            mixer_gain_grad.astype(jnp.bfloat16), "seq", scatter_dimension=0, tiled=True
        ).astype(jnp.float32),
        lax.psum_scatter(
            in_wgrad.astype(jnp.bfloat16), "seq", scatter_dimension=0, tiled=True
        ).astype(jnp.float32),
        lax.psum_scatter(
            kernel_grad.astype(jnp.bfloat16), "seq", scatter_dimension=0, tiled=True
        ).astype(jnp.float32),
        lax.psum_scatter(
            out_wgrad.astype(jnp.bfloat16), "seq", scatter_dimension=0, tiled=True
        ).astype(jnp.float32),
    )
    in_part, out_part = (
        lax.psum_scatter(
            in_part.astype(jnp.bfloat16), "row", scatter_dimension=1, tiled=True
        ).astype(jnp.float32),
        lax.psum_scatter(
            out_part.astype(jnp.bfloat16), "row", scatter_dimension=1, tiled=True
        ).astype(jnp.float32),
    )
    mixer_gain_part, feed_gain_part, kernel_part = lax.psum(
        (mixer_gain_part, feed_gain_part, kernel_part), "row"
    )
    return (
        output,
        input_grad,
        mixer_gain_part,
        in_part,
        kernel_part,
        out_part,
        feed_gain_part,
        gate_part,
        up_part,
        down_part,
    )


LINKS = {"x": ("row", 2), "y": ("seq", 1), "z0": ("seq", 2), "z1": ("seq", 4)}


def settle(value, order):
    names = [name for name in ("x", "z1", "z0", "y") if name in order[len(order) - value.ndim + 2 :]]
    for name in order[len(order) - len(names) :]:
        at = names.index(name)
        names.remove(name)
        give = lax.index_in_dim(value, 0, at, keepdims=False)
        keep = lax.index_in_dim(value, 1, at, keepdims=False)
        value = wide(keep, swapped(narrow(give), *LINKS[name]))
        if names:
            value = narrow(value)
    return value


def fast(
    hidden_in,
    mixer_gain,
    in_weight,
    conv_kernel,
    out_weight,
    feed_gain,
    gate_weight,
    up_weight,
    down_weight,
    document_lengths,
    valid_tokens,
    cotangent,
):
    row_count, span_length, model_width = hidden_in.shape
    token_count = row_count * span_length
    hidden_width = gate_weight.shape[1]
    block = hidden_width // 4
    chunks = 3
    part = block // chunks
    seq = lax.axis_index("seq")
    row = lax.axis_index("row")
    row_x, core = row // 2, row % 2
    seq_y, seq_z0, seq_z1 = seq % 2, (seq // 2) % 2, seq // 4
    place = jnp.stack(
        [row ^ 2, row]
        + [i ^ seq ^ 7 for i in range(8)]
        + [1 - row_x, row_x, 1 - ((1 - row_x) ^ seq_z1), 1 - (row_x ^ seq_z1)]
        + [row ^ 3, row ^ 1, row ^ 2, row]
    ).astype(jnp.int32)
    positions = seq * span_length + jnp.arange(span_length, dtype=jnp.int32)
    starts = jnp.cumsum(document_lengths, axis=1) - document_lengths

    def unstarted(shift):
        return 1.0 - jnp.any((positions + shift)[None, :, None] == starts[:, None, :], axis=2).astype(FULL)

    here, last, one_on, two_on = (unstarted(shift) for shift in (0, -1, 1, 2))
    valid = (positions[None, :] < valid_tokens[:, None]).astype(FULL)
    blank = jnp.zeros_like(valid)
    marks = jnp.stack([here, here * last, valid, one_on, two_on * one_on, blank, blank, blank], axis=2).reshape(
        token_count, 8
    )
    valid_mask = marks[:, 2:3]
    scales = jnp.concatenate(
        [mixer_gain[None], feed_gain[None], conv_kernel.T, jnp.zeros((3, model_width), conv_kernel.dtype)]
    ).astype(FULL)
    hidden = hidden_in.reshape(token_count, model_width)
    upstream = cotangent.reshape(token_count, model_width)
    rim = passed_along(hidden_in[:, span_length - 2 :, :], "seq", 1)
    rim = jnp.pad(rim, ((0, 0), (MARGIN - 2, 0), (0, 0))).reshape(row_count * MARGIN, model_width)
    feed_grad = narrow(valid_mask * upstream.astype(FULL))
    other_grad = swapped(feed_grad, "row", 1)
    normed, input_gate, output_gate, values, product, mixed_in, residual, normed_two, before = mixer_forward(
        marks, hidden, rim, in_weight, out_weight, scales
    )
    other_normed = swapped(normed_two, "row", 1)

    def chunk_grads(start, chunk):
        return feed_chunk(
            start, normed_two, other_normed, feed_grad, other_grad, gate_weight, up_weight, down_weight, chunk, chunks
        )

    def sent(made):
        gs, us, ds = made[3], made[5], made[7]
        return swapped(gs, "seq", 2), swapped(us, "seq", 1), swapped(ds, "row", 2)

    def first_sums(made, taken, behind):
        (gk, uk, dk, taken), _ = lax.optimization_barrier(((made[4], made[6], made[8], taken), behind))
        gate, up, down = (wide(keep, take) for keep, take in zip((gk, uk, dk), taken))
        return narrow(gate[0]), narrow(gate[1]), narrow(up[0]), narrow(up[1]), narrow(down)

    def follow(value, *ahead):
        return lax.optimization_barrier((value,) + ahead)[0]

    made0 = chunk_grads(place, 0)
    taken0 = sent(made0)
    made1 = chunk_grads(follow(place, made0[0]), 1)
    taken1 = sent(made1)
    sums0 = first_sums(made0, taken0, made1[0])
    gate0, up0 = swapped(sums0[0], "row", 2), swapped(sums0[2], "row", 2)
    made2 = chunk_grads(follow(place, sums0), 2)
    taken2 = sent(made2)
    sums1 = first_sums(made1, taken1, made2[0])
    gate1, up1 = swapped(sums1[0], "row", 2), swapped(sums1[2], "row", 2)
    made = (made0, made1, made2)
    acts, gates, ups = ([one[i] for one in made] for i in range(3))
    own_ntg, give_ntg = feed_sum(
        follow(place, sums1), [gates, ups], [gate_weight, up_weight], True, block, "normed_two_grad"
    )
    take_ntg = swapped(give_ntg, "row", 1)
    sums2 = first_sums(made2, taken2, own_ntg)
    gate2, up2 = swapped(sums2[0], "row", 2), swapped(sums2[2], "row", 2)
    down = jnp.concatenate([sums0[4], sums1[4], sums2[4]], axis=1)
    low_half, high_half = down[:, : block // 2], down[:, block // 2 :]
    down_keep = jnp.where(seq_y == 0, low_half, high_half)
    down_take = swapped(jnp.where(seq_y == 0, high_half, low_half), "seq", 1)
    own_feed, give_feed = feed_sum(
        follow(place, sums2), [acts], [down_weight], False, block, "feed_out"
    )
    take_feed = swapped(give_feed, "row", 1)

    residual_grad, mixer_grad, open_grad, conv_grad, sums = mixer_middle(
        follow(marks, own_feed), own_ntg, take_ntg, residual, upstream, product, before, output_gate, out_weight, scales
    )
    after = passed_along(conv_grad.reshape(row_count, span_length, model_width)[:, :2, :], "seq", -1)
    after = jnp.pad(after, ((0, 0), (0, 6), (0, 0))).reshape(row_count * 8, model_width)

    (gate_take, up_take), _ = lax.optimization_barrier((([gate0, gate1, gate2], [up0, up1, up2]), mixer_grad))
    sums_all = (sums0, sums1, sums2)
    gate = jnp.stack([wide(one[1], take) for one, take in zip(sums_all, gate_take)])
    gate_keep, gate_give = narrow(gate[:, :, 1]), narrow(gate[:, :, 0])
    up = jnp.stack(
        [wide(one[3], take).reshape(2, 2, model_width // 8, part) for one, take in zip(sums_all, up_take)]
    )
    up_keep, up_give = narrow(up[:, :, 1]), narrow(up[:, :, 0])
    gate_take = swapped(gate_give, "seq", 1)
    up_take = swapped(up_give, "seq", 2)

    project_grad = project_grads(
        follow(marks, gate_give, up_give), conv_grad, after, input_gate, values, open_grad, scales
    )
    (in_give,) = pair_grads(place, normed, project_grad, (0,), "in_grads_give")
    in_take = swapped(in_give, "row", 1)
    (in_keep,) = pair_grads(follow(place, in_give), normed, project_grad, (1,), "in_grads_keep")
    out_give, out_keep = pair_grads(follow(place, in_keep), mixed_in, mixer_grad, (0, 1), "out_grads")

    def sided(value):
        return value.reshape(2, 2, 2, 2, value.shape[-2], value.shape[-1])

    orders = (("x", "y", "z0", "z1"), ("y", "x", "z0", "z1"), ("z0", "x", "y", "z1"))
    (in_keep, in_take), _ = lax.optimization_barrier(((in_keep, in_take), out_keep))
    in_sum = sided(narrow(wide(in_keep, in_take)))
    third = in_sum.shape[-1] // 3
    names = ["x", "z1", "z0", "y"]
    firsts = []
    for i, order in enumerate(orders):
        piece = in_sum[..., i * third : (i + 1) * third]
        at = names.index(order[0])
        firsts.append((lax.index_in_dim(piece, 1, at, False), lax.index_in_dim(piece, 0, at, False)))
    in_moved = [swapped(give, *LINKS[order[0]]) for (_, give), order in zip(firsts, orders)]
    out_take = swapped(out_give, "row", 1)
    down = narrow(wide(down_keep, down_take))
    down_keep, down_give = down[1], down[0]
    down_take = swapped(down_give, "seq", 4)

    input_grad, small = mixer_backward(
        follow(project_grad, [give for _, give in firsts], down_give), in_weight, hidden, residual_grad, sums, scales
    )
    in_moved, _ = lax.optimization_barrier((in_moved, input_grad))
    input_grad = input_grad.reshape(row_count, span_length, model_width)
    in_part = jnp.concatenate(
        [
            settle(narrow(wide(keep, take)), order)
            for (keep, _), take, order in zip(firsts, in_moved, orders)
        ],
        axis=1,
    )
    out_part = settle(sided(narrow(wide(out_keep, out_take))), ("y", "z0", "x", "z1"))
    for axis, bit in (("row", 1), ("row", 2), ("seq", 1), ("seq", 2), ("seq", 4)):
        small = small + swapped(small, axis, bit)
    small = lax.dynamic_slice_in_dim(small, seq * (model_width // 8), model_width // 8, 1)

    output = narrow(residual + valid_mask * wide(own_feed, take_feed)).reshape(row_count, span_length, model_width)
    (gate_take, up_take), _ = lax.optimization_barrier(((gate_take, up_take), input_grad))
    gate = wide(gate_keep, gate_take)
    gate = wide(narrow(gate[:, 1]), swapped(narrow(gate[:, 0]), "seq", 4))
    gate_part = jnp.concatenate([gate[i] for i in range(chunks)], axis=1)
    up = wide(up_keep, up_take)
    up = wide(narrow(up[:, 1]), swapped(narrow(up[:, 0]), "seq", 4))
    up_part = jnp.concatenate([up[i] for i in range(chunks)], axis=1)
    down_take, _ = lax.optimization_barrier((down_take, input_grad))
    down = narrow(wide(down_keep, down_take))
    holder = [[(r & 1) == ((s >> 1) & 1) for r in range(4)] for s in range(8)]
    down = wide(
        down,
        lax.ppermute(
            down,
            ("seq", "row"),
            [(s * 4 + r, (s ^ 2) * 4 + r) for s in range(8) for r in range(4) if not holder[s][r]],
        ),
    )
    quarter = model_width // 4
    down_own = jnp.where(core == 0, down[:, :quarter], down[:, quarter:])
    down_other = narrow(jnp.where(core == 0, down[:, quarter:], down[:, :quarter]))
    down_other = lax.ppermute(
        down_other,
        ("seq", "row"),
        [(s * 4 + r, s * 4 + (r ^ 1)) for s in range(8) for r in range(4) if holder[s][r]],
    )
    down_part = jnp.where(core == seq_z0, down_own, down_other.astype(jnp.float32))
    return (
        output,
        input_grad,
        small[0],
        in_part,
        small[2:5].T,
        out_part,
        small[1],
        gate_part,
        up_part,
        down_part,
    )


def local(*args):
    hidden_in, gate_weight = args[0], args[6]
    tokens = hidden_in.shape[0] * hidden_in.shape[1]
    width, hidden = gate_weight.shape
    tiled = lax.axis_size("seq") == 8 and lax.axis_size("row") == 4 and hidden % (4 * 3 * 128) == 0
    if tiled and width % 1024 == 0 and tokens % 512 == 0:
        return fast(*args)
    return plain(*args)


def solution(mesh):
    in_specs = (
        P("row", "seq", None),
        P(),
        P(),
        P(),
        P(),
        P(),
        P(),
        P(),
        P(),
        P("row", None),
        P("row"),
        P("row", "seq", None),
    )
    out_specs = (
        P("row", "seq", None),
        P("row", "seq", None),
        P("seq"),
        P("seq", "row"),
        P("seq", None),
        P("seq", "row"),
        P("seq"),
        P("seq", "row"),
        P("seq", "row"),
        P("seq", "row"),
    )
    return jax.shard_map(local, mesh=mesh, in_specs=in_specs, out_specs=out_specs, check_vma=False)
```

```python
import jax
import jax.numpy as jnp
from jax import lax
from jax.experimental import pallas as pl
from jax.experimental.pallas import tpu as pltpu
from jax.sharding import PartitionSpec as P

EPS = 1e-05


def passed_along(value, axis, by):
    length = lax.axis_size(axis)
    pairs = [(i, i + by) for i in range(length) if 0 <= i + by < length]
    return lax.ppermute(value, axis, pairs)


def contract_rows(left, right):
    return lax.dot_general(
        left, right, (((0,), (0,)), ((), ())), preferred_element_type=jnp.float32
    )


def contract_cols(left, right):
    return lax.dot_general(
        left, right, (((1,), (1,)), ((), ())), preferred_element_type=jnp.float32
    )


def swapped(value, axis, bit):
    length = lax.axis_size(axis)
    return lax.ppermute(value, axis, [(i, i ^ bit) for i in range(length)])


def wide(left, right):
    return left.astype(jnp.float32) + right.astype(jnp.float32)


def narrow(value):
    return value.astype(jnp.bfloat16)


def feed_chunk(place, own_in, other_in, own_grad, other_grad, gate_weight, up_weight, down_weight, chunk, chunks):
    tokens, width = own_in.shape
    hidden = gate_weight.shape[1]
    rows = 2
    block = hidden // 4
    part = block // chunks
    span = rows * part
    tile = min(512, tokens)
    tiles = 2 * tokens // tile
    half_tiles = tokens // tile
    eighth = width // 8
    step = 256

    def kernel(
        place_ref, own_ref, other_ref, own_grad_ref, other_grad_ref, gate_ref, up_ref, down_ref,
        act_out, gate_out, up_out, gate_send, gate_keep, up_send, up_keep, down_send, down_keep,
        tok, grd, wg, wu, wd, act, gg, ug, gw, uw, dw, in_sem, w_sem, out_sem, grad_sem,
    ):
        def token_copy(t, which):
            buf = (tok, grd)[which]
            src = ((own_ref, other_ref), (own_grad_ref, other_grad_ref))[which][0 if t < half_tiles else 1]
            return pltpu.make_async_copy(
                src.at[pl.ds((t % half_tiles) * tile, tile)],
                buf.at[pl.ds(t * tile, tile)],
                in_sem.at[which, t],
            )

        weight_copies = []
        for n, (ref, buf) in enumerate(((gate_ref, wg), (up_ref, wu))):
            weight_copies.append([
                pltpu.make_async_copy(
                    ref.at[:, pl.ds(pl.multiple_of(place_ref[j] * block + chunk * part, 128), part)],
                    buf.at[:, pl.ds(j * part, part)],
                    w_sem.at[n, j],
                )
                for j in range(2)
            ])
        weight_copies.append([
            pltpu.make_async_copy(
                down_ref.at[pl.ds(pl.multiple_of(place_ref[j] * block + chunk * part, 128), part), :],
                wd.at[pl.ds(j * part, part), :],
                w_sem.at[2, j],
            )
            for j in range(2)
        ])
        token_copy(0, 0).start()
        for copy in weight_copies[0]:
            copy.start()
        for copy in weight_copies[1]:
            copy.start()
        token_copy(0, 1).start()
        for copy in weight_copies[2]:
            copy.start()
        outs = []
        for t in range(tiles):
            at = pl.ds(t * tile, tile)
            token_copy(t, 0).wait()
            if t == 0:
                for copy in weight_copies[0] + weight_copies[1]:
                    copy.wait()
            if t + 1 < tiles:
                token_copy(t + 1, 0).start()
                token_copy(t + 1, 1).start()
            token_copy(t, 1).wait()
            if t == 0:
                for copy in weight_copies[2]:
                    copy.wait()
            for n in range(span // step):
                cols = pl.ds(n * step, step)
                gate = jnp.dot(tok[at, :], wg[:, cols], preferred_element_type=jnp.float32)
                up = jnp.dot(tok[at, :], wu[:, cols], preferred_element_type=jnp.float32)
                grad = contract_cols(grd[at, :], wd[cols, :])
                sig = jax.nn.sigmoid(gate)
                gate_sig = gate * sig
                act[at, cols] = narrow(gate_sig * up)
                ug[at, cols] = narrow(grad * gate_sig)
                gg[at, cols] = narrow(grad * up * (sig + gate_sig * (1.0 - sig)))
            for n, (buf, out) in enumerate(((act, act_out), (gg, gate_out), (ug, up_out))):
                copy = pltpu.make_async_copy(buf.at[at], out.at[at], out_sem.at[n, t])
                copy.start()
                outs.append(copy)

        for buf, grad in ((gw, gg), (uw, ug)):
            for n in range(span // step):
                cols = pl.ds(n * step, step)
                total = narrow(contract_rows(tok[...], grad[:, cols]))
                for i in range(8):
                    spot = place_ref[2 + i]
                    rows_i = total[i * eighth : (i + 1) * eighth]
                    for c in range(step // 128):
                        col = n * step + c * 128
                        buf[col // part, spot, :, pl.ds(col % part, 128)] = rows_i[:, c * 128 : (c + 1) * 128]
            if buf is gw:
                pairs = [
                    (gw.at[j, pl.ds(4 * h + 2 * z, 2)], out.at[:, j, h], grad_sem.at[8 + 4 * z + 2 * j + h])
                    for z, out in enumerate((gate_send, gate_keep))
                    for j in range(2)
                    for h in range(2)
                ]
            else:
                pairs = [
                    (uw.at[j, 4 * h + 2 * z + y], out.at[z, j, h], grad_sem.at[16 + 8 * y + 4 * z + 2 * j + h])
                    for y, out in enumerate((up_send, up_keep))
                    for z in range(2)
                    for j in range(2)
                    for h in range(2)
                ]
            for src, out, sem in pairs:
                copy = pltpu.make_async_copy(src, out, sem)
                copy.start()
                outs.append(copy)
        for side in range(2):
            for n in range(2):
                cols = pl.ds(pl.multiple_of(place_ref[10 + side] * (width // 2) + n * (width // 4), 128), width // 4)
                total = narrow(contract_rows(act[...], grd[:, cols]))
                for j in range(2):
                    dw[side, place_ref[12 + j], :, pl.ds(n * (width // 4), width // 4)] = total[j * part : (j + 1) * part]
            copy = pltpu.make_async_copy(dw.at[side], (down_send, down_keep)[side], grad_sem.at[side])
            copy.start()
            outs.append(copy)
        for copy in outs:
            copy.wait()

    any_spec = pl.BlockSpec(memory_space=pltpu.HBM)
    low = jnp.bfloat16
    both = 2 * tokens
    flops = 6 * 2 * both * width * span
    return pl.pallas_call(
        kernel,
        out_shape=[jax.ShapeDtypeStruct((both, span), low)] * 3
        + [jax.ShapeDtypeStruct((2, 2, 2, eighth, part), low)] * 4
        + [jax.ShapeDtypeStruct((2, part, width // 2), low)] * 2,
        grid_spec=pltpu.PrefetchScalarGridSpec(
            num_scalar_prefetch=1,
            grid=(1,),
            in_specs=[any_spec] * 7,
            out_specs=[any_spec] * 9,
            scratch_shapes=[
                pltpu.VMEM((both, width), low),
                pltpu.VMEM((both, width), low),
                pltpu.VMEM((width, span), low),
                pltpu.VMEM((width, span), low),
                pltpu.VMEM((span, width), low),
                pltpu.VMEM((both, span), low),
                pltpu.VMEM((both, span), low),
                pltpu.VMEM((both, span), low),
                pltpu.VMEM((2, 8, eighth, part), low),
                pltpu.VMEM((2, 8, eighth, part), low),
                pltpu.VMEM((2, 2, part, width // 2), low),
                pltpu.SemaphoreType.DMA((2, tiles)),
                pltpu.SemaphoreType.DMA((3, 2)),
                pltpu.SemaphoreType.DMA((3, tiles)),
                pltpu.SemaphoreType.DMA((32,)),
            ],
        ),
        compiler_params=pltpu.CompilerParams(vmem_limit_bytes=56 << 20),
        cost_estimate=pl.CostEstimate(flops=flops, bytes_accessed=24 << 20, transcendentals=both * span),
        name=f"feed_{chunk}",
    )(place, own_in, other_in, own_grad, other_grad, gate_weight, up_weight, down_weight)


def feed_sum(place, groups, weights, across, block, name):
    chunks = len(groups[0])
    both, span = groups[0][0].shape
    part = span // 2
    width = weights[0].shape[0] if across else weights[0].shape[1]
    tokens = both // 2
    tile = min(512, tokens)
    tiles = both // tile
    half_tiles = tiles // 2
    kinds = len(groups)

    def kernel(place_ref, *refs):
        lefts = [refs[g * chunks : (g + 1) * chunks] for g in range(kinds)]
        rights = refs[kinds * chunks : kinds * chunks + kinds]
        own_out, other_out, lbuf, wbuf, total, obuf, l_sem, w_sem, o_sem = refs[kinds * chunks + kinds :]

        def weight_copies(k):
            slot = k % 2
            copies = []
            for g in range(kinds):
                for j in range(2):
                    rows = pl.ds(pl.multiple_of(place_ref[j] * block + k * part, 128), part)
                    if across:
                        src, dst = rights[g].at[:, rows], wbuf.at[slot, g, :, pl.ds(j * part, part)]
                    else:
                        src, dst = rights[g].at[rows, :], wbuf.at[slot, g, pl.ds(j * part, part), :]
                    copies.append(pltpu.make_async_copy(src, dst, w_sem.at[slot, g, j]))
            return copies

        def left_copies(k, t, slot):
            return [
                pltpu.make_async_copy(lefts[g][k].at[pl.ds(t * tile, tile)], lbuf.at[slot, g], l_sem.at[slot, g])
                for g in range(kinds)
            ]

        def out_copy(t, slot):
            ref = own_out if t < half_tiles else other_out
            return pltpu.make_async_copy(
                obuf.at[slot], ref.at[pl.ds((t % half_tiles) * tile, tile)], o_sem.at[slot]
            )

        for copy in left_copies(0, 0, 0) + weight_copies(0):
            copy.start()
        for k in range(chunks):
            for t in range(tiles):
                n = k * tiles + t
                for copy in left_copies(k, t, n % 2):
                    copy.wait()
                if t == 0:
                    for copy in weight_copies(k):
                        copy.wait()
                if n + 1 < chunks * tiles:
                    for copy in left_copies((n + 1) // tiles, (n + 1) % tiles, (n + 1) % 2):
                        copy.start()
                if t == 0 and k + 1 < chunks:
                    for copy in weight_copies(k + 1):
                        copy.start()
                value = None
                for g in range(kinds):
                    left, right = lbuf[n % 2, g], wbuf[k % 2, g]
                    term = contract_cols(left, right) if across else jnp.dot(left, right, preferred_element_type=jnp.float32)
                    value = term if value is None else value + term
                if k > 0:
                    value = value + total[t]
                if k + 1 < chunks:
                    total[t] = value
                else:
                    if t >= 2:
                        out_copy(t - 2, t % 2).wait()
                    obuf[t % 2] = narrow(value)
                    out_copy(t, t % 2).start()
        for t in range(max(0, tiles - 2), tiles):
            out_copy(t, t % 2).wait()

    any_spec = pl.BlockSpec(memory_space=pltpu.HBM)
    low = jnp.bfloat16
    wshape = (width, span) if across else (span, width)
    return pl.pallas_call(
        kernel,
        out_shape=[jax.ShapeDtypeStruct((tokens, width), low)] * 2,
        grid_spec=pltpu.PrefetchScalarGridSpec(
            num_scalar_prefetch=1,
            grid=(1,),
            in_specs=[any_spec] * (kinds * chunks + kinds),
            out_specs=[any_spec] * 2,
            scratch_shapes=[
                pltpu.VMEM((2, kinds, tile, span), low),
                pltpu.VMEM((2, kinds) + wshape, low),
                pltpu.VMEM((tiles, tile, width), jnp.float32),
                pltpu.VMEM((2, tile, width), low),
                pltpu.SemaphoreType.DMA((2, kinds)),
                pltpu.SemaphoreType.DMA((2, kinds, 2)),
                pltpu.SemaphoreType.DMA((2,)),
            ],
        ),
        compiler_params=pltpu.CompilerParams(vmem_limit_bytes=48 << 20),
        cost_estimate=pl.CostEstimate(
            flops=kinds * chunks * 2 * both * width * span, bytes_accessed=24 << 20, transcendentals=0
        ),
        name=name,
    )(place, *[item for group in groups for item in group], *weights)


LOW = jnp.bfloat16
FULL = jnp.float32
MARGIN = 16


def whole(shape):
    return pl.BlockSpec(shape, lambda *_: (0,) * len(shape), pipeline_mode=pl.Buffered(1))


def mixer_forward(marks, hidden, rim, in_weight, out_weight, scales):
    tokens, width = hidden.shape
    tile = 256
    per_row = tokens // 2 // tile
    steps = tokens // tile

    def kernel(
        marks_ref, hidden_ref, rim_ref, in_ref, out_ref, scale_ref,
        normed_out, gate_out, open_out, value_out, product_out, mixed_out, residual_out, next_out, before_out,
        ext, carry,
    ):
        at = pl.program_id(0) % per_row
        tile_in = hidden_ref[...].astype(FULL)

        @pl.when(at == 0)
        def _():
            carry[...] = rim_ref[...].astype(FULL)

        source = jnp.concatenate([carry[...], tile_in], axis=0)
        carry[...] = tile_in[tile - MARGIN :]
        inverse = lax.rsqrt(jnp.mean(source * source, axis=1, keepdims=True) + EPS)
        normed = narrow(source * inverse * scale_ref[0:1, :])
        gate = jnp.dot(normed, in_ref[:, :width], preferred_element_type=FULL)
        value = jnp.dot(normed, in_ref[:, 2 * width :], preferred_element_type=FULL)
        product = narrow(gate * value)
        ext[...] = product.astype(FULL)
        opened = jnp.dot(normed[MARGIN:], in_ref[:, width : 2 * width], preferred_element_type=FULL)
        conv = (
            scale_ref[2:3, :] * ext[MARGIN:, :]
            + marks_ref[:, 0:1] * scale_ref[3:4, :] * ext[MARGIN - 1 : MARGIN - 1 + tile, :]
            + marks_ref[:, 1:2] * scale_ref[4:5, :] * ext[MARGIN - 2 : MARGIN - 2 + tile, :]
        )
        mixed = narrow(opened * conv)
        residual = tile_in + marks_ref[:, 2:3] * jnp.dot(mixed, out_ref[...], preferred_element_type=FULL)
        inverse_two = lax.rsqrt(jnp.mean(residual * residual, axis=1, keepdims=True) + EPS)
        next_out[...] = narrow(residual * inverse_two * scale_ref[1:2, :])
        normed_out[...] = normed[MARGIN:]
        gate_out[...] = narrow(gate[MARGIN:])
        open_out[...] = narrow(opened)
        value_out[...] = narrow(value[MARGIN:])
        product_out[...] = product[MARGIN:]
        mixed_out[...] = mixed
        residual_out[...] = residual

        @pl.when(at == 0)
        def _():
            before_out[...] = product[:MARGIN]

    def rows(last, size=tile):
        return pl.BlockSpec((size, last), lambda i: (i, 0))

    row_spec = pl.BlockSpec((MARGIN, width), lambda i: (i // per_row, 0))
    return pl.pallas_call(
        kernel,
        grid=(steps,),
        in_specs=[rows(8), rows(width), row_spec, whole(in_weight.shape), whole(out_weight.shape), whole(scales.shape)],
        out_specs=[rows(width)] * 8 + [row_spec],
        out_shape=[jax.ShapeDtypeStruct((tokens, width), LOW)] * 6
        + [jax.ShapeDtypeStruct((tokens, width), FULL), jax.ShapeDtypeStruct((tokens, width), LOW)]
        + [jax.ShapeDtypeStruct((2 * MARGIN, width), LOW)],
        scratch_shapes=[pltpu.VMEM((tile + MARGIN, width), FULL), pltpu.VMEM((MARGIN, width), FULL)],
        compiler_params=pltpu.CompilerParams(vmem_limit_bytes=44 << 20),
        cost_estimate=pl.CostEstimate(flops=8 * tokens * width * width, bytes_accessed=28 << 20, transcendentals=0),
        name="mixer_forward",
    )(marks, hidden, rim, in_weight, out_weight, scales)


def mixer_middle(marks, own, other, residual, cotangent, product, before, opened, out_weight, scales):
    tokens, width = own.shape
    tile = 256
    per_row = tokens // 2 // tile
    steps = tokens // tile

    def kernel(
        marks_ref, own_ref, other_ref, residual_ref, cot_ref, product_ref, before_ref, open_ref, out_ref, scale_ref,
        grad_out, mixer_out, open_grad_out, conv_out, sums_out,
        ext, carry,
    ):
        step = pl.program_id(0)
        at = step % per_row

        @pl.when(at == 0)
        def _():
            carry[...] = before_ref[...].astype(FULL)

        @pl.when(step == 0)
        def _():
            sums_out[...] = jnp.zeros_like(sums_out)

        grad = own_ref[...].astype(FULL) + other_ref[...].astype(FULL)
        residual = residual_ref[...]
        inverse = lax.rsqrt(jnp.mean(residual * residual, axis=1, keepdims=True) + EPS)
        sums_out[1:2, :] += jnp.sum(grad * (residual * inverse), axis=0, keepdims=True)
        scaled = scale_ref[1:2, :] * grad
        lean = (inverse * inverse * inverse) * jnp.mean(scaled * residual, axis=1, keepdims=True)
        residual_grad = cot_ref[...].astype(FULL) + inverse * scaled - residual * lean
        grad_out[...] = residual_grad
        mixer = narrow(marks_ref[:, 2:3] * residual_grad)
        mixer_out[...] = mixer
        mixed = contract_cols(mixer, out_ref[...])
        product = product_ref[...].astype(FULL)
        ext[:MARGIN, :] = carry[...]
        ext[MARGIN:, :] = product
        carry[...] = product[tile - MARGIN :]
        one = marks_ref[:, 0:1] * ext[MARGIN - 1 : MARGIN - 1 + tile, :]
        two = marks_ref[:, 1:2] * ext[MARGIN - 2 : MARGIN - 2 + tile, :]
        conv = scale_ref[2:3, :] * product + scale_ref[3:4, :] * one + scale_ref[4:5, :] * two
        open_grad_out[...] = narrow(mixed * conv)
        conv_grad = mixed * open_ref[...].astype(FULL)
        conv_out[...] = conv_grad
        sums_out[2:3, :] += jnp.sum(conv_grad * product, axis=0, keepdims=True)
        sums_out[3:4, :] += jnp.sum(conv_grad * one, axis=0, keepdims=True)
        sums_out[4:5, :] += jnp.sum(conv_grad * two, axis=0, keepdims=True)

    def rows(last):
        return pl.BlockSpec((tile, last), lambda i: (i, 0))

    row_spec = pl.BlockSpec((MARGIN, width), lambda i: (i // per_row, 0))
    return pl.pallas_call(
        kernel,
        grid=(steps,),
        in_specs=[rows(8)] + [rows(width)] * 5 + [row_spec, rows(width), whole(out_weight.shape), whole(scales.shape)],
        out_specs=[rows(width)] * 4 + [pl.BlockSpec((8, width), lambda i: (0, 0))],
        out_shape=[jax.ShapeDtypeStruct((tokens, width), kind) for kind in (FULL, LOW, LOW, FULL)]
        + [jax.ShapeDtypeStruct((8, width), FULL)],
        scratch_shapes=[pltpu.VMEM((tile + MARGIN, width), FULL), pltpu.VMEM((MARGIN, width), FULL)],
        compiler_params=pltpu.CompilerParams(vmem_limit_bytes=44 << 20),
        cost_estimate=pl.CostEstimate(flops=2 * tokens * width * width, bytes_accessed=32 << 20, transcendentals=0),
        name="mixer_middle",
    )(marks, own, other, residual, cotangent, product, before, opened, out_weight, scales)


def project_grads(marks, conv_grad, after, gate, value, open_grad, scales):
    tokens, width = conv_grad.shape
    tile = 256
    per_row = tokens // 2 // tile
    steps = tokens // tile

    def kernel(marks_ref, conv_ref, after_ref, gate_ref, value_ref, open_ref, scale_ref, grad_out, ext, carry):
        at = (steps - 1 - pl.program_id(0)) % per_row

        @pl.when(at == per_row - 1)
        def _():
            carry[...] = after_ref[...]

        grad = conv_ref[...]
        ext[:tile, :] = grad
        ext[tile:, :] = carry[...]
        carry[...] = grad[:8]
        product_grad = (
            scale_ref[2:3, :] * grad
            + marks_ref[:, 3:4] * scale_ref[3:4, :] * ext[1 : 1 + tile, :]
            + marks_ref[:, 4:5] * scale_ref[4:5, :] * ext[2 : 2 + tile, :]
        )
        grad_out[:, :width] = narrow(product_grad * value_ref[...].astype(FULL))
        grad_out[:, width : 2 * width] = open_ref[...]
        grad_out[:, 2 * width :] = narrow(product_grad * gate_ref[...].astype(FULL))

    def rows(last):
        return pl.BlockSpec((tile, last), lambda i: (steps - 1 - i, 0))

    row_spec = pl.BlockSpec((8, width), lambda i: ((steps - 1 - i) // per_row, 0))
    return pl.pallas_call(
        kernel,
        grid=(steps,),
        in_specs=[rows(8), rows(width), row_spec, rows(width), rows(width), rows(width), whole(scales.shape)],
        out_specs=rows(3 * width),
        out_shape=jax.ShapeDtypeStruct((tokens, 3 * width), LOW),
        scratch_shapes=[pltpu.VMEM((tile + 8, width), FULL), pltpu.VMEM((8, width), FULL)],
        compiler_params=pltpu.CompilerParams(vmem_limit_bytes=32 << 20),
        cost_estimate=pl.CostEstimate(flops=10 * tokens * width, bytes_accessed=16 << 20, transcendentals=0),
        name="project_grads",
    )(marks, conv_grad, after, gate, value, open_grad, scales)


def pair_grads(place, left, right, cores, name):
    tokens, width = left.shape
    block = right.shape[1] // 4
    eighth = width // 8
    count = len(cores)
    step = 256

    def kernel(place_ref, left_ref, right_ref, *outs):
        at = pl.program_id(0)
        for n in range(block // step):
            total = narrow(contract_rows(left_ref[...], right_ref[:, n * step : (n + 1) * step]))
            for c in range(count):
                @pl.when(at // 2 == c)
                def _():
                    for i in range(8):
                        outs[c][0, place_ref[2 + i], :, n * step : (n + 1) * step] = total[i * eighth : (i + 1) * eighth]

    def column(i, place_ref):
        return (0, place_ref[14 + 2 * cores[0] + i])

    def out_spec(c):
        return pl.BlockSpec(
            (1, 8, eighth, block), lambda i, place_ref: (jnp.clip(i - 2 * c, 0, 1), 0, 0, 0)
        )

    return pl.pallas_call(
        kernel,
        grid_spec=pltpu.PrefetchScalarGridSpec(
            num_scalar_prefetch=1,
            grid=(2 * count,),
            in_specs=[
                pl.BlockSpec((tokens, width), lambda i, place_ref: (0, 0), pipeline_mode=pl.Buffered(1)),
                pl.BlockSpec((tokens, block), column),
            ],
            out_specs=[out_spec(c) for c in range(count)],
        ),
        out_shape=[jax.ShapeDtypeStruct((2, 8, eighth, block), LOW)] * count,
        compiler_params=pltpu.CompilerParams(vmem_limit_bytes=32 << 20),
        cost_estimate=pl.CostEstimate(
            flops=count * 4 * tokens * width * block, bytes_accessed=8 << 20, transcendentals=0
        ),
        name=name,
    )(place, left, right)


def mixer_backward(project_grad, in_weight, hidden, residual_grad, sums, scales):
    tokens, width = hidden.shape
    tile = 256
    steps = tokens // tile

    def kernel(grad_ref, in_ref, hidden_ref, residual_ref, sums_ref, scale_ref, input_out, sums_out):
        @pl.when(pl.program_id(0) == 0)
        def _():
            sums_out[...] = sums_ref[...]

        normed_grad = contract_cols(grad_ref[...], in_ref[...])
        source = hidden_ref[...].astype(FULL)
        inverse = lax.rsqrt(jnp.mean(source * source, axis=1, keepdims=True) + EPS)
        sums_out[0:1, :] += jnp.sum(normed_grad * (source * inverse), axis=0, keepdims=True)
        scaled = scale_ref[0:1, :] * normed_grad
        lean = (inverse * inverse * inverse) * jnp.mean(scaled * source, axis=1, keepdims=True)
        input_out[...] = narrow(residual_ref[...] + inverse * scaled - source * lean)

    def rows(last):
        return pl.BlockSpec((tile, last), lambda i: (i, 0))

    small = pl.BlockSpec((8, width), lambda i: (0, 0))
    return pl.pallas_call(
        kernel,
        grid=(steps,),
        in_specs=[rows(3 * width), whole(in_weight.shape), rows(width), rows(width), small, whole(scales.shape)],
        out_specs=[rows(width), small],
        out_shape=[jax.ShapeDtypeStruct((tokens, width), LOW), jax.ShapeDtypeStruct((8, width), FULL)],
        compiler_params=pltpu.CompilerParams(vmem_limit_bytes=32 << 20),
        cost_estimate=pl.CostEstimate(flops=6 * tokens * width * width, bytes_accessed=20 << 20, transcendentals=0),
        name="mixer_backward",
    )(project_grad, in_weight, hidden, residual_grad, sums, scales)


def plain(
    hidden_in,
    mixer_gain,
    in_weight,
    conv_kernel,
    out_weight,
    feed_gain,
    gate_weight,
    up_weight,
    down_weight,
    document_lengths,
    valid_tokens,
    cotangent,
):
    row_count, span_length, model_width = hidden_in.shape
    token_count = row_count * span_length
    offset = lax.axis_index("seq") * span_length
    positions = offset + jnp.arange(span_length, dtype=jnp.int32)
    starts = jnp.cumsum(document_lengths, axis=1) - document_lengths
    is_start = jnp.any(positions[None, :, None] == starts[:, None, :], axis=2)
    before = jnp.any((positions - 1)[None, :, None] == starts[:, None, :], axis=2)
    keep_one = (1.0 - is_start.astype(jnp.float32))[:, :, None]
    keep_two = keep_one * (1.0 - before.astype(jnp.float32))[:, :, None]
    valid_mask = (
        (positions[None, :] < valid_tokens[:, None]).astype(jnp.float32).reshape(token_count, 1)
    )
    mixer_scale = mixer_gain.astype(jnp.float32)
    feed_scale = feed_gain.astype(jnp.float32)
    kernel = conv_kernel.astype(jnp.float32)
    source = hidden_in.astype(jnp.float32).reshape(token_count, model_width)
    inverse_one = lax.rsqrt(jnp.mean(source * source, axis=1, keepdims=True) + EPS)
    normed = (source * inverse_one * mixer_scale).astype(jnp.bfloat16)
    project = jnp.dot(normed, in_weight, preferred_element_type=jnp.float32)
    input_gate = project[:, :model_width]
    output_gate = project[:, model_width : 2 * model_width]
    values = project[:, 2 * model_width :]
    product = (
        (input_gate * values).astype(jnp.bfloat16).reshape(row_count, span_length, model_width)
    )
    rim_values = passed_along(product[:, span_length - 2 :, :], "seq", 1)
    extended = jnp.concatenate([rim_values, product], axis=1).astype(jnp.float32)
    tap_zero = extended[:, 2:, :]
    tap_one = keep_one * extended[:, 1:-1, :]
    tap_two = keep_two * extended[:, :-2, :]
    conv_out = (kernel[:, 0] * tap_zero + kernel[:, 1] * tap_one + kernel[:, 2] * tap_two).reshape(
        token_count, model_width
    )
    mixed_in = (output_gate * conv_out).astype(jnp.bfloat16)
    mixer_out = jnp.dot(mixed_in, out_weight, preferred_element_type=jnp.float32)
    residual = source + valid_mask * mixer_out
    inverse_two = lax.rsqrt(jnp.mean(residual * residual, axis=1, keepdims=True) + EPS)
    normed_two = (residual * inverse_two * feed_scale).astype(jnp.bfloat16)
    gate_pre = jnp.dot(normed_two, gate_weight, preferred_element_type=jnp.float32)
    up_pre = jnp.dot(normed_two, up_weight, preferred_element_type=jnp.float32)
    sigmoid_gate = jax.nn.sigmoid(gate_pre)
    activation = (gate_pre * sigmoid_gate * up_pre).astype(jnp.bfloat16)
    feed_out = jnp.dot(activation, down_weight, preferred_element_type=jnp.float32)
    output = (
        (residual + valid_mask * feed_out)
        .astype(jnp.bfloat16)
        .reshape(row_count, span_length, model_width)
    )
    upstream = cotangent.astype(jnp.float32).reshape(token_count, model_width)
    feed_grad = (valid_mask * upstream).astype(jnp.bfloat16)
    down_grad = contract_rows(activation, feed_grad)
    activation_grad = contract_cols(feed_grad, down_weight)
    up_grad = (activation_grad * gate_pre * sigmoid_gate).astype(jnp.bfloat16)
    gate_grad = (
        activation_grad * up_pre * sigmoid_gate * (1.0 + gate_pre * (1.0 - sigmoid_gate))
    ).astype(jnp.bfloat16)
    gate_wgrad = contract_rows(normed_two, gate_grad)
    up_wgrad = contract_rows(normed_two, up_grad)
    normed_two_grad = contract_cols(gate_grad, gate_weight) + contract_cols(up_grad, up_weight)
    feed_gain_grad = jnp.sum(normed_two_grad * residual * inverse_two, axis=0)
    scaled_two = feed_scale * normed_two_grad
    residual_grad = (
        upstream
        + inverse_two * scaled_two
        - residual
        * (inverse_two * inverse_two * inverse_two)
        * jnp.mean(scaled_two * residual, axis=1, keepdims=True)
    )
    feed_gain_part, gate_part, up_part, down_part = (
        lax.psum_scatter(
            feed_gain_grad.astype(jnp.bfloat16), "seq", scatter_dimension=0, tiled=True
        ).astype(jnp.float32),
        lax.psum_scatter(
            gate_wgrad.astype(jnp.bfloat16), "seq", scatter_dimension=0, tiled=True
        ).astype(jnp.float32),
        lax.psum_scatter(
            up_wgrad.astype(jnp.bfloat16), "seq", scatter_dimension=0, tiled=True
        ).astype(jnp.float32),
        lax.psum_scatter(
            down_grad.astype(jnp.bfloat16), "seq", scatter_dimension=0, tiled=True
        ).astype(jnp.float32),
    )
    gate_part, up_part, down_part = (
        lax.psum_scatter(
            gate_part.astype(jnp.bfloat16), "row", scatter_dimension=1, tiled=True
        ).astype(jnp.float32),
        lax.psum_scatter(
            up_part.astype(jnp.bfloat16), "row", scatter_dimension=1, tiled=True
        ).astype(jnp.float32),
        lax.psum_scatter(
            down_part.astype(jnp.bfloat16), "row", scatter_dimension=1, tiled=True
        ).astype(jnp.float32),
    )
    mixer_grad = (valid_mask * residual_grad).astype(jnp.bfloat16)
    out_wgrad = contract_rows(mixed_in, mixer_grad)
    mixed_grad = contract_cols(mixer_grad, out_weight)
    output_gate_grad = mixed_grad * conv_out
    conv_grad = (mixed_grad * output_gate).reshape(row_count, span_length, model_width)
    kernel_grad = jnp.stack(
        [
            jnp.sum(conv_grad * tap_zero, axis=(0, 1)),
            jnp.sum(conv_grad * tap_one, axis=(0, 1)),
            jnp.sum(conv_grad * tap_two, axis=(0, 1)),
        ],
        axis=1,
    )
    grad_zero = kernel[:, 0] * conv_grad
    grad_one = keep_one * kernel[:, 1] * conv_grad
    grad_two = keep_two * kernel[:, 2] * conv_grad
    extended_grad = (
        jnp.pad(grad_zero, ((0, 0), (2, 0), (0, 0)))
        + jnp.pad(grad_one, ((0, 0), (1, 1), (0, 0)))
        + jnp.pad(grad_two, ((0, 0), (0, 2), (0, 0)))
    )
    returned = passed_along(extended_grad[:, :2, :], "seq", -1)
    product_grad = extended_grad[:, 2:, :] + jnp.pad(
        returned, ((0, 0), (span_length - 2, 0), (0, 0))
    )
    flat_grad = product_grad.reshape(token_count, model_width)
    project_grad = jnp.concatenate(
        [flat_grad * values, output_gate_grad, flat_grad * input_gate], axis=1
    ).astype(jnp.bfloat16)
    in_wgrad = contract_rows(normed, project_grad)
    normed_grad = contract_cols(project_grad, in_weight)
    mixer_gain_grad = jnp.sum(normed_grad * source * inverse_one, axis=0)
    scaled_one = mixer_scale * normed_grad
    input_grad = (
        residual_grad
        + inverse_one * scaled_one
        - source
        * (inverse_one * inverse_one * inverse_one)
        * jnp.mean(scaled_one * source, axis=1, keepdims=True)
    )
    input_grad = input_grad.astype(jnp.bfloat16).reshape(row_count, span_length, model_width)
    mixer_gain_part, in_part, kernel_part, out_part = (
        lax.psum_scatter(
            mixer_gain_grad.astype(jnp.bfloat16), "seq", scatter_dimension=0, tiled=True
        ).astype(jnp.float32),
        lax.psum_scatter(
            in_wgrad.astype(jnp.bfloat16), "seq", scatter_dimension=0, tiled=True
        ).astype(jnp.float32),
        lax.psum_scatter(
            kernel_grad.astype(jnp.bfloat16), "seq", scatter_dimension=0, tiled=True
        ).astype(jnp.float32),
        lax.psum_scatter(
            out_wgrad.astype(jnp.bfloat16), "seq", scatter_dimension=0, tiled=True
        ).astype(jnp.float32),
    )
    in_part, out_part = (
        lax.psum_scatter(
            in_part.astype(jnp.bfloat16), "row", scatter_dimension=1, tiled=True
        ).astype(jnp.float32),
        lax.psum_scatter(
            out_part.astype(jnp.bfloat16), "row", scatter_dimension=1, tiled=True
        ).astype(jnp.float32),
    )
    mixer_gain_part, feed_gain_part, kernel_part = lax.psum(
        (mixer_gain_part, feed_gain_part, kernel_part), "row"
    )
    return (
        output,
        input_grad,
        mixer_gain_part,
        in_part,
        kernel_part,
        out_part,
        feed_gain_part,
        gate_part,
        up_part,
        down_part,
    )


def joined(keeps, takes, name):
    count = len(keeps)
    shape = (count,) + keeps[0].shape[1:]

    def kernel(*refs):
        for n in range(count):
            for side in range(2):
                refs[2 * count + side][n] = narrow(wide(refs[n][side], refs[count + n][side]))

    return pl.pallas_call(
        kernel,
        out_shape=[jax.ShapeDtypeStruct(shape, LOW)] * 2,
        compiler_params=pltpu.CompilerParams(vmem_limit_bytes=32 << 20),
        name=name,
    )(*keeps, *takes)


def side_by_side(keeps, takes):
    count = len(keeps)
    widths = [keep.shape[-1] for keep in keeps]
    shape = (2, keeps[0].shape[-2], sum(widths))

    def kernel(*refs):
        for n in range(count):
            at = pl.ds(sum(widths[:n]), widths[n])
            for side in range(2):
                for h in range(2):
                    refs[2 * count + side][h, :, at] = narrow(
                        wide(refs[n][2 * h + side], refs[count + n][2 * h + side])
                    )

    return pl.pallas_call(
        kernel,
        out_shape=[jax.ShapeDtypeStruct(shape, LOW)] * 2,
        compiler_params=pltpu.CompilerParams(vmem_limit_bytes=32 << 20),
        name="side_by_side",
    )(*keeps, *takes)


def last_sums(keeps, takes):
    counts = [keep.shape[0] for keep in keeps]
    height, part = keeps[0].shape[1:]
    shape = (height, sum(counts) // 2 * part)

    def kernel(*refs):
        n = 0
        for i, count in enumerate(counts):
            for k in range(count):
                refs[2 * len(counts) + n % 2][:, pl.ds(n // 2 * part, part)] = wide(
                    refs[i][k], refs[len(counts) + i][k]
                )
                n += 1

    return pl.pallas_call(
        kernel,
        out_shape=[jax.ShapeDtypeStruct(shape, FULL)] * 2,
        compiler_params=pltpu.CompilerParams(vmem_limit_bytes=32 << 20),
        name="last_sums",
    )(*keeps, *takes)


def fast(
    hidden_in,
    mixer_gain,
    in_weight,
    conv_kernel,
    out_weight,
    feed_gain,
    gate_weight,
    up_weight,
    down_weight,
    document_lengths,
    valid_tokens,
    cotangent,
):
    row_count, span_length, model_width = hidden_in.shape
    token_count = row_count * span_length
    hidden_width = gate_weight.shape[1]
    block = hidden_width // 4
    chunks = 3
    part = block // chunks
    seq = lax.axis_index("seq")
    row = lax.axis_index("row")
    row_x, core = row // 2, row % 2
    seq_y, seq_z0, seq_z1 = seq % 2, (seq // 2) % 2, seq // 4
    place = jnp.stack(
        [row ^ 2, row]
        + [i ^ seq ^ 7 for i in range(8)]
        + [1 - row_x, row_x, 1 - ((1 - row_x) ^ seq_z1), 1 - (row_x ^ seq_z1)]
        + [row ^ 3, row ^ 1, row ^ 2, row]
    ).astype(jnp.int32)
    positions = seq * span_length + jnp.arange(span_length, dtype=jnp.int32)
    starts = jnp.cumsum(document_lengths, axis=1) - document_lengths

    def unstarted(shift):
        return 1.0 - jnp.any((positions + shift)[None, :, None] == starts[:, None, :], axis=2).astype(FULL)

    here, last, one_on, two_on = (unstarted(shift) for shift in (0, -1, 1, 2))
    valid = (positions[None, :] < valid_tokens[:, None]).astype(FULL)
    blank = jnp.zeros_like(valid)
    marks = jnp.stack([here, here * last, valid, one_on, two_on * one_on, blank, blank, blank], axis=2).reshape(
        token_count, 8
    )
    valid_mask = marks[:, 2:3]
    scales = jnp.concatenate(
        [mixer_gain[None], feed_gain[None], conv_kernel.T, jnp.zeros((3, model_width), conv_kernel.dtype)]
    ).astype(FULL)
    hidden = hidden_in.reshape(token_count, model_width)
    upstream = cotangent.reshape(token_count, model_width)
    rim = passed_along(hidden_in[:, span_length - 2 :, :], "seq", 1)
    rim = jnp.pad(rim, ((0, 0), (MARGIN - 2, 0), (0, 0))).reshape(row_count * MARGIN, model_width)
    feed_grad = narrow(valid_mask * upstream.astype(FULL))
    other_grad = swapped(feed_grad, "row", 1)
    normed, input_gate, output_gate, values, product, mixed_in, residual, normed_two, before = mixer_forward(
        marks, hidden, rim, in_weight, out_weight, scales
    )
    other_normed = swapped(normed_two, "row", 1)

    def chunk_grads(start, chunk):
        return feed_chunk(
            start, normed_two, other_normed, feed_grad, other_grad, gate_weight, up_weight, down_weight, chunk, chunks
        )

    def sent(made):
        gs, us, ds = made[3], made[5], made[7]
        return swapped(gs, "seq", 2), swapped(us, "seq", 1), swapped(ds, "row", 2)

    def together(*values):
        return lax.optimization_barrier(values)

    def follow(value, *ahead):
        return lax.optimization_barrier((value,) + ahead)[0]

    def first_sums(made, taken):
        pairs = ((made[4], taken[0]), (made[6], taken[1]))
        halves = [narrow(wide(keep[i], take[i])) for keep, take in pairs for i in range(2)]
        return halves + [narrow(wide(made[8], taken[2]))]

    def second(sums):
        return swapped(sums[0], "seq", 1), swapped(sums[2], "seq", 2)

    def split(keep, take, at):
        return [
            narrow(wide(lax.index_in_dim(keep, i, at, False), lax.index_in_dim(take, i, at, False))) for i in range(2)
        ]

    made0 = chunk_grads(place, 0)
    taken0 = sent(made0)
    made1, taken0 = together(chunk_grads(follow(place, made0[0]), 1), taken0)
    taken1 = sent(made1)
    sums0 = first_sums(made0, taken0)
    second0 = second(sums0)
    made2, taken1, second0 = together(chunk_grads(follow(place, sums0), 2), taken1, second0)
    taken2 = sent(made2)
    sums1 = first_sums(made1, taken1)
    second1 = second(sums1)
    acts, gates, ups = ([one[i] for one in (made0, made1, made2)] for i in range(3))
    (own_ntg, give_ntg), taken2, second1 = together(
        feed_sum(follow(place, sums1), [gates, ups], [gate_weight, up_weight], True, block, "normed_two_grad"),
        taken2,
        second1,
    )
    take_ntg = swapped(give_ntg, "row", 1)
    sums2 = first_sums(made2, taken2)
    second2 = second(sums2)
    third_give, third_keep = joined([sums0[1], sums0[3], sums1[1], sums1[3]], second0 + second1, "third_sums")
    third_take = swapped(third_give, "row", 2)

    (residual_grad, mixer_grad, open_grad, conv_grad, sums), second2 = together(
        mixer_middle(
            follow(marks, sums2, third_keep), own_ntg, take_ntg, residual, upstream, product, before, output_gate,
            out_weight, scales,
        ),
        second2,
    )
    after = passed_along(conv_grad.reshape(row_count, span_length, model_width)[:, :2, :], "seq", -1)
    late_give, late_keep = joined([sums2[1], sums2[3]], second2, "late_sums")
    late_take = swapped(late_give, "row", 2)
    down = jnp.concatenate(follow([sums0[4], sums1[4], sums2[4]], mixer_grad), axis=1)
    low_half, high_half = down[:, : block // 2], down[:, block // 2 :]
    down_keep = jnp.where(seq_y == 0, low_half, high_half)
    down_give = jnp.where(seq_y == 0, high_half, low_half)

    (out_give, out_keep), after, third_take, down_give = together(
        pair_grads(follow(place, late_keep, down_keep, down_give), mixed_in, mixer_grad, (0, 1), "out_grads"),
        after,
        third_take,
        down_give,
    )
    down_takes = [swapped(down_give[0], "seq", 1)]
    out_take = swapped(out_give, "row", 1)
    after = jnp.pad(after, ((0, 0), (0, 6), (0, 0))).reshape(row_count * 8, model_width)
    fourth_give, fourth_keep = split(third_keep, third_take, 1)
    fourth_takes = [swapped(fourth_give[:2], "seq", 4)]

    project_grad = project_grads(
        follow(marks, out_keep, fourth_give, fourth_keep), conv_grad, after, input_gate, values, open_grad, scales
    )
    (in_give,), out_take, late_take, down_takes, fourth_takes = together(
        pair_grads(place, normed, project_grad, (0,), "in_grads_give"), out_take, late_take, down_takes, fourth_takes
    )
    in_take = swapped(in_give, "row", 1)
    out_give, out_keep = split(out_keep, out_take, 0)
    out_take = swapped(out_give, "row", 2)
    down_takes.append(swapped(follow(down_give[1], out_give), "seq", 1))
    fourth_takes.append(swapped(follow(fourth_give[2:], out_give), "seq", 4))
    late_give, late_keep = split(late_keep, late_take, 1)

    (in_keep,), in_take, out_take, down_takes, fourth_takes, late_give = together(
        pair_grads(
            follow(place, in_give, out_give, out_keep, late_give, late_keep), normed, project_grad, (1,), "in_grads_keep"
        ),
        in_take,
        out_take,
        down_takes,
        fourth_takes,
        late_give,
    )
    late_take = swapped(late_give, "seq", 4)
    half = in_keep.shape[-1] // 2
    left_give, left_keep = split(in_keep[..., :half], in_take[..., :half], 0)
    left_take = swapped(left_give, "row", 2)
    eighths = (2, 4, 2, model_width // 8, half)
    right_give, right_keep = split(in_keep[..., half:].reshape(eighths), in_take[..., half:].reshape(eighths), 2)
    right_take = swapped(right_give, "seq", 1)
    eighths = (4, 2, model_width // 8, out_keep.shape[-1])
    out_give, out_keep = split(out_keep.reshape(eighths), out_take.reshape(eighths), 1)
    down_give, down_keep = (narrow(wide(down_keep[i], down_takes[i])) for i in range(2))

    (input_grad, small), late_take, out_give, down_give = together(
        mixer_backward(
            follow(
                project_grad, left_give, left_keep, right_give, right_keep, out_give, out_keep, down_give, down_keep,
            ),
            in_weight, hidden, residual_grad, sums, scales,
        ),
        late_take,
        out_give,
        down_give,
    )
    small_take = swapped(small, "row", 1)
    out_take = swapped(out_give, "seq", 1)
    quarter = down_give.shape[0] // 2
    down_takes = [swapped(down_give[:quarter], "seq", 4)]
    (own_feed, give_feed), left_take, right_take, out_take, small_take, down_takes = together(
        feed_sum(follow(place, input_grad), [acts], [down_weight], False, block, "feed_out"),
        left_take,
        right_take,
        out_take,
        small_take,
        down_takes,
    )
    down_takes.append(swapped(follow(down_give[quarter:], own_feed), "seq", 4))
    take_feed = swapped(give_feed, "row", 1)
    eighths = (4, 2, model_width // 8, half)
    left_give, left_keep = split(left_keep.reshape(eighths), left_take.reshape(eighths), 1)
    left_take = swapped(left_give, "seq", 1)
    right_give, right_keep = split(right_keep, right_take, 0)
    right_take = swapped(right_give, "row", 2)
    small = small + small_take
    small_take = swapped(small, "row", 2)
    (gate_part, up_part), left_take, right_take, take_feed, small_take = together(
        last_sums(*follow(([fourth_keep[:2], fourth_keep[2:], late_keep], fourth_takes + [late_take]), left_give, right_give, small)),
        left_take,
        right_take,
        take_feed,
        small_take,
    )
    give, keep = side_by_side([left_keep, right_keep, out_keep], [left_take, right_take, out_take])
    take = swapped(give, "seq", 2)
    small = small + small_take
    small_take = swapped(small, "seq", 1)
    output = narrow(residual + valid_mask * wide(own_feed, follow(take_feed, give)))
    output, small_take, down_takes = together(output, small_take, down_takes)
    output = output.reshape(row_count, span_length, model_width)
    down = narrow(wide(down_keep, jnp.concatenate(down_takes)))
    small = small + small_take
    small_take = swapped(small, "seq", 2)
    holder = [[(r & 1) == ((s >> 1) & 1) for r in range(4)] for s in range(8)]
    down_take = lax.ppermute(
        down,
        ("seq", "row"),
        [(s * 4 + r, (s ^ 2) * 4 + r) for s in range(8) for r in range(4) if not holder[s][r]],
    )
    take, small_take = together(take, small_take)
    give, keep = split(keep, take, 0)
    take = swapped(give, "seq", 4)
    small = small + small_take
    small_take = swapped(small, "seq", 4)
    down = wide(down, follow(down_take, give))
    quarter = model_width // 4
    down_own = jnp.where(core == 0, down[:, :quarter], down[:, quarter:])
    down_other = narrow(jnp.where(core == 0, down[:, quarter:], down[:, :quarter]))
    down_other = lax.ppermute(
        down_other,
        ("seq", "row"),
        [(s * 4 + r, s * 4 + (r ^ 1)) for s in range(8) for r in range(4) if holder[s][r]],
    )
    down_part = jnp.where(core == seq_z0, down_own, down_other.astype(jnp.float32))
    input_grad = input_grad.reshape(row_count, span_length, model_width)
    both_part = wide(keep, take)
    in_part, out_part = both_part[:, : 2 * half], both_part[:, 2 * half :]
    small = small + small_take
    small = lax.dynamic_slice_in_dim(small, seq * (model_width // 8), model_width // 8, 1)
    return (
        output,
        input_grad,
        small[0],
        in_part,
        small[2:5].T,
        out_part,
        small[1],
        gate_part,
        up_part,
        down_part,
    )


def local(*args):
    hidden_in, gate_weight = args[0], args[6]
    tokens = hidden_in.shape[0] * hidden_in.shape[1]
    width, hidden = gate_weight.shape
    tiled = lax.axis_size("seq") == 8 and lax.axis_size("row") == 4 and hidden % (4 * 3 * 128) == 0
    if tiled and width % 1024 == 0 and tokens % 512 == 0:
        return fast(*args)
    return plain(*args)


def solution(mesh):
    in_specs = (
        P("row", "seq", None),
        P(),
        P(),
        P(),
        P(),
        P(),
        P(),
        P(),
        P(),
        P("row", None),
        P("row"),
        P("row", "seq", None),
    )
    out_specs = (
        P("row", "seq", None),
        P("row", "seq", None),
        P("seq"),
        P("seq", "row"),
        P("seq", None),
        P("seq", "row"),
        P("seq"),
        P("seq", "row"),
        P("seq", "row"),
        P("seq", "row"),
    )
    return jax.shard_map(local, mesh=mesh, in_specs=in_specs, out_specs=out_specs, check_vma=False)
```

```python
import jax
import jax.numpy as jnp
from jax import lax
from jax.experimental import pallas as pl
from jax.experimental.pallas import tpu as pltpu
from jax.sharding import PartitionSpec as P

EPS = 1e-05


def passed_along(value, axis, by):
    length = lax.axis_size(axis)
    pairs = [(i, i + by) for i in range(length) if 0 <= i + by < length]
    return lax.ppermute(value, axis, pairs)


def contract_rows(left, right):
    return lax.dot_general(
        left, right, (((0,), (0,)), ((), ())), preferred_element_type=jnp.float32
    )


def contract_cols(left, right):
    return lax.dot_general(
        left, right, (((1,), (1,)), ((), ())), preferred_element_type=jnp.float32
    )


def far(*values):
    return [pltpu.with_memory_space_constraint(value, pltpu.HBM) for value in values]


def swapped(value, axis, bit):
    length = lax.axis_size(axis)
    return lax.ppermute(value, axis, [(i, i ^ bit) for i in range(length)])


def wide(left, right):
    return left.astype(jnp.float32) + right.astype(jnp.float32)


def narrow(value):
    return value.astype(jnp.bfloat16)


def feed_chunk(place, own_in, other_in, own_grad, other_grad, gate_weight, up_weight, down_weight, chunk, chunks):
    tokens, width = own_in.shape
    hidden = gate_weight.shape[1]
    rows = 2
    block = hidden // 4
    part = block // chunks
    span = rows * part
    tile = min(512, tokens)
    tiles = 2 * tokens // tile
    half_tiles = tokens // tile
    eighth = width // 8
    step = 256

    def kernel(
        place_ref, own_ref, other_ref, own_grad_ref, other_grad_ref, gate_ref, up_ref, down_ref,
        act_out, gate_out, up_out, gate_send, gate_keep, up_send, up_keep, down_send, down_keep,
        tok, grd, wg, wu, wd, act, gg, ug, gw, uw, dw, tok_t, act_t, in_sem, w_sem, out_sem, grad_sem,
    ):
        def token_copy(t, which):
            buf = (tok, grd)[which]
            src = ((own_ref, other_ref), (own_grad_ref, other_grad_ref))[which][0 if t < half_tiles else 1]
            return pltpu.make_async_copy(
                src.at[pl.ds((t % half_tiles) * tile, tile)],
                buf.at[pl.ds(t * tile, tile)],
                in_sem.at[which, t],
            )

        weight_copies = []
        for n, (ref, buf) in enumerate(((gate_ref, wg), (up_ref, wu))):
            weight_copies.append([
                pltpu.make_async_copy(
                    ref.at[:, pl.ds(pl.multiple_of(place_ref[j] * block + chunk * part, 128), part)],
                    buf.at[:, pl.ds(j * part, part)],
                    w_sem.at[n, j],
                )
                for j in range(2)
            ])
        weight_copies.append([
            pltpu.make_async_copy(
                down_ref.at[pl.ds(pl.multiple_of(place_ref[j] * block + chunk * part, 128), part), :],
                wd.at[pl.ds(j * part, part), :],
                w_sem.at[2, j],
            )
            for j in range(2)
        ])
        token_copy(0, 0).start()
        for copy in weight_copies[0]:
            copy.start()
        for copy in weight_copies[1]:
            copy.start()
        token_copy(0, 1).start()
        for copy in weight_copies[2]:
            copy.start()
        outs = []
        for t in range(tiles):
            at = pl.ds(t * tile, tile)
            token_copy(t, 0).wait()
            if t == 0:
                for copy in weight_copies[0] + weight_copies[1]:
                    copy.wait()
            if t + 1 < tiles:
                token_copy(t + 1, 0).start()
                token_copy(t + 1, 1).start()
            token_copy(t, 1).wait()
            if t == 0:
                for copy in weight_copies[2]:
                    copy.wait()
            tok_t[:, at] = tok[at, :].T
            for n in range(span // step):
                cols = pl.ds(n * step, step)
                gate = jnp.dot(tok[at, :], wg[:, cols], preferred_element_type=jnp.float32)
                up = jnp.dot(tok[at, :], wu[:, cols], preferred_element_type=jnp.float32)
                grad = contract_cols(grd[at, :], wd[cols, :])
                sig = jax.nn.sigmoid(gate)
                gate_sig = gate * sig
                made = narrow(gate_sig * up)
                act[at, cols] = made
                act_t[cols, at] = made.T
                ug[at, cols] = narrow(grad * gate_sig)
                gg[at, cols] = narrow(grad * up * (sig + gate_sig * (1.0 - sig)))
            for n, (buf, out) in enumerate(((act, act_out), (gg, gate_out), (ug, up_out))):
                copy = pltpu.make_async_copy(buf.at[at], out.at[at], out_sem.at[n, t])
                copy.start()
                outs.append(copy)

        for buf, grad in ((gw, gg), (uw, ug)):
            for n in range(span // step):
                cols = pl.ds(n * step, step)
                total = narrow(jnp.dot(tok_t[...], grad[:, cols], preferred_element_type=jnp.float32))
                for i in range(8):
                    spot = place_ref[2 + i]
                    rows_i = total[i * eighth : (i + 1) * eighth]
                    for c in range(step // 128):
                        col = n * step + c * 128
                        buf[col // part, spot, :, pl.ds(col % part, 128)] = rows_i[:, c * 128 : (c + 1) * 128]
            if buf is gw:
                pairs = [
                    (gw.at[j, pl.ds(4 * h + 2 * z, 2)], out.at[:, j, h], grad_sem.at[8 + 4 * z + 2 * j + h])
                    for z, out in enumerate((gate_send, gate_keep))
                    for j in range(2)
                    for h in range(2)
                ]
            else:
                pairs = [
                    (uw.at[j, 4 * h + 2 * z + y], out.at[z, j, h], grad_sem.at[16 + 8 * y + 4 * z + 2 * j + h])
                    for y, out in enumerate((up_send, up_keep))
                    for z in range(2)
                    for j in range(2)
                    for h in range(2)
                ]
            for src, out, sem in pairs:
                copy = pltpu.make_async_copy(src, out, sem)
                copy.start()
                outs.append(copy)
        for side in range(2):
            for n in range(2):
                cols = pl.ds(pl.multiple_of(place_ref[10 + side] * (width // 2) + n * (width // 4), 128), width // 4)
                total = narrow(jnp.dot(act_t[...], grd[:, cols], preferred_element_type=jnp.float32))
                for j in range(2):
                    dw[side, place_ref[12 + j], :, pl.ds(n * (width // 4), width // 4)] = total[j * part : (j + 1) * part]
            copy = pltpu.make_async_copy(dw.at[side], (down_send, down_keep)[side], grad_sem.at[side])
            copy.start()
            outs.append(copy)
        for copy in outs:
            copy.wait()

    any_spec = pl.BlockSpec(memory_space=pltpu.HBM)
    low = jnp.bfloat16
    both = 2 * tokens
    flops = 6 * 2 * both * width * span
    return pl.pallas_call(
        kernel,
        out_shape=[jax.ShapeDtypeStruct((both, span), low)] * 3
        + [jax.ShapeDtypeStruct((2, 2, 2, eighth, part), low)] * 4
        + [jax.ShapeDtypeStruct((2, part, width // 2), low)] * 2,
        grid_spec=pltpu.PrefetchScalarGridSpec(
            num_scalar_prefetch=1,
            grid=(1,),
            in_specs=[any_spec] * 7,
            out_specs=[any_spec] * 9,
            scratch_shapes=[
                pltpu.VMEM((both, width), low),
                pltpu.VMEM((both, width), low),
                pltpu.VMEM((width, span), low),
                pltpu.VMEM((width, span), low),
                pltpu.VMEM((span, width), low),
                pltpu.VMEM((both, span), low),
                pltpu.VMEM((both, span), low),
                pltpu.VMEM((both, span), low),
                pltpu.VMEM((2, 8, eighth, part), low),
                pltpu.VMEM((2, 8, eighth, part), low),
                pltpu.VMEM((2, 2, part, width // 2), low),
                pltpu.VMEM((width, both), low),
                pltpu.VMEM((span, both), low),
                pltpu.SemaphoreType.DMA((2, tiles)),
                pltpu.SemaphoreType.DMA((3, 2)),
                pltpu.SemaphoreType.DMA((3, tiles)),
                pltpu.SemaphoreType.DMA((32,)),
            ],
        ),
        compiler_params=pltpu.CompilerParams(vmem_limit_bytes=56 << 20),
        cost_estimate=pl.CostEstimate(flops=flops, bytes_accessed=24 << 20, transcendentals=both * span),
        name=f"feed_{chunk}",
    )(place, own_in, other_in, own_grad, other_grad, gate_weight, up_weight, down_weight)


def feed_sum(place, groups, weights, across, block, name, sides=(0, 1)):
    chunks = len(groups[0])
    both, span = groups[0][0].shape
    part = span // 2
    width = weights[0].shape[0] if across else weights[0].shape[1]
    tokens = both // 2
    tile = min(512, tokens)
    half_tiles = tokens // tile
    tiles = len(sides) * half_tiles
    kinds = len(groups)

    def kernel(place_ref, *refs):
        lefts = [refs[g * chunks : (g + 1) * chunks] for g in range(kinds)]
        rights = refs[kinds * chunks : kinds * chunks + kinds]
        sums_out = refs[kinds * chunks + kinds : kinds * chunks + kinds + len(sides)]
        lbuf, wbuf, total, obuf, l_sem, w_sem, o_sem = refs[kinds * chunks + kinds + len(sides) :]

        def weight_copies(k):
            slot = k % 2
            copies = []
            for g in range(kinds):
                for j in range(2):
                    rows = pl.ds(pl.multiple_of(place_ref[j] * block + k * part, 128), part)
                    if across:
                        src, dst = rights[g].at[:, rows], wbuf.at[slot, g, :, pl.ds(j * part, part)]
                    else:
                        src, dst = rights[g].at[rows, :], wbuf.at[slot, g, pl.ds(j * part, part), :]
                    copies.append(pltpu.make_async_copy(src, dst, w_sem.at[slot, g, j]))
            return copies

        def left_copies(k, t, slot):
            row = (sides[t // half_tiles] * half_tiles + t % half_tiles) * tile
            return [
                pltpu.make_async_copy(lefts[g][k].at[pl.ds(row, tile)], lbuf.at[slot, g], l_sem.at[slot, g])
                for g in range(kinds)
            ]

        def out_copy(t, slot):
            ref = sums_out[t // half_tiles]
            return pltpu.make_async_copy(
                obuf.at[slot], ref.at[pl.ds((t % half_tiles) * tile, tile)], o_sem.at[slot]
            )

        for copy in left_copies(0, 0, 0) + weight_copies(0):
            copy.start()
        for k in range(chunks):
            for t in range(tiles):
                n = k * tiles + t
                for copy in left_copies(k, t, n % 2):
                    copy.wait()
                if t == 0:
                    for copy in weight_copies(k):
                        copy.wait()
                if n + 1 < chunks * tiles:
                    for copy in left_copies((n + 1) // tiles, (n + 1) % tiles, (n + 1) % 2):
                        copy.start()
                if t == 0 and k + 1 < chunks:
                    for copy in weight_copies(k + 1):
                        copy.start()
                value = None
                for g in range(kinds):
                    left, right = lbuf[n % 2, g], wbuf[k % 2, g]
                    term = contract_cols(left, right) if across else jnp.dot(left, right, preferred_element_type=jnp.float32)
                    value = term if value is None else value + term
                if k > 0:
                    value = value + total[t]
                if k + 1 < chunks:
                    total[t] = value
                else:
                    if t >= 2:
                        out_copy(t - 2, t % 2).wait()
                    obuf[t % 2] = narrow(value)
                    out_copy(t, t % 2).start()
        for t in range(max(0, tiles - 2), tiles):
            out_copy(t, t % 2).wait()

    any_spec = pl.BlockSpec(memory_space=pltpu.HBM)
    low = jnp.bfloat16
    wshape = (width, span) if across else (span, width)
    return pl.pallas_call(
        kernel,
        out_shape=[jax.ShapeDtypeStruct((tokens, width), low)] * len(sides),
        grid_spec=pltpu.PrefetchScalarGridSpec(
            num_scalar_prefetch=1,
            grid=(1,),
            in_specs=[any_spec] * (kinds * chunks + kinds),
            out_specs=[any_spec] * len(sides),
            scratch_shapes=[
                pltpu.VMEM((2, kinds, tile, span), low),
                pltpu.VMEM((2, kinds) + wshape, low),
                pltpu.VMEM((tiles, tile, width), jnp.float32),
                pltpu.VMEM((2, tile, width), low),
                pltpu.SemaphoreType.DMA((2, kinds)),
                pltpu.SemaphoreType.DMA((2, kinds, 2)),
                pltpu.SemaphoreType.DMA((2,)),
            ],
        ),
        compiler_params=pltpu.CompilerParams(vmem_limit_bytes=48 << 20),
        cost_estimate=pl.CostEstimate(
            flops=kinds * chunks * 2 * both * width * span, bytes_accessed=24 << 20, transcendentals=0
        ),
        name=name,
    )(place, *[item for group in groups for item in group], *weights)


LOW = jnp.bfloat16
FULL = jnp.float32
MARGIN = 16


def whole(shape):
    return pl.BlockSpec(shape, lambda *_: (0,) * len(shape), pipeline_mode=pl.Buffered(1))


def mixer_forward(marks, hidden, rim, in_weight, out_weight, scales):
    tokens, width = hidden.shape
    tile = 256
    per_row = tokens // 2 // tile
    steps = tokens // tile

    def kernel(
        marks_ref, hidden_ref, rim_ref, in_ref, out_ref, scale_ref,
        normed_out, gate_out, open_out, value_out, product_out, mixed_out, residual_out, next_out, before_out,
        ext, carry,
    ):
        at = pl.program_id(0) % per_row
        tile_in = hidden_ref[...].astype(FULL)

        @pl.when(at == 0)
        def _():
            carry[...] = rim_ref[...].astype(FULL)

        source = jnp.concatenate([carry[...], tile_in], axis=0)
        carry[...] = tile_in[tile - MARGIN :]
        inverse = lax.rsqrt(jnp.mean(source * source, axis=1, keepdims=True) + EPS)
        normed = narrow(source * inverse * scale_ref[0:1, :])
        gate = jnp.dot(normed, in_ref[:, :width], preferred_element_type=FULL)
        value = jnp.dot(normed, in_ref[:, 2 * width :], preferred_element_type=FULL)
        product = narrow(gate * value)
        ext[...] = product.astype(FULL)
        opened = jnp.dot(normed[MARGIN:], in_ref[:, width : 2 * width], preferred_element_type=FULL)
        conv = (
            scale_ref[2:3, :] * ext[MARGIN:, :]
            + marks_ref[:, 0:1] * scale_ref[3:4, :] * ext[MARGIN - 1 : MARGIN - 1 + tile, :]
            + marks_ref[:, 1:2] * scale_ref[4:5, :] * ext[MARGIN - 2 : MARGIN - 2 + tile, :]
        )
        mixed = narrow(opened * conv)
        residual = tile_in + marks_ref[:, 2:3] * jnp.dot(mixed, out_ref[...], preferred_element_type=FULL)
        inverse_two = lax.rsqrt(jnp.mean(residual * residual, axis=1, keepdims=True) + EPS)
        next_out[...] = narrow(residual * inverse_two * scale_ref[1:2, :])
        normed_out[...] = normed[MARGIN:]
        gate_out[...] = narrow(gate[MARGIN:])
        open_out[...] = narrow(opened)
        value_out[...] = narrow(value[MARGIN:])
        product_out[...] = product[MARGIN:]
        mixed_out[...] = mixed
        residual_out[...] = residual

        @pl.when(at == 0)
        def _():
            before_out[...] = product[:MARGIN]

    def rows(last, size=tile):
        return pl.BlockSpec((size, last), lambda i: (i, 0))

    row_spec = pl.BlockSpec((MARGIN, width), lambda i: (i // per_row, 0))
    return pl.pallas_call(
        kernel,
        grid=(steps,),
        in_specs=[rows(8), rows(width), row_spec, whole(in_weight.shape), whole(out_weight.shape), whole(scales.shape)],
        out_specs=[rows(width)] * 8 + [row_spec],
        out_shape=[pltpu.HBM((tokens, width), LOW)] * 6
        + [pltpu.HBM((tokens, width), FULL), pltpu.HBM((tokens, width), LOW)]
        + [pltpu.HBM((2 * MARGIN, width), LOW)],
        scratch_shapes=[pltpu.VMEM((tile + MARGIN, width), FULL), pltpu.VMEM((MARGIN, width), FULL)],
        compiler_params=pltpu.CompilerParams(vmem_limit_bytes=44 << 20),
        cost_estimate=pl.CostEstimate(flops=8 * tokens * width * width, bytes_accessed=28 << 20, transcendentals=0),
        name="mixer_forward",
    )(marks, hidden, rim, in_weight, out_weight, scales)


def mixer_middle(marks, own, other, residual, cotangent, product, before, opened, out_weight, scales):
    tokens, width = own.shape
    tile = 256
    per_row = tokens // 2 // tile
    steps = tokens // tile

    def kernel(
        marks_ref, own_ref, other_ref, residual_ref, cot_ref, product_ref, before_ref, open_ref, out_ref, scale_ref,
        grad_out, mixer_out, open_grad_out, conv_out, sums_out,
        ext, carry,
    ):
        step = pl.program_id(0)
        at = step % per_row

        @pl.when(at == 0)
        def _():
            carry[...] = before_ref[...].astype(FULL)

        @pl.when(step == 0)
        def _():
            sums_out[...] = jnp.zeros_like(sums_out)

        grad = own_ref[...].astype(FULL) + other_ref[...].astype(FULL)
        residual = residual_ref[...]
        inverse = lax.rsqrt(jnp.mean(residual * residual, axis=1, keepdims=True) + EPS)
        sums_out[1:2, :] += jnp.sum(grad * (residual * inverse), axis=0, keepdims=True)
        scaled = scale_ref[1:2, :] * grad
        lean = (inverse * inverse * inverse) * jnp.mean(scaled * residual, axis=1, keepdims=True)
        residual_grad = cot_ref[...].astype(FULL) + inverse * scaled - residual * lean
        grad_out[...] = residual_grad
        mixer = narrow(marks_ref[:, 2:3] * residual_grad)
        mixer_out[...] = mixer
        mixed = contract_cols(mixer, out_ref[...])
        product = product_ref[...].astype(FULL)
        ext[:MARGIN, :] = carry[...]
        ext[MARGIN:, :] = product
        carry[...] = product[tile - MARGIN :]
        one = marks_ref[:, 0:1] * ext[MARGIN - 1 : MARGIN - 1 + tile, :]
        two = marks_ref[:, 1:2] * ext[MARGIN - 2 : MARGIN - 2 + tile, :]
        conv = scale_ref[2:3, :] * product + scale_ref[3:4, :] * one + scale_ref[4:5, :] * two
        open_grad_out[...] = narrow(mixed * conv)
        conv_grad = mixed * open_ref[...].astype(FULL)
        conv_out[...] = conv_grad
        sums_out[2:3, :] += jnp.sum(conv_grad * product, axis=0, keepdims=True)
        sums_out[3:4, :] += jnp.sum(conv_grad * one, axis=0, keepdims=True)
        sums_out[4:5, :] += jnp.sum(conv_grad * two, axis=0, keepdims=True)

    def rows(last):
        return pl.BlockSpec((tile, last), lambda i: (i, 0))

    row_spec = pl.BlockSpec((MARGIN, width), lambda i: (i // per_row, 0))
    return pl.pallas_call(
        kernel,
        grid=(steps,),
        in_specs=[rows(8)] + [rows(width)] * 5 + [row_spec, rows(width), whole(out_weight.shape), whole(scales.shape)],
        out_specs=[rows(width)] * 4 + [pl.BlockSpec((8, width), lambda i: (0, 0))],
        out_shape=[jax.ShapeDtypeStruct((tokens, width), kind) for kind in (FULL, LOW, LOW, FULL)]
        + [jax.ShapeDtypeStruct((8, width), FULL)],
        scratch_shapes=[pltpu.VMEM((tile + MARGIN, width), FULL), pltpu.VMEM((MARGIN, width), FULL)],
        compiler_params=pltpu.CompilerParams(vmem_limit_bytes=44 << 20),
        cost_estimate=pl.CostEstimate(flops=2 * tokens * width * width, bytes_accessed=32 << 20, transcendentals=0),
        name="mixer_middle",
    )(marks, own, other, residual, cotangent, product, before, opened, out_weight, scales)


def project_grads(marks, conv_grad, after, gate, value, open_grad, scales):
    tokens, width = conv_grad.shape
    tile = 256
    per_row = tokens // 2 // tile
    steps = tokens // tile

    def kernel(marks_ref, conv_ref, after_ref, gate_ref, value_ref, open_ref, scale_ref, grad_out, ext, carry):
        at = (steps - 1 - pl.program_id(0)) % per_row

        @pl.when(at == per_row - 1)
        def _():
            carry[...] = after_ref[...]

        grad = conv_ref[...]
        ext[:tile, :] = grad
        ext[tile:, :] = carry[...]
        carry[...] = grad[:8]
        product_grad = (
            scale_ref[2:3, :] * grad
            + marks_ref[:, 3:4] * scale_ref[3:4, :] * ext[1 : 1 + tile, :]
            + marks_ref[:, 4:5] * scale_ref[4:5, :] * ext[2 : 2 + tile, :]
        )
        grad_out[:, :width] = narrow(product_grad * value_ref[...].astype(FULL))
        grad_out[:, width : 2 * width] = open_ref[...]
        grad_out[:, 2 * width :] = narrow(product_grad * gate_ref[...].astype(FULL))

    def rows(last):
        return pl.BlockSpec((tile, last), lambda i: (steps - 1 - i, 0))

    row_spec = pl.BlockSpec((8, width), lambda i: ((steps - 1 - i) // per_row, 0))
    return pl.pallas_call(
        kernel,
        grid=(steps,),
        in_specs=[rows(8), rows(width), row_spec, rows(width), rows(width), rows(width), whole(scales.shape)],
        out_specs=rows(3 * width),
        out_shape=jax.ShapeDtypeStruct((tokens, 3 * width), LOW),
        scratch_shapes=[pltpu.VMEM((tile + 8, width), FULL), pltpu.VMEM((8, width), FULL)],
        compiler_params=pltpu.CompilerParams(vmem_limit_bytes=32 << 20),
        cost_estimate=pl.CostEstimate(flops=10 * tokens * width, bytes_accessed=16 << 20, transcendentals=0),
        name="project_grads",
    )(marks, conv_grad, after, gate, value, open_grad, scales)


def pair_grads(place, left, right, cores, name):
    tokens, width = left.shape
    block = right.shape[1] // 4
    eighth = width // 8
    count = len(cores)
    step = 256

    def kernel(place_ref, left_ref, right_ref, *outs):
        at = pl.program_id(0)
        for n in range(block // step):
            total = narrow(contract_rows(left_ref[...], right_ref[:, n * step : (n + 1) * step]))
            for c in range(count):
                @pl.when(at // 2 == c)
                def _():
                    for i in range(8):
                        outs[c][0, place_ref[2 + i], :, n * step : (n + 1) * step] = total[i * eighth : (i + 1) * eighth]

    def column(i, place_ref):
        return (0, place_ref[14 + 2 * cores[0] + i])

    def out_spec(c):
        return pl.BlockSpec(
            (1, 8, eighth, block), lambda i, place_ref: (jnp.clip(i - 2 * c, 0, 1), 0, 0, 0)
        )

    return pl.pallas_call(
        kernel,
        grid_spec=pltpu.PrefetchScalarGridSpec(
            num_scalar_prefetch=1,
            grid=(2 * count,),
            in_specs=[
                pl.BlockSpec((tokens, width), lambda i, place_ref: (0, 0), pipeline_mode=pl.Buffered(1)),
                pl.BlockSpec((tokens, block), column),
            ],
            out_specs=[out_spec(c) for c in range(count)],
        ),
        out_shape=[jax.ShapeDtypeStruct((2, 8, eighth, block), LOW)] * count,
        compiler_params=pltpu.CompilerParams(vmem_limit_bytes=32 << 20),
        cost_estimate=pl.CostEstimate(
            flops=count * 4 * tokens * width * block, bytes_accessed=8 << 20, transcendentals=0
        ),
        name=name,
    )(place, left, right)


def mixer_backward(project_grad, in_weight, hidden, residual_grad, sums, scales):
    tokens, width = hidden.shape
    tile = 256
    steps = tokens // tile

    def kernel(grad_ref, in_ref, hidden_ref, residual_ref, sums_ref, scale_ref, input_out, sums_out):
        @pl.when(pl.program_id(0) == 0)
        def _():
            sums_out[...] = sums_ref[...]

        normed_grad = contract_cols(grad_ref[...], in_ref[...])
        source = hidden_ref[...].astype(FULL)
        inverse = lax.rsqrt(jnp.mean(source * source, axis=1, keepdims=True) + EPS)
        sums_out[0:1, :] += jnp.sum(normed_grad * (source * inverse), axis=0, keepdims=True)
        scaled = scale_ref[0:1, :] * normed_grad
        lean = (inverse * inverse * inverse) * jnp.mean(scaled * source, axis=1, keepdims=True)
        input_out[...] = narrow(residual_ref[...] + inverse * scaled - source * lean)

    def rows(last):
        return pl.BlockSpec((tile, last), lambda i: (i, 0))

    small = pl.BlockSpec((8, width), lambda i: (0, 0))
    return pl.pallas_call(
        kernel,
        grid=(steps,),
        in_specs=[rows(3 * width), whole(in_weight.shape), rows(width), rows(width), small, whole(scales.shape)],
        out_specs=[rows(width), small],
        out_shape=[jax.ShapeDtypeStruct((tokens, width), LOW), jax.ShapeDtypeStruct((8, width), FULL)],
        compiler_params=pltpu.CompilerParams(vmem_limit_bytes=32 << 20),
        cost_estimate=pl.CostEstimate(flops=6 * tokens * width * width, bytes_accessed=20 << 20, transcendentals=0),
        name="mixer_backward",
    )(project_grad, in_weight, hidden, residual_grad, sums, scales)


def plain(
    hidden_in,
    mixer_gain,
    in_weight,
    conv_kernel,
    out_weight,
    feed_gain,
    gate_weight,
    up_weight,
    down_weight,
    document_lengths,
    valid_tokens,
    cotangent,
):
    row_count, span_length, model_width = hidden_in.shape
    token_count = row_count * span_length
    offset = lax.axis_index("seq") * span_length
    positions = offset + jnp.arange(span_length, dtype=jnp.int32)
    starts = jnp.cumsum(document_lengths, axis=1) - document_lengths
    is_start = jnp.any(positions[None, :, None] == starts[:, None, :], axis=2)
    before = jnp.any((positions - 1)[None, :, None] == starts[:, None, :], axis=2)
    keep_one = (1.0 - is_start.astype(jnp.float32))[:, :, None]
    keep_two = keep_one * (1.0 - before.astype(jnp.float32))[:, :, None]
    valid_mask = (
        (positions[None, :] < valid_tokens[:, None]).astype(jnp.float32).reshape(token_count, 1)
    )
    mixer_scale = mixer_gain.astype(jnp.float32)
    feed_scale = feed_gain.astype(jnp.float32)
    kernel = conv_kernel.astype(jnp.float32)
    source = hidden_in.astype(jnp.float32).reshape(token_count, model_width)
    inverse_one = lax.rsqrt(jnp.mean(source * source, axis=1, keepdims=True) + EPS)
    normed = (source * inverse_one * mixer_scale).astype(jnp.bfloat16)
    project = jnp.dot(normed, in_weight, preferred_element_type=jnp.float32)
    input_gate = project[:, :model_width]
    output_gate = project[:, model_width : 2 * model_width]
    values = project[:, 2 * model_width :]
    product = (
        (input_gate * values).astype(jnp.bfloat16).reshape(row_count, span_length, model_width)
    )
    rim_values = passed_along(product[:, span_length - 2 :, :], "seq", 1)
    extended = jnp.concatenate([rim_values, product], axis=1).astype(jnp.float32)
    tap_zero = extended[:, 2:, :]
    tap_one = keep_one * extended[:, 1:-1, :]
    tap_two = keep_two * extended[:, :-2, :]
    conv_out = (kernel[:, 0] * tap_zero + kernel[:, 1] * tap_one + kernel[:, 2] * tap_two).reshape(
        token_count, model_width
    )
    mixed_in = (output_gate * conv_out).astype(jnp.bfloat16)
    mixer_out = jnp.dot(mixed_in, out_weight, preferred_element_type=jnp.float32)
    residual = source + valid_mask * mixer_out
    inverse_two = lax.rsqrt(jnp.mean(residual * residual, axis=1, keepdims=True) + EPS)
    normed_two = (residual * inverse_two * feed_scale).astype(jnp.bfloat16)
    gate_pre = jnp.dot(normed_two, gate_weight, preferred_element_type=jnp.float32)
    up_pre = jnp.dot(normed_two, up_weight, preferred_element_type=jnp.float32)
    sigmoid_gate = jax.nn.sigmoid(gate_pre)
    activation = (gate_pre * sigmoid_gate * up_pre).astype(jnp.bfloat16)
    feed_out = jnp.dot(activation, down_weight, preferred_element_type=jnp.float32)
    output = (
        (residual + valid_mask * feed_out)
        .astype(jnp.bfloat16)
        .reshape(row_count, span_length, model_width)
    )
    upstream = cotangent.astype(jnp.float32).reshape(token_count, model_width)
    feed_grad = (valid_mask * upstream).astype(jnp.bfloat16)
    down_grad = contract_rows(activation, feed_grad)
    activation_grad = contract_cols(feed_grad, down_weight)
    up_grad = (activation_grad * gate_pre * sigmoid_gate).astype(jnp.bfloat16)
    gate_grad = (
        activation_grad * up_pre * sigmoid_gate * (1.0 + gate_pre * (1.0 - sigmoid_gate))
    ).astype(jnp.bfloat16)
    gate_wgrad = contract_rows(normed_two, gate_grad)
    up_wgrad = contract_rows(normed_two, up_grad)
    normed_two_grad = contract_cols(gate_grad, gate_weight) + contract_cols(up_grad, up_weight)
    feed_gain_grad = jnp.sum(normed_two_grad * residual * inverse_two, axis=0)
    scaled_two = feed_scale * normed_two_grad
    residual_grad = (
        upstream
        + inverse_two * scaled_two
        - residual
        * (inverse_two * inverse_two * inverse_two)
        * jnp.mean(scaled_two * residual, axis=1, keepdims=True)
    )
    feed_gain_part, gate_part, up_part, down_part = (
        lax.psum_scatter(
            feed_gain_grad.astype(jnp.bfloat16), "seq", scatter_dimension=0, tiled=True
        ).astype(jnp.float32),
        lax.psum_scatter(
            gate_wgrad.astype(jnp.bfloat16), "seq", scatter_dimension=0, tiled=True
        ).astype(jnp.float32),
        lax.psum_scatter(
            up_wgrad.astype(jnp.bfloat16), "seq", scatter_dimension=0, tiled=True
        ).astype(jnp.float32),
        lax.psum_scatter(
            down_grad.astype(jnp.bfloat16), "seq", scatter_dimension=0, tiled=True
        ).astype(jnp.float32),
    )
    gate_part, up_part, down_part = (
        lax.psum_scatter(
            gate_part.astype(jnp.bfloat16), "row", scatter_dimension=1, tiled=True
        ).astype(jnp.float32),
        lax.psum_scatter(
            up_part.astype(jnp.bfloat16), "row", scatter_dimension=1, tiled=True
        ).astype(jnp.float32),
        lax.psum_scatter(
            down_part.astype(jnp.bfloat16), "row", scatter_dimension=1, tiled=True
        ).astype(jnp.float32),
    )
    mixer_grad = (valid_mask * residual_grad).astype(jnp.bfloat16)
    out_wgrad = contract_rows(mixed_in, mixer_grad)
    mixed_grad = contract_cols(mixer_grad, out_weight)
    output_gate_grad = mixed_grad * conv_out
    conv_grad = (mixed_grad * output_gate).reshape(row_count, span_length, model_width)
    kernel_grad = jnp.stack(
        [
            jnp.sum(conv_grad * tap_zero, axis=(0, 1)),
            jnp.sum(conv_grad * tap_one, axis=(0, 1)),
            jnp.sum(conv_grad * tap_two, axis=(0, 1)),
        ],
        axis=1,
    )
    grad_zero = kernel[:, 0] * conv_grad
    grad_one = keep_one * kernel[:, 1] * conv_grad
    grad_two = keep_two * kernel[:, 2] * conv_grad
    extended_grad = (
        jnp.pad(grad_zero, ((0, 0), (2, 0), (0, 0)))
        + jnp.pad(grad_one, ((0, 0), (1, 1), (0, 0)))
        + jnp.pad(grad_two, ((0, 0), (0, 2), (0, 0)))
    )
    returned = passed_along(extended_grad[:, :2, :], "seq", -1)
    product_grad = extended_grad[:, 2:, :] + jnp.pad(
        returned, ((0, 0), (span_length - 2, 0), (0, 0))
    )
    flat_grad = product_grad.reshape(token_count, model_width)
    project_grad = jnp.concatenate(
        [flat_grad * values, output_gate_grad, flat_grad * input_gate], axis=1
    ).astype(jnp.bfloat16)
    in_wgrad = contract_rows(normed, project_grad)
    normed_grad = contract_cols(project_grad, in_weight)
    mixer_gain_grad = jnp.sum(normed_grad * source * inverse_one, axis=0)
    scaled_one = mixer_scale * normed_grad
    input_grad = (
        residual_grad
        + inverse_one * scaled_one
        - source
        * (inverse_one * inverse_one * inverse_one)
        * jnp.mean(scaled_one * source, axis=1, keepdims=True)
    )
    input_grad = input_grad.astype(jnp.bfloat16).reshape(row_count, span_length, model_width)
    mixer_gain_part, in_part, kernel_part, out_part = (
        lax.psum_scatter(
            mixer_gain_grad.astype(jnp.bfloat16), "seq", scatter_dimension=0, tiled=True
        ).astype(jnp.float32),
        lax.psum_scatter(
            in_wgrad.astype(jnp.bfloat16), "seq", scatter_dimension=0, tiled=True
        ).astype(jnp.float32),
        lax.psum_scatter(
            kernel_grad.astype(jnp.bfloat16), "seq", scatter_dimension=0, tiled=True
        ).astype(jnp.float32),
        lax.psum_scatter(
            out_wgrad.astype(jnp.bfloat16), "seq", scatter_dimension=0, tiled=True
        ).astype(jnp.float32),
    )
    in_part, out_part = (
        lax.psum_scatter(
            in_part.astype(jnp.bfloat16), "row", scatter_dimension=1, tiled=True
        ).astype(jnp.float32),
        lax.psum_scatter(
            out_part.astype(jnp.bfloat16), "row", scatter_dimension=1, tiled=True
        ).astype(jnp.float32),
    )
    mixer_gain_part, feed_gain_part, kernel_part = lax.psum(
        (mixer_gain_part, feed_gain_part, kernel_part), "row"
    )
    return (
        output,
        input_grad,
        mixer_gain_part,
        in_part,
        kernel_part,
        out_part,
        feed_gain_part,
        gate_part,
        up_part,
        down_part,
    )


def joined(keeps, takes, name):
    count = len(keeps)
    shape = (count,) + keeps[0].shape[1:]

    def kernel(*refs):
        for n in range(count):
            for side in range(2):
                refs[2 * count + side][n] = narrow(wide(refs[n][side], refs[count + n][side]))

    def spec(first):
        return pl.BlockSpec((first, 1) + shape[2:], lambda i: (0, i, 0, 0))

    return pl.pallas_call(
        kernel,
        grid=(shape[1],),
        in_specs=[spec(2)] * (2 * count),
        out_specs=[spec(count)] * 2,
        out_shape=[pltpu.HBM(shape, LOW)] * 2,
        compiler_params=pltpu.CompilerParams(vmem_limit_bytes=32 << 20),
        name=name,
    )(*far(*keeps, *takes))


def side_by_side(keeps, takes):
    count = len(keeps)
    widths = [keep.shape[-1] for keep in keeps]
    shape = (2, keeps[0].shape[-2], sum(widths))

    def kernel(*refs):
        for n in range(count):
            at = pl.ds(sum(widths[:n]), widths[n])
            for side in range(2):
                refs[2 * count + side][0, :, at] = narrow(wide(refs[n][side], refs[count + n][side]))

    def spec(first, last):
        return pl.BlockSpec((first, shape[1], last), lambda i: (i, 0, 0))

    return pl.pallas_call(
        kernel,
        grid=(2,),
        in_specs=[spec(2, size) for size in widths] * 2,
        out_specs=[spec(1, shape[2])] * 2,
        out_shape=[pltpu.HBM(shape, LOW)] * 2,
        compiler_params=pltpu.CompilerParams(vmem_limit_bytes=32 << 20),
        name="side_by_side",
    )(*far(*keeps, *takes))


def last_sums(keeps, takes):
    counts = [keep.shape[0] for keep in keeps]
    height, part = keeps[0].shape[1:]
    shape = (height, sum(counts) // 2 * part)

    def kernel(*refs):
        n = 0
        for i, count in enumerate(counts):
            for k in range(count):
                refs[2 * len(counts) + n % 2][:, pl.ds(n // 2 * part, part)] = wide(
                    refs[i][k], refs[len(counts) + i][k]
                )
                n += 1

    rows = height // 2
    return pl.pallas_call(
        kernel,
        grid=(2,),
        in_specs=[pl.BlockSpec((count, rows, part), lambda i: (0, i, 0)) for count in counts] * 2,
        out_specs=[pl.BlockSpec((rows, shape[1]), lambda i: (i, 0))] * 2,
        out_shape=[pltpu.HBM(shape, FULL)] * 2,
        compiler_params=pltpu.CompilerParams(vmem_limit_bytes=32 << 20),
        name="last_sums",
    )(*far(*keeps, *takes))


def fast(
    hidden_in,
    mixer_gain,
    in_weight,
    conv_kernel,
    out_weight,
    feed_gain,
    gate_weight,
    up_weight,
    down_weight,
    document_lengths,
    valid_tokens,
    cotangent,
):
    row_count, span_length, model_width = hidden_in.shape
    token_count = row_count * span_length
    hidden_width = gate_weight.shape[1]
    block = hidden_width // 4
    chunks = 3
    part = block // chunks
    seq = lax.axis_index("seq")
    row = lax.axis_index("row")
    row_x, core = row // 2, row % 2
    seq_y, seq_z0, seq_z1 = seq % 2, (seq // 2) % 2, seq // 4
    place = jnp.stack(
        [row ^ 2, row]
        + [i ^ seq ^ 7 for i in range(8)]
        + [1 - row_x, row_x, 1 - ((1 - row_x) ^ seq_z1), 1 - (row_x ^ seq_z1)]
        + [row ^ 3, row ^ 1, row ^ 2, row]
    ).astype(jnp.int32)
    positions = seq * span_length + jnp.arange(span_length, dtype=jnp.int32)
    starts = jnp.cumsum(document_lengths, axis=1) - document_lengths

    def unstarted(shift):
        return 1.0 - jnp.any((positions + shift)[None, :, None] == starts[:, None, :], axis=2).astype(FULL)

    here, last, one_on, two_on = (unstarted(shift) for shift in (0, -1, 1, 2))
    valid = (positions[None, :] < valid_tokens[:, None]).astype(FULL)
    blank = jnp.zeros_like(valid)
    marks = jnp.stack([here, here * last, valid, one_on, two_on * one_on, blank, blank, blank], axis=2).reshape(
        token_count, 8
    )
    valid_mask = marks[:, 2:3]
    scales = jnp.concatenate(
        [mixer_gain[None], feed_gain[None], conv_kernel.T, jnp.zeros((3, model_width), conv_kernel.dtype)]
    ).astype(FULL)
    hidden = hidden_in.reshape(token_count, model_width)
    upstream = cotangent.reshape(token_count, model_width)
    rim = passed_along(hidden_in[:, span_length - 2 :, :], "seq", 1)
    rim = jnp.pad(rim, ((0, 0), (MARGIN - 2, 0), (0, 0))).reshape(row_count * MARGIN, model_width)
    feed_grad = narrow(valid_mask * upstream.astype(FULL))
    other_grad = swapped(feed_grad, "row", 1)
    normed, input_gate, output_gate, values, product, mixed_in, residual, normed_two, before = mixer_forward(
        marks, hidden, rim, in_weight, out_weight, scales
    )
    other_normed = swapped(normed_two, "row", 1)

    def chunk_grads(start, chunk):
        return feed_chunk(
            start, normed_two, other_normed, feed_grad, other_grad, gate_weight, up_weight, down_weight, chunk, chunks
        )

    def sent(made):
        gs, us, ds = made[3], made[5], made[7]
        return swapped(gs, "seq", 2), swapped(us, "seq", 1), swapped(ds, "row", 2)

    def together(*values):
        return lax.optimization_barrier(values)

    def follow(value, *ahead):
        return lax.optimization_barrier((value,) + ahead)[0]

    def first_sums(made, taken):
        pairs = ((made[4], taken[0]), (made[6], taken[1]))
        halves = [narrow(wide(keep[i], take[i])) for keep, take in pairs for i in range(2)]
        return halves + [narrow(wide(made[8], taken[2]))]

    def second(sums):
        return swapped(sums[0], "seq", 1), swapped(sums[2], "seq", 2)

    def split(keep, take, at):
        return [
            narrow(wide(lax.index_in_dim(keep, i, at, False), lax.index_in_dim(take, i, at, False))) for i in range(2)
        ]

    made0 = chunk_grads(place, 0)
    taken0 = sent(made0)
    made1, taken0 = together(chunk_grads(follow(place, made0[0]), 1), taken0)
    taken1 = sent(made1)
    sums0 = first_sums(made0, taken0)
    second0 = second(sums0)
    made2, taken1, second0 = together(chunk_grads(follow(place, sums0), 2), taken1, second0)
    taken2 = sent(made2)
    sums1 = first_sums(made1, taken1)
    second1 = second(sums1)
    acts, gates, ups = ([one[i] for one in (made0, made1, made2)] for i in range(3))
    (own_ntg, give_ntg), taken2, second1 = together(
        feed_sum(follow(place, sums1), [gates, ups], [gate_weight, up_weight], True, block, "normed_two_grad"),
        taken2,
        second1,
    )
    take_ntg = swapped(give_ntg, "row", 1)
    sums2 = first_sums(made2, taken2)
    second2 = second(sums2)
    third_give, third_keep = joined([sums0[1], sums0[3], sums1[1], sums1[3]], second0 + second1, "third_sums")
    third_take = swapped(third_give, "row", 2)

    (residual_grad, mixer_grad, open_grad, conv_grad, sums), second2 = together(
        mixer_middle(
            follow(marks, sums2, third_keep), own_ntg, take_ntg, residual, upstream, product, before, output_gate,
            out_weight, scales,
        ),
        second2,
    )
    after = passed_along(conv_grad.reshape(row_count, span_length, model_width)[:, :2, :], "seq", -1)
    late_give, late_keep = joined([sums2[1], sums2[3]], second2, "late_sums")
    late_take = swapped(late_give, "row", 2)
    down = jnp.concatenate(follow([sums0[4], sums1[4], sums2[4]], mixer_grad), axis=1)
    low_half, high_half = down[:, : block // 2], down[:, block // 2 :]
    down_keep = jnp.where(seq_y == 0, low_half, high_half)
    down_give = jnp.where(seq_y == 0, high_half, low_half)

    (out_give, out_keep), after, third_take, down_give = together(
        pair_grads(follow(place, late_keep, down_keep, down_give), mixed_in, mixer_grad, (0, 1), "out_grads"),
        after,
        third_take,
        down_give,
    )
    down_takes = [swapped(down_give[0], "seq", 1)]
    out_take = swapped(out_give, "row", 1)
    after = jnp.pad(after, ((0, 0), (0, 6), (0, 0))).reshape(row_count * 8, model_width)
    fourth_give, fourth_keep = split(third_keep, third_take, 1)
    fourth_take = swapped(fourth_give, "seq", 4)

    project_grad = project_grads(
        follow(marks, out_keep, fourth_give, fourth_keep), conv_grad, after, input_gate, values, open_grad, scales
    )
    (in_give,), out_take, late_take, down_takes, fourth_take = together(
        pair_grads(place, normed, project_grad, (0,), "in_grads_give"), out_take, late_take, down_takes, fourth_take
    )
    in_take = swapped(in_give, "row", 1)
    out_give, out_keep = split(out_keep, out_take, 0)
    out_take = swapped(out_give, "row", 2)
    down_takes.append(swapped(follow(down_give[1], out_give), "seq", 1))
    late_give, late_keep = split(late_keep, late_take, 1)
    late_take = swapped(late_give, "seq", 4)

    (in_keep,), in_take, out_take, down_takes, late_take = together(
        pair_grads(
            follow(place, in_give, out_give, out_keep, late_give, late_keep), normed, project_grad, (1,), "in_grads_keep"
        ),
        in_take,
        out_take,
        down_takes,
        late_take,
    )
    half = in_keep.shape[-1] // 2
    left_give, left_keep = split(in_keep[..., :half], in_take[..., :half], 0)
    left_take = swapped(left_give, "row", 2)
    eighths = (2, 4, 2, model_width // 8, half)
    right_give, right_keep = split(in_keep[..., half:].reshape(eighths), in_take[..., half:].reshape(eighths), 2)
    right_take = swapped(right_give, "seq", 1)
    eighths = (4, 2, model_width // 8, out_keep.shape[-1])
    out_give, out_keep = split(out_keep.reshape(eighths), out_take.reshape(eighths), 1)
    down_give, down_keep = (narrow(wide(down_keep[i], down_takes[i])) for i in range(2))
    quarter = down_give.shape[0] // 2
    down_takes = [swapped(down_give[:quarter], "seq", 4)]

    (input_grad, small), left_take, right_take, down_takes, out_give, down_give = together(
        mixer_backward(
            follow(
                project_grad, left_give, left_keep, right_give, right_keep, out_give, out_keep, down_give, down_keep,
            ),
            in_weight, hidden, residual_grad, sums, scales,
        ),
        left_take,
        right_take,
        down_takes,
        out_give,
        down_give,
    )
    eighths = (4, 2, model_width // 8, half)
    left_give, left_keep = split(left_keep.reshape(eighths), left_take.reshape(eighths), 1)
    left_take = swapped(left_give, "seq", 1)
    right_give, right_keep = split(right_keep, right_take, 0)
    right_take = swapped(right_give, "row", 2)
    small_take = swapped(small, "row", 1)
    down_takes.append(swapped(down_give[quarter:], "seq", 4))
    out_take = swapped(follow(out_give, left_give), "seq", 1)

    (give_feed,), left_take, right_take, out_take, small_take, down_takes = together(
        feed_sum(
            follow(place, left_give, left_keep, right_give, right_keep),
            [acts], [down_weight], False, block, "feed_out_give", (1,),
        ),
        left_take,
        right_take,
        out_take,
        small_take,
        down_takes,
    )
    give, keep = side_by_side([left_keep, right_keep, out_keep], [left_take, right_take, out_take])
    take = swapped(give, "seq", 2)
    take_feed = swapped(give_feed, "row", 1)
    small = small + small_take
    small_take = swapped(small, "row", 2)
    down = narrow(wide(down_keep, jnp.concatenate(follow(down_takes, give))))
    holder = [[(r & 1) == ((s >> 1) & 1) for r in range(4)] for s in range(8)]
    down_take = lax.ppermute(
        down,
        ("seq", "row"),
        [(s * 4 + r, (s ^ 2) * 4 + r) for s in range(8) for r in range(4) if not holder[s][r]],
    )

    (own_feed,), take, take_feed, small_take, down_take = together(
        feed_sum(
            follow(place, give, keep, small, down), [acts], [down_weight], False, block, "feed_out_keep", (0,)
        ),
        take,
        take_feed,
        small_take,
        down_take,
    )
    give, keep = split(keep, take, 0)
    take = swapped(give, "seq", 4)
    small = small + small_take
    small_take = swapped(small, "seq", 1)
    down = wide(down, down_take)
    quarter = model_width // 4
    down_own = jnp.where(core == 0, down[:, :quarter], down[:, quarter:])
    down_other = narrow(jnp.where(core == 0, down[:, quarter:], down[:, :quarter]))
    down_other = lax.ppermute(
        down_other,
        ("seq", "row"),
        [(s * 4 + r, s * 4 + (r ^ 1)) for s in range(8) for r in range(4) if holder[s][r]],
    )
    (gate_part, up_part), small_take = together(
        last_sums(*follow(([fourth_keep, late_keep], [fourth_take, late_take]), give)), small_take
    )
    small = small + small_take
    small_take = swapped(small, "seq", 2)
    output = narrow(residual + valid_mask * wide(own_feed, follow(take_feed, small)))
    output, small_take = together(output, small_take)
    output = output.reshape(row_count, span_length, model_width)
    small = small + small_take
    small_take = swapped(small, "seq", 4)
    down_part = jnp.where(core == seq_z0, down_own, down_other.astype(jnp.float32))
    input_grad = input_grad.reshape(row_count, span_length, model_width)
    both_part = wide(keep, take)
    in_part, out_part = both_part[:, : 2 * half], both_part[:, 2 * half :]
    small = small + small_take
    small = lax.dynamic_slice_in_dim(small, seq * (model_width // 8), model_width // 8, 1)
    return (
        output,
        input_grad,
        small[0],
        in_part,
        small[2:5].T,
        out_part,
        small[1],
        gate_part,
        up_part,
        down_part,
    )


def local(*args):
    hidden_in, gate_weight = args[0], args[6]
    tokens = hidden_in.shape[0] * hidden_in.shape[1]
    width, hidden = gate_weight.shape
    tiled = lax.axis_size("seq") == 8 and lax.axis_size("row") == 4 and hidden % (4 * 3 * 128) == 0
    if tiled and width % 1024 == 0 and tokens % 512 == 0:
        return fast(*args)
    return plain(*args)


def solution(mesh):
    in_specs = (
        P("row", "seq", None),
        P(),
        P(),
        P(),
        P(),
        P(),
        P(),
        P(),
        P(),
        P("row", None),
        P("row"),
        P("row", "seq", None),
    )
    out_specs = (
        P("row", "seq", None),
        P("row", "seq", None),
        P("seq"),
        P("seq", "row"),
        P("seq", None),
        P("seq", "row"),
        P("seq"),
        P("seq", "row"),
        P("seq", "row"),
        P("seq", "row"),
    )
    return jax.shard_map(local, mesh=mesh, in_specs=in_specs, out_specs=out_specs, check_vma=False)
```

```python
import jax
import jax.numpy as jnp
from jax import lax
from jax.experimental import pallas as pl
from jax.experimental.pallas import tpu as pltpu
from jax.sharding import PartitionSpec as P

EPS = 1e-05


def passed_along(value, axis, by):
    length = lax.axis_size(axis)
    pairs = [(i, i + by) for i in range(length) if 0 <= i + by < length]
    return lax.ppermute(value, axis, pairs)


def contract_rows(left, right):
    return lax.dot_general(
        left, right, (((0,), (0,)), ((), ())), preferred_element_type=jnp.float32
    )


def contract_cols(left, right):
    return lax.dot_general(
        left, right, (((1,), (1,)), ((), ())), preferred_element_type=jnp.float32
    )


def far(*values):
    return [pltpu.with_memory_space_constraint(value, pltpu.HBM) for value in values]


def swapped(value, axis, bit):
    length = lax.axis_size(axis)
    return lax.ppermute(value, axis, [(i, i ^ bit) for i in range(length)])


def wide(left, right):
    return left.astype(jnp.float32) + right.astype(jnp.float32)


def narrow(value):
    return value.astype(jnp.bfloat16)


def feed_chunk(place, own_in, other_in, own_grad, other_grad, gate_weight, up_weight, down_weight, chunk, chunks):
    tokens, width = own_in.shape
    hidden = gate_weight.shape[1]
    rows = 2
    block = hidden // 4
    part = block // chunks
    span = rows * part
    tile = min(512, tokens)
    tiles = 2 * tokens // tile
    half_tiles = tokens // tile
    eighth = width // 8
    step = 256

    def kernel(
        place_ref, own_ref, other_ref, own_grad_ref, other_grad_ref, gate_ref, up_ref, down_ref,
        act_out, gate_out, up_out, gate_send, gate_keep, up_send, up_keep, down_send, down_keep,
        tok, grd, wg, wu, wd, act, gg, ug, gw, uw, dw, tok_t, act_t, in_sem, w_sem, out_sem, grad_sem,
    ):
        def token_copy(t, which):
            buf = (tok, grd)[which]
            src = ((own_ref, other_ref), (own_grad_ref, other_grad_ref))[which][0 if t < half_tiles else 1]
            return pltpu.make_async_copy(
                src.at[pl.ds((t % half_tiles) * tile, tile)],
                buf.at[pl.ds(t * tile, tile)],
                in_sem.at[which, t],
            )

        weight_copies = []
        for n, (ref, buf) in enumerate(((gate_ref, wg), (up_ref, wu))):
            weight_copies.append([
                pltpu.make_async_copy(
                    ref.at[:, pl.ds(pl.multiple_of(place_ref[j] * block + chunk * part, 128), part)],
                    buf.at[:, pl.ds(j * part, part)],
                    w_sem.at[n, j],
                )
                for j in range(2)
            ])
        weight_copies.append([
            pltpu.make_async_copy(
                down_ref.at[pl.ds(pl.multiple_of(place_ref[j] * block + chunk * part, 128), part), :],
                wd.at[pl.ds(j * part, part), :],
                w_sem.at[2, j],
            )
            for j in range(2)
        ])
        token_copy(0, 0).start()
        for copy in weight_copies[0]:
            copy.start()
        for copy in weight_copies[1]:
            copy.start()
        token_copy(0, 1).start()
        for copy in weight_copies[2]:
            copy.start()
        outs = []
        for t in range(tiles):
            at = pl.ds(t * tile, tile)
            token_copy(t, 0).wait()
            if t == 0:
                for copy in weight_copies[0] + weight_copies[1]:
                    copy.wait()
            if t + 1 < tiles:
                token_copy(t + 1, 0).start()
                token_copy(t + 1, 1).start()
            token_copy(t, 1).wait()
            if t == 0:
                for copy in weight_copies[2]:
                    copy.wait()
            tok_t[:, at] = tok[at, :].T
            for n in range(span // step):
                cols = pl.ds(n * step, step)
                gate = jnp.dot(tok[at, :], wg[:, cols], preferred_element_type=jnp.float32)
                up = jnp.dot(tok[at, :], wu[:, cols], preferred_element_type=jnp.float32)
                grad = contract_cols(grd[at, :], wd[cols, :])
                sig = jax.nn.sigmoid(gate)
                gate_sig = gate * sig
                made = narrow(gate_sig * up)
                act[at, cols] = made
                act_t[cols, at] = made.T
                ug[at, cols] = narrow(grad * gate_sig)
                gg[at, cols] = narrow(grad * up * (sig + gate_sig * (1.0 - sig)))
            for n, (buf, out) in enumerate(((act, act_out), (gg, gate_out), (ug, up_out))):
                copy = pltpu.make_async_copy(buf.at[at], out.at[at], out_sem.at[n, t])
                copy.start()
                outs.append(copy)

        for buf, grad in ((gw, gg), (uw, ug)):
            for n in range(span // step):
                cols = pl.ds(n * step, step)
                total = narrow(jnp.dot(tok_t[...], grad[:, cols], preferred_element_type=jnp.float32))
                for i in range(8):
                    spot = place_ref[2 + i]
                    rows_i = total[i * eighth : (i + 1) * eighth]
                    for c in range(step // 128):
                        col = n * step + c * 128
                        buf[col // part, spot, :, pl.ds(col % part, 128)] = rows_i[:, c * 128 : (c + 1) * 128]
            if buf is gw:
                pairs = [
                    (gw.at[j, pl.ds(4 * h + 2 * z, 2)], out.at[:, j, h], grad_sem.at[8 + 4 * z + 2 * j + h])
                    for z, out in enumerate((gate_send, gate_keep))
                    for j in range(2)
                    for h in range(2)
                ]
            else:
                pairs = [
                    (uw.at[j, 4 * h + 2 * z + y], out.at[z, j, h], grad_sem.at[16 + 8 * y + 4 * z + 2 * j + h])
                    for y, out in enumerate((up_send, up_keep))
                    for z in range(2)
                    for j in range(2)
                    for h in range(2)
                ]
            for src, out, sem in pairs:
                copy = pltpu.make_async_copy(src, out, sem)
                copy.start()
                outs.append(copy)
        for side in range(2):
            for n in range(2):
                cols = pl.ds(pl.multiple_of(place_ref[10 + side] * (width // 2) + n * (width // 4), 128), width // 4)
                total = narrow(jnp.dot(act_t[...], grd[:, cols], preferred_element_type=jnp.float32))
                for j in range(2):
                    dw[side, place_ref[12 + j], :, pl.ds(n * (width // 4), width // 4)] = total[j * part : (j + 1) * part]
            copy = pltpu.make_async_copy(dw.at[side], (down_send, down_keep)[side], grad_sem.at[side])
            copy.start()
            outs.append(copy)
        for copy in outs:
            copy.wait()

    any_spec = pl.BlockSpec(memory_space=pltpu.HBM)
    low = jnp.bfloat16
    both = 2 * tokens
    flops = 6 * 2 * both * width * span
    return pl.pallas_call(
        kernel,
        out_shape=[jax.ShapeDtypeStruct((both, span), low)] * 3
        + [jax.ShapeDtypeStruct((2, 2, 2, eighth, part), low)] * 4
        + [jax.ShapeDtypeStruct((2, part, width // 2), low)] * 2,
        grid_spec=pltpu.PrefetchScalarGridSpec(
            num_scalar_prefetch=1,
            grid=(1,),
            in_specs=[any_spec] * 7,
            out_specs=[any_spec] * 9,
            scratch_shapes=[
                pltpu.VMEM((both, width), low),
                pltpu.VMEM((both, width), low),
                pltpu.VMEM((width, span), low),
                pltpu.VMEM((width, span), low),
                pltpu.VMEM((span, width), low),
                pltpu.VMEM((both, span), low),
                pltpu.VMEM((both, span), low),
                pltpu.VMEM((both, span), low),
                pltpu.VMEM((2, 8, eighth, part), low),
                pltpu.VMEM((2, 8, eighth, part), low),
                pltpu.VMEM((2, 2, part, width // 2), low),
                pltpu.VMEM((width, both), low),
                pltpu.VMEM((span, both), low),
                pltpu.SemaphoreType.DMA((2, tiles)),
                pltpu.SemaphoreType.DMA((3, 2)),
                pltpu.SemaphoreType.DMA((3, tiles)),
                pltpu.SemaphoreType.DMA((32,)),
            ],
        ),
        compiler_params=pltpu.CompilerParams(vmem_limit_bytes=56 << 20),
        cost_estimate=pl.CostEstimate(flops=flops, bytes_accessed=24 << 20, transcendentals=both * span),
        name=f"feed_{chunk}",
    )(place, own_in, other_in, own_grad, other_grad, gate_weight, up_weight, down_weight)


def feed_sum(place, groups, weights, across, block, name, sides=(0, 1)):
    chunks = len(groups[0])
    both, span = groups[0][0].shape
    part = span // 2
    width = weights[0].shape[0] if across else weights[0].shape[1]
    tokens = both // 2
    tile = min(512, tokens)
    half_tiles = tokens // tile
    tiles = len(sides) * half_tiles
    kinds = len(groups)

    def kernel(place_ref, *refs):
        lefts = [refs[g * chunks : (g + 1) * chunks] for g in range(kinds)]
        rights = refs[kinds * chunks : kinds * chunks + kinds]
        sums_out = refs[kinds * chunks + kinds : kinds * chunks + kinds + len(sides)]
        lbuf, wbuf, total, obuf, l_sem, w_sem, o_sem = refs[kinds * chunks + kinds + len(sides) :]

        def weight_copies(k):
            slot = k % 2
            copies = []
            for g in range(kinds):
                for j in range(2):
                    rows = pl.ds(pl.multiple_of(place_ref[j] * block + k * part, 128), part)
                    if across:
                        src, dst = rights[g].at[:, rows], wbuf.at[slot, g, :, pl.ds(j * part, part)]
                    else:
                        src, dst = rights[g].at[rows, :], wbuf.at[slot, g, pl.ds(j * part, part), :]
                    copies.append(pltpu.make_async_copy(src, dst, w_sem.at[slot, g, j]))
            return copies

        def left_copies(k, t, slot):
            row = (sides[t // half_tiles] * half_tiles + t % half_tiles) * tile
            return [
                pltpu.make_async_copy(lefts[g][k].at[pl.ds(row, tile)], lbuf.at[slot, g], l_sem.at[slot, g])
                for g in range(kinds)
            ]

        def out_copy(t, slot):
            ref = sums_out[t // half_tiles]
            return pltpu.make_async_copy(
                obuf.at[slot], ref.at[pl.ds((t % half_tiles) * tile, tile)], o_sem.at[slot]
            )

        for copy in left_copies(0, 0, 0) + weight_copies(0):
            copy.start()
        for k in range(chunks):
            for t in range(tiles):
                n = k * tiles + t
                for copy in left_copies(k, t, n % 2):
                    copy.wait()
                if t == 0:
                    for copy in weight_copies(k):
                        copy.wait()
                if n + 1 < chunks * tiles:
                    for copy in left_copies((n + 1) // tiles, (n + 1) % tiles, (n + 1) % 2):
                        copy.start()
                if t == 0 and k + 1 < chunks:
                    for copy in weight_copies(k + 1):
                        copy.start()
                value = None
                for g in range(kinds):
                    left, right = lbuf[n % 2, g], wbuf[k % 2, g]
                    term = contract_cols(left, right) if across else jnp.dot(left, right, preferred_element_type=jnp.float32)
                    value = term if value is None else value + term
                if k > 0:
                    value = value + total[t]
                if k + 1 < chunks:
                    total[t] = value
                else:
                    if t >= 2:
                        out_copy(t - 2, t % 2).wait()
                    obuf[t % 2] = narrow(value)
                    out_copy(t, t % 2).start()
        for t in range(max(0, tiles - 2), tiles):
            out_copy(t, t % 2).wait()

    any_spec = pl.BlockSpec(memory_space=pltpu.HBM)
    low = jnp.bfloat16
    wshape = (width, span) if across else (span, width)
    return pl.pallas_call(
        kernel,
        out_shape=[jax.ShapeDtypeStruct((tokens, width), low)] * len(sides),
        grid_spec=pltpu.PrefetchScalarGridSpec(
            num_scalar_prefetch=1,
            grid=(1,),
            in_specs=[any_spec] * (kinds * chunks + kinds),
            out_specs=[any_spec] * len(sides),
            scratch_shapes=[
                pltpu.VMEM((2, kinds, tile, span), low),
                pltpu.VMEM((2, kinds) + wshape, low),
                pltpu.VMEM((tiles, tile, width), jnp.float32),
                pltpu.VMEM((2, tile, width), low),
                pltpu.SemaphoreType.DMA((2, kinds)),
                pltpu.SemaphoreType.DMA((2, kinds, 2)),
                pltpu.SemaphoreType.DMA((2,)),
            ],
        ),
        compiler_params=pltpu.CompilerParams(vmem_limit_bytes=48 << 20),
        cost_estimate=pl.CostEstimate(
            flops=kinds * chunks * 2 * both * width * span, bytes_accessed=24 << 20, transcendentals=0
        ),
        name=name,
    )(place, *[item for group in groups for item in group], *weights)


LOW = jnp.bfloat16
FULL = jnp.float32
MARGIN = 16


def whole(shape):
    return pl.BlockSpec(shape, lambda *_: (0,) * len(shape), pipeline_mode=pl.Buffered(1))


def mixer_forward(marks, hidden, rim, in_weight, out_weight, scales):
    tokens, width = hidden.shape
    tile = 256
    per_row = tokens // 2 // tile
    steps = tokens // tile

    def kernel(
        marks_ref, hidden_ref, rim_ref, in_ref, out_ref, scale_ref,
        normed_out, gate_out, open_out, value_out, product_out, mixed_out, residual_out, next_out, before_out,
        ext, carry,
    ):
        at = pl.program_id(0) % per_row
        tile_in = hidden_ref[...].astype(FULL)

        @pl.when(at == 0)
        def _():
            carry[...] = rim_ref[...].astype(FULL)

        source = jnp.concatenate([carry[...], tile_in], axis=0)
        carry[...] = tile_in[tile - MARGIN :]
        inverse = lax.rsqrt(jnp.mean(source * source, axis=1, keepdims=True) + EPS)
        normed = narrow(source * inverse * scale_ref[0:1, :])
        gate = jnp.dot(normed, in_ref[:, :width], preferred_element_type=FULL)
        value = jnp.dot(normed, in_ref[:, 2 * width :], preferred_element_type=FULL)
        product = narrow(gate * value)
        ext[...] = product.astype(FULL)
        opened = jnp.dot(normed[MARGIN:], in_ref[:, width : 2 * width], preferred_element_type=FULL)
        conv = (
            scale_ref[2:3, :] * ext[MARGIN:, :]
            + marks_ref[:, 0:1] * scale_ref[3:4, :] * ext[MARGIN - 1 : MARGIN - 1 + tile, :]
            + marks_ref[:, 1:2] * scale_ref[4:5, :] * ext[MARGIN - 2 : MARGIN - 2 + tile, :]
        )
        mixed = narrow(opened * conv)
        residual = tile_in + marks_ref[:, 2:3] * jnp.dot(mixed, out_ref[...], preferred_element_type=FULL)
        inverse_two = lax.rsqrt(jnp.mean(residual * residual, axis=1, keepdims=True) + EPS)
        next_out[...] = narrow(residual * inverse_two * scale_ref[1:2, :])
        normed_out[...] = normed[MARGIN:]
        gate_out[...] = narrow(gate[MARGIN:])
        open_out[...] = narrow(opened)
        value_out[...] = narrow(value[MARGIN:])
        product_out[...] = product[MARGIN:]
        mixed_out[...] = mixed
        residual_out[...] = residual

        @pl.when(at == 0)
        def _():
            before_out[...] = product[:MARGIN]

    def rows(last, size=tile):
        return pl.BlockSpec((size, last), lambda i: (i, 0))

    row_spec = pl.BlockSpec((MARGIN, width), lambda i: (i // per_row, 0))
    return pl.pallas_call(
        kernel,
        grid=(steps,),
        in_specs=[rows(8), rows(width), row_spec, whole(in_weight.shape), whole(out_weight.shape), whole(scales.shape)],
        out_specs=[rows(width)] * 8 + [row_spec],
        out_shape=[pltpu.HBM((tokens, width), LOW)] * 6
        + [pltpu.HBM((tokens, width), FULL), pltpu.HBM((tokens, width), LOW)]
        + [pltpu.HBM((2 * MARGIN, width), LOW)],
        scratch_shapes=[pltpu.VMEM((tile + MARGIN, width), FULL), pltpu.VMEM((MARGIN, width), FULL)],
        compiler_params=pltpu.CompilerParams(vmem_limit_bytes=44 << 20),
        cost_estimate=pl.CostEstimate(flops=8 * tokens * width * width, bytes_accessed=28 << 20, transcendentals=0),
        name="mixer_forward",
    )(marks, hidden, rim, in_weight, out_weight, scales)


def mixer_middle(marks, own, other, residual, cotangent, product, before, opened, out_weight, scales):
    tokens, width = own.shape
    tile = 256
    per_row = tokens // 2 // tile
    steps = tokens // tile

    def kernel(
        marks_ref, own_ref, other_ref, residual_ref, cot_ref, product_ref, before_ref, open_ref, out_ref, scale_ref,
        grad_out, mixer_out, open_grad_out, conv_out, sums_out,
        ext, carry,
    ):
        step = pl.program_id(0)
        at = step % per_row

        @pl.when(at == 0)
        def _():
            carry[...] = before_ref[...].astype(FULL)

        @pl.when(step == 0)
        def _():
            sums_out[...] = jnp.zeros_like(sums_out)

        grad = own_ref[...].astype(FULL) + other_ref[...].astype(FULL)
        residual = residual_ref[...]
        inverse = lax.rsqrt(jnp.mean(residual * residual, axis=1, keepdims=True) + EPS)
        sums_out[1:2, :] += jnp.sum(grad * (residual * inverse), axis=0, keepdims=True)
        scaled = scale_ref[1:2, :] * grad
        lean = (inverse * inverse * inverse) * jnp.mean(scaled * residual, axis=1, keepdims=True)
        residual_grad = cot_ref[...].astype(FULL) + inverse * scaled - residual * lean
        grad_out[...] = residual_grad
        mixer = narrow(marks_ref[:, 2:3] * residual_grad)
        mixer_out[...] = mixer
        mixed = contract_cols(mixer, out_ref[...])
        product = product_ref[...].astype(FULL)
        ext[:MARGIN, :] = carry[...]
        ext[MARGIN:, :] = product
        carry[...] = product[tile - MARGIN :]
        one = marks_ref[:, 0:1] * ext[MARGIN - 1 : MARGIN - 1 + tile, :]
        two = marks_ref[:, 1:2] * ext[MARGIN - 2 : MARGIN - 2 + tile, :]
        conv = scale_ref[2:3, :] * product + scale_ref[3:4, :] * one + scale_ref[4:5, :] * two
        open_grad_out[...] = narrow(mixed * conv)
        conv_grad = mixed * open_ref[...].astype(FULL)
        conv_out[...] = conv_grad
        sums_out[2:3, :] += jnp.sum(conv_grad * product, axis=0, keepdims=True)
        sums_out[3:4, :] += jnp.sum(conv_grad * one, axis=0, keepdims=True)
        sums_out[4:5, :] += jnp.sum(conv_grad * two, axis=0, keepdims=True)

    def rows(last):
        return pl.BlockSpec((tile, last), lambda i: (i, 0))

    row_spec = pl.BlockSpec((MARGIN, width), lambda i: (i // per_row, 0))
    return pl.pallas_call(
        kernel,
        grid=(steps,),
        in_specs=[rows(8)] + [rows(width)] * 5 + [row_spec, rows(width), whole(out_weight.shape), whole(scales.shape)],
        out_specs=[rows(width)] * 4 + [pl.BlockSpec((8, width), lambda i: (0, 0))],
        out_shape=[jax.ShapeDtypeStruct((tokens, width), kind) for kind in (FULL, LOW, LOW, FULL)]
        + [jax.ShapeDtypeStruct((8, width), FULL)],
        scratch_shapes=[pltpu.VMEM((tile + MARGIN, width), FULL), pltpu.VMEM((MARGIN, width), FULL)],
        compiler_params=pltpu.CompilerParams(vmem_limit_bytes=44 << 20),
        cost_estimate=pl.CostEstimate(flops=2 * tokens * width * width, bytes_accessed=32 << 20, transcendentals=0),
        name="mixer_middle",
    )(marks, own, other, residual, cotangent, product, before, opened, out_weight, scales)


def project_grads(marks, conv_grad, after, gate, value, open_grad, scales):
    tokens, width = conv_grad.shape
    tile = 256
    per_row = tokens // 2 // tile
    steps = tokens // tile

    def kernel(marks_ref, conv_ref, after_ref, gate_ref, value_ref, open_ref, scale_ref, grad_out, ext, carry):
        at = (steps - 1 - pl.program_id(0)) % per_row

        @pl.when(at == per_row - 1)
        def _():
            carry[...] = after_ref[...]

        grad = conv_ref[...]
        ext[:tile, :] = grad
        ext[tile:, :] = carry[...]
        carry[...] = grad[:8]
        product_grad = (
            scale_ref[2:3, :] * grad
            + marks_ref[:, 3:4] * scale_ref[3:4, :] * ext[1 : 1 + tile, :]
            + marks_ref[:, 4:5] * scale_ref[4:5, :] * ext[2 : 2 + tile, :]
        )
        grad_out[:, :width] = narrow(product_grad * value_ref[...].astype(FULL))
        grad_out[:, width : 2 * width] = open_ref[...]
        grad_out[:, 2 * width :] = narrow(product_grad * gate_ref[...].astype(FULL))

    def rows(last):
        return pl.BlockSpec((tile, last), lambda i: (steps - 1 - i, 0))

    row_spec = pl.BlockSpec((8, width), lambda i: ((steps - 1 - i) // per_row, 0))
    return pl.pallas_call(
        kernel,
        grid=(steps,),
        in_specs=[rows(8), rows(width), row_spec, rows(width), rows(width), rows(width), whole(scales.shape)],
        out_specs=rows(3 * width),
        out_shape=jax.ShapeDtypeStruct((tokens, 3 * width), LOW),
        scratch_shapes=[pltpu.VMEM((tile + 8, width), FULL), pltpu.VMEM((8, width), FULL)],
        compiler_params=pltpu.CompilerParams(vmem_limit_bytes=32 << 20),
        cost_estimate=pl.CostEstimate(flops=10 * tokens * width, bytes_accessed=16 << 20, transcendentals=0),
        name="project_grads",
    )(marks, *far(conv_grad, after, gate, value, open_grad), scales)


def pair_grads(place, left, right, cores, name):
    tokens, width = left.shape
    block = right.shape[1] // 4
    eighth = width // 8
    count = len(cores)
    step = 256

    def kernel(place_ref, left_ref, right_ref, *outs):
        at = pl.program_id(0)
        for n in range(block // step):
            total = narrow(contract_rows(left_ref[...], right_ref[:, n * step : (n + 1) * step]))
            for c in range(count):
                @pl.when(at // 2 == c)
                def _():
                    for i in range(8):
                        outs[c][0, place_ref[2 + i], :, n * step : (n + 1) * step] = total[i * eighth : (i + 1) * eighth]

    def column(i, place_ref):
        return (0, place_ref[14 + 2 * cores[0] + i])

    def out_spec(c):
        return pl.BlockSpec(
            (1, 8, eighth, block), lambda i, place_ref: (jnp.clip(i - 2 * c, 0, 1), 0, 0, 0)
        )

    return pl.pallas_call(
        kernel,
        grid_spec=pltpu.PrefetchScalarGridSpec(
            num_scalar_prefetch=1,
            grid=(2 * count,),
            in_specs=[
                pl.BlockSpec((tokens, width), lambda i, place_ref: (0, 0), pipeline_mode=pl.Buffered(1)),
                pl.BlockSpec((tokens, block), column),
            ],
            out_specs=[out_spec(c) for c in range(count)],
        ),
        out_shape=[jax.ShapeDtypeStruct((2, 8, eighth, block), LOW)] * count,
        compiler_params=pltpu.CompilerParams(vmem_limit_bytes=32 << 20),
        cost_estimate=pl.CostEstimate(
            flops=count * 4 * tokens * width * block, bytes_accessed=8 << 20, transcendentals=0
        ),
        name=name,
    )(place, left, right)


def mixer_backward(project_grad, in_weight, hidden, residual_grad, sums, scales):
    tokens, width = hidden.shape
    tile = 256
    steps = tokens // tile

    def kernel(grad_ref, in_ref, hidden_ref, residual_ref, sums_ref, scale_ref, input_out, sums_out):
        @pl.when(pl.program_id(0) == 0)
        def _():
            sums_out[...] = sums_ref[...]

        normed_grad = contract_cols(grad_ref[...], in_ref[...])
        source = hidden_ref[...].astype(FULL)
        inverse = lax.rsqrt(jnp.mean(source * source, axis=1, keepdims=True) + EPS)
        sums_out[0:1, :] += jnp.sum(normed_grad * (source * inverse), axis=0, keepdims=True)
        scaled = scale_ref[0:1, :] * normed_grad
        lean = (inverse * inverse * inverse) * jnp.mean(scaled * source, axis=1, keepdims=True)
        input_out[...] = narrow(residual_ref[...] + inverse * scaled - source * lean)

    def rows(last):
        return pl.BlockSpec((tile, last), lambda i: (i, 0))

    small = pl.BlockSpec((8, width), lambda i: (0, 0))
    return pl.pallas_call(
        kernel,
        grid=(steps,),
        in_specs=[rows(3 * width), whole(in_weight.shape), rows(width), rows(width), small, whole(scales.shape)],
        out_specs=[rows(width), small],
        out_shape=[jax.ShapeDtypeStruct((tokens, width), LOW), jax.ShapeDtypeStruct((8, width), FULL)],
        compiler_params=pltpu.CompilerParams(vmem_limit_bytes=32 << 20),
        cost_estimate=pl.CostEstimate(flops=6 * tokens * width * width, bytes_accessed=20 << 20, transcendentals=0),
        name="mixer_backward",
    )(project_grad, in_weight, hidden, residual_grad, sums, scales)


def plain(
    hidden_in,
    mixer_gain,
    in_weight,
    conv_kernel,
    out_weight,
    feed_gain,
    gate_weight,
    up_weight,
    down_weight,
    document_lengths,
    valid_tokens,
    cotangent,
):
    row_count, span_length, model_width = hidden_in.shape
    token_count = row_count * span_length
    offset = lax.axis_index("seq") * span_length
    positions = offset + jnp.arange(span_length, dtype=jnp.int32)
    starts = jnp.cumsum(document_lengths, axis=1) - document_lengths
    is_start = jnp.any(positions[None, :, None] == starts[:, None, :], axis=2)
    before = jnp.any((positions - 1)[None, :, None] == starts[:, None, :], axis=2)
    keep_one = (1.0 - is_start.astype(jnp.float32))[:, :, None]
    keep_two = keep_one * (1.0 - before.astype(jnp.float32))[:, :, None]
    valid_mask = (
        (positions[None, :] < valid_tokens[:, None]).astype(jnp.float32).reshape(token_count, 1)
    )
    mixer_scale = mixer_gain.astype(jnp.float32)
    feed_scale = feed_gain.astype(jnp.float32)
    kernel = conv_kernel.astype(jnp.float32)
    source = hidden_in.astype(jnp.float32).reshape(token_count, model_width)
    inverse_one = lax.rsqrt(jnp.mean(source * source, axis=1, keepdims=True) + EPS)
    normed = (source * inverse_one * mixer_scale).astype(jnp.bfloat16)
    project = jnp.dot(normed, in_weight, preferred_element_type=jnp.float32)
    input_gate = project[:, :model_width]
    output_gate = project[:, model_width : 2 * model_width]
    values = project[:, 2 * model_width :]
    product = (
        (input_gate * values).astype(jnp.bfloat16).reshape(row_count, span_length, model_width)
    )
    rim_values = passed_along(product[:, span_length - 2 :, :], "seq", 1)
    extended = jnp.concatenate([rim_values, product], axis=1).astype(jnp.float32)
    tap_zero = extended[:, 2:, :]
    tap_one = keep_one * extended[:, 1:-1, :]
    tap_two = keep_two * extended[:, :-2, :]
    conv_out = (kernel[:, 0] * tap_zero + kernel[:, 1] * tap_one + kernel[:, 2] * tap_two).reshape(
        token_count, model_width
    )
    mixed_in = (output_gate * conv_out).astype(jnp.bfloat16)
    mixer_out = jnp.dot(mixed_in, out_weight, preferred_element_type=jnp.float32)
    residual = source + valid_mask * mixer_out
    inverse_two = lax.rsqrt(jnp.mean(residual * residual, axis=1, keepdims=True) + EPS)
    normed_two = (residual * inverse_two * feed_scale).astype(jnp.bfloat16)
    gate_pre = jnp.dot(normed_two, gate_weight, preferred_element_type=jnp.float32)
    up_pre = jnp.dot(normed_two, up_weight, preferred_element_type=jnp.float32)
    sigmoid_gate = jax.nn.sigmoid(gate_pre)
    activation = (gate_pre * sigmoid_gate * up_pre).astype(jnp.bfloat16)
    feed_out = jnp.dot(activation, down_weight, preferred_element_type=jnp.float32)
    output = (
        (residual + valid_mask * feed_out)
        .astype(jnp.bfloat16)
        .reshape(row_count, span_length, model_width)
    )
    upstream = cotangent.astype(jnp.float32).reshape(token_count, model_width)
    feed_grad = (valid_mask * upstream).astype(jnp.bfloat16)
    down_grad = contract_rows(activation, feed_grad)
    activation_grad = contract_cols(feed_grad, down_weight)
    up_grad = (activation_grad * gate_pre * sigmoid_gate).astype(jnp.bfloat16)
    gate_grad = (
        activation_grad * up_pre * sigmoid_gate * (1.0 + gate_pre * (1.0 - sigmoid_gate))
    ).astype(jnp.bfloat16)
    gate_wgrad = contract_rows(normed_two, gate_grad)
    up_wgrad = contract_rows(normed_two, up_grad)
    normed_two_grad = contract_cols(gate_grad, gate_weight) + contract_cols(up_grad, up_weight)
    feed_gain_grad = jnp.sum(normed_two_grad * residual * inverse_two, axis=0)
    scaled_two = feed_scale * normed_two_grad
    residual_grad = (
        upstream
        + inverse_two * scaled_two
        - residual
        * (inverse_two * inverse_two * inverse_two)
        * jnp.mean(scaled_two * residual, axis=1, keepdims=True)
    )
    feed_gain_part, gate_part, up_part, down_part = (
        lax.psum_scatter(
            feed_gain_grad.astype(jnp.bfloat16), "seq", scatter_dimension=0, tiled=True
        ).astype(jnp.float32),
        lax.psum_scatter(
            gate_wgrad.astype(jnp.bfloat16), "seq", scatter_dimension=0, tiled=True
        ).astype(jnp.float32),
        lax.psum_scatter(
            up_wgrad.astype(jnp.bfloat16), "seq", scatter_dimension=0, tiled=True
        ).astype(jnp.float32),
        lax.psum_scatter(
            down_grad.astype(jnp.bfloat16), "seq", scatter_dimension=0, tiled=True
        ).astype(jnp.float32),
    )
    gate_part, up_part, down_part = (
        lax.psum_scatter(
            gate_part.astype(jnp.bfloat16), "row", scatter_dimension=1, tiled=True
        ).astype(jnp.float32),
        lax.psum_scatter(
            up_part.astype(jnp.bfloat16), "row", scatter_dimension=1, tiled=True
        ).astype(jnp.float32),
        lax.psum_scatter(
            down_part.astype(jnp.bfloat16), "row", scatter_dimension=1, tiled=True
        ).astype(jnp.float32),
    )
    mixer_grad = (valid_mask * residual_grad).astype(jnp.bfloat16)
    out_wgrad = contract_rows(mixed_in, mixer_grad)
    mixed_grad = contract_cols(mixer_grad, out_weight)
    output_gate_grad = mixed_grad * conv_out
    conv_grad = (mixed_grad * output_gate).reshape(row_count, span_length, model_width)
    kernel_grad = jnp.stack(
        [
            jnp.sum(conv_grad * tap_zero, axis=(0, 1)),
            jnp.sum(conv_grad * tap_one, axis=(0, 1)),
            jnp.sum(conv_grad * tap_two, axis=(0, 1)),
        ],
        axis=1,
    )
    grad_zero = kernel[:, 0] * conv_grad
    grad_one = keep_one * kernel[:, 1] * conv_grad
    grad_two = keep_two * kernel[:, 2] * conv_grad
    extended_grad = (
        jnp.pad(grad_zero, ((0, 0), (2, 0), (0, 0)))
        + jnp.pad(grad_one, ((0, 0), (1, 1), (0, 0)))
        + jnp.pad(grad_two, ((0, 0), (0, 2), (0, 0)))
    )
    returned = passed_along(extended_grad[:, :2, :], "seq", -1)
    product_grad = extended_grad[:, 2:, :] + jnp.pad(
        returned, ((0, 0), (span_length - 2, 0), (0, 0))
    )
    flat_grad = product_grad.reshape(token_count, model_width)
    project_grad = jnp.concatenate(
        [flat_grad * values, output_gate_grad, flat_grad * input_gate], axis=1
    ).astype(jnp.bfloat16)
    in_wgrad = contract_rows(normed, project_grad)
    normed_grad = contract_cols(project_grad, in_weight)
    mixer_gain_grad = jnp.sum(normed_grad * source * inverse_one, axis=0)
    scaled_one = mixer_scale * normed_grad
    input_grad = (
        residual_grad
        + inverse_one * scaled_one
        - source
        * (inverse_one * inverse_one * inverse_one)
        * jnp.mean(scaled_one * source, axis=1, keepdims=True)
    )
    input_grad = input_grad.astype(jnp.bfloat16).reshape(row_count, span_length, model_width)
    mixer_gain_part, in_part, kernel_part, out_part = (
        lax.psum_scatter(
            mixer_gain_grad.astype(jnp.bfloat16), "seq", scatter_dimension=0, tiled=True
        ).astype(jnp.float32),
        lax.psum_scatter(
            in_wgrad.astype(jnp.bfloat16), "seq", scatter_dimension=0, tiled=True
        ).astype(jnp.float32),
        lax.psum_scatter(
            kernel_grad.astype(jnp.bfloat16), "seq", scatter_dimension=0, tiled=True
        ).astype(jnp.float32),
        lax.psum_scatter(
            out_wgrad.astype(jnp.bfloat16), "seq", scatter_dimension=0, tiled=True
        ).astype(jnp.float32),
    )
    in_part, out_part = (
        lax.psum_scatter(
            in_part.astype(jnp.bfloat16), "row", scatter_dimension=1, tiled=True
        ).astype(jnp.float32),
        lax.psum_scatter(
            out_part.astype(jnp.bfloat16), "row", scatter_dimension=1, tiled=True
        ).astype(jnp.float32),
    )
    mixer_gain_part, feed_gain_part, kernel_part = lax.psum(
        (mixer_gain_part, feed_gain_part, kernel_part), "row"
    )
    return (
        output,
        input_grad,
        mixer_gain_part,
        in_part,
        kernel_part,
        out_part,
        feed_gain_part,
        gate_part,
        up_part,
        down_part,
    )


def joined(keeps, takes, name):
    count = len(keeps)
    shape = (keeps[0].shape[1], count) + keeps[0].shape[2:]

    def kernel(*refs):
        for n in range(count):
            for side in range(2):
                refs[2 * count + side][0, n] = narrow(wide(refs[n][side, 0], refs[count + n][side, 0]))

    return pl.pallas_call(
        kernel,
        grid=(shape[0],),
        in_specs=[pl.BlockSpec((2, 1) + shape[2:], lambda i: (0, i, 0, 0))] * (2 * count),
        out_specs=[pl.BlockSpec((1,) + shape[1:], lambda i: (i, 0, 0, 0))] * 2,
        out_shape=[pltpu.HBM(shape, LOW)] * 2,
        compiler_params=pltpu.CompilerParams(vmem_limit_bytes=32 << 20),
        name=name,
    )(*far(*keeps, *takes))


def side_by_side(keeps, takes, name):
    count = len(keeps)
    widths = [keep.shape[-1] for keep in keeps]
    shape = (keeps[0].shape[0] // 2, keeps[0].shape[-2], sum(widths))

    def kernel(*refs):
        for n in range(count):
            at = pl.ds(sum(widths[:n]), widths[n])
            for side in range(2):
                refs[2 * count + side][0, :, at] = narrow(wide(refs[n][side], refs[count + n][side]))

    def spec(first, last):
        return pl.BlockSpec((first, shape[1], last), lambda i: (i, 0, 0))

    return pl.pallas_call(
        kernel,
        grid=(shape[0],),
        in_specs=[spec(2, size) for size in widths] * 2,
        out_specs=[spec(1, shape[2])] * 2,
        out_shape=[pltpu.HBM(shape, LOW)] * 2,
        compiler_params=pltpu.CompilerParams(vmem_limit_bytes=32 << 20),
        name=name,
    )(*far(*keeps, *takes))


def last_sums(keeps, takes):
    counts = [keep.shape[0] for keep in keeps]
    height, part = keeps[0].shape[1:]
    shape = (height, sum(counts) // 2 * part)

    def kernel(*refs):
        n = 0
        for i, count in enumerate(counts):
            for k in range(count):
                refs[2 * len(counts) + n % 2][:, pl.ds(n // 2 * part, part)] = wide(
                    refs[i][k], refs[len(counts) + i][k]
                )
                n += 1

    rows = height // 2
    return pl.pallas_call(
        kernel,
        grid=(2,),
        in_specs=[pl.BlockSpec((count, rows, part), lambda i: (0, i, 0)) for count in counts] * 2,
        out_specs=[pl.BlockSpec((rows, shape[1]), lambda i: (i, 0))] * 2,
        out_shape=[pltpu.HBM(shape, FULL)] * 2,
        compiler_params=pltpu.CompilerParams(vmem_limit_bytes=32 << 20),
        name="last_sums",
    )(*far(*keeps, *takes))


def fast(
    hidden_in,
    mixer_gain,
    in_weight,
    conv_kernel,
    out_weight,
    feed_gain,
    gate_weight,
    up_weight,
    down_weight,
    document_lengths,
    valid_tokens,
    cotangent,
):
    row_count, span_length, model_width = hidden_in.shape
    token_count = row_count * span_length
    hidden_width = gate_weight.shape[1]
    block = hidden_width // 4
    chunks = 3
    part = block // chunks
    seq = lax.axis_index("seq")
    row = lax.axis_index("row")
    row_x, core = row // 2, row % 2
    seq_y, seq_z0, seq_z1 = seq % 2, (seq // 2) % 2, seq // 4
    place = jnp.stack(
        [row ^ 2, row]
        + [i ^ seq ^ 7 for i in range(8)]
        + [1 - row_x, row_x, 1 - ((1 - row_x) ^ seq_z1), 1 - (row_x ^ seq_z1)]
        + [row ^ 3, row ^ 1, row ^ 2, row]
    ).astype(jnp.int32)
    positions = seq * span_length + jnp.arange(span_length, dtype=jnp.int32)
    starts = jnp.cumsum(document_lengths, axis=1) - document_lengths

    def unstarted(shift):
        return 1.0 - jnp.any((positions + shift)[None, :, None] == starts[:, None, :], axis=2).astype(FULL)

    here, last, one_on, two_on = (unstarted(shift) for shift in (0, -1, 1, 2))
    valid = (positions[None, :] < valid_tokens[:, None]).astype(FULL)
    blank = jnp.zeros_like(valid)
    marks = jnp.stack([here, here * last, valid, one_on, two_on * one_on, blank, blank, blank], axis=2).reshape(
        token_count, 8
    )
    valid_mask = marks[:, 2:3]
    scales = jnp.concatenate(
        [mixer_gain[None], feed_gain[None], conv_kernel.T, jnp.zeros((3, model_width), conv_kernel.dtype)]
    ).astype(FULL)
    hidden = hidden_in.reshape(token_count, model_width)
    upstream = cotangent.reshape(token_count, model_width)
    rim = passed_along(hidden_in[:, span_length - 2 :, :], "seq", 1)
    rim = jnp.pad(rim, ((0, 0), (MARGIN - 2, 0), (0, 0))).reshape(row_count * MARGIN, model_width)
    feed_grad = narrow(valid_mask * upstream.astype(FULL))
    other_grad = swapped(feed_grad, "row", 1)
    normed, input_gate, output_gate, values, product, mixed_in, residual, normed_two, before = mixer_forward(
        marks, hidden, rim, in_weight, out_weight, scales
    )
    other_normed = swapped(normed_two, "row", 1)

    def chunk_grads(start, chunk):
        return feed_chunk(
            start, normed_two, other_normed, feed_grad, other_grad, gate_weight, up_weight, down_weight, chunk, chunks
        )

    def sent(made):
        gs, us, ds = made[3], made[5], made[7]
        return swapped(gs, "seq", 2), swapped(us, "seq", 1), swapped(ds, "row", 2)

    def together(*values):
        return lax.optimization_barrier(values)

    def follow(value, *ahead):
        return lax.optimization_barrier((value,) + ahead)[0]

    def first_sums(made, taken):
        pairs = ((made[4], taken[0]), (made[6], taken[1]))
        halves = [narrow(wide(keep[i], take[i])) for keep, take in pairs for i in range(2)]
        return halves + [narrow(wide(made[8], taken[2]))]

    def second(sums):
        return swapped(sums[0], "seq", 1), swapped(sums[2], "seq", 2)

    def split(keep, take, at):
        return [
            narrow(wide(lax.index_in_dim(keep, i, at, False), lax.index_in_dim(take, i, at, False))) for i in range(2)
        ]

    made0 = chunk_grads(place, 0)
    taken0 = sent(made0)
    made1, taken0 = together(chunk_grads(follow(place, made0[0]), 1), taken0)
    taken1 = sent(made1)
    sums0 = first_sums(made0, taken0)
    second0 = second(sums0)
    made2, taken1, second0 = together(chunk_grads(follow(place, sums0), 2), taken1, second0)
    taken2 = sent(made2)
    sums1 = first_sums(made1, taken1)
    second1 = second(sums1)
    acts, gates, ups = ([one[i] for one in (made0, made1, made2)] for i in range(3))
    (own_ntg, give_ntg), taken2, second1 = together(
        feed_sum(follow(place, sums1), [gates, ups], [gate_weight, up_weight], True, block, "normed_two_grad"),
        taken2,
        second1,
    )
    take_ntg = swapped(give_ntg, "row", 1)
    sums2 = first_sums(made2, taken2)
    second2 = second(sums2)
    third_give, third_keep = joined([sums0[1], sums0[3], sums1[1], sums1[3]], second0 + second1, "third_sums")
    third_take = swapped(third_give, "row", 2)

    (residual_grad, mixer_grad, open_grad, conv_grad, sums), second2 = together(
        mixer_middle(
            follow(marks, sums2, third_keep), own_ntg, take_ntg, residual, upstream, product, before, output_gate,
            out_weight, scales,
        ),
        second2,
    )
    after = passed_along(conv_grad.reshape(row_count, span_length, model_width)[:, :2, :], "seq", -1)
    late_give, late_keep = joined([sums2[1], sums2[3]], second2, "late_sums")
    late_take = swapped(late_give, "row", 2)
    down = jnp.concatenate(follow([sums0[4], sums1[4], sums2[4]], mixer_grad), axis=1)
    low_half, high_half = down[:, : block // 2], down[:, block // 2 :]
    down_keep = jnp.where(seq_y == 0, low_half, high_half)
    down_give = jnp.where(seq_y == 0, high_half, low_half)

    (out_give, out_keep), after, third_take, down_give = together(
        pair_grads(follow(place, late_keep, down_keep, down_give), mixed_in, mixer_grad, (0, 1), "out_grads"),
        after,
        third_take,
        down_give,
    )
    after = jnp.pad(after, ((0, 0), (0, 6), (0, 0))).reshape(row_count * 8, model_width)
    fourth_give, fourth_keep = split(third_keep, third_take, 0)
    fourth_take = swapped(fourth_give, "seq", 4)
    down_give, out_give = follow((down_give, out_give), fourth_give)
    down_takes = [swapped(down_give[0], "seq", 1)]
    out_take = swapped(out_give, "row", 1)

    project_grad = project_grads(
        follow(marks, out_keep, fourth_give, fourth_keep), conv_grad, after, input_gate, values, open_grad, scales
    )
    (in_give,), out_take, late_take, down_takes, fourth_take = together(
        pair_grads(place, normed, project_grad, (0,), "in_grads_give"), out_take, late_take, down_takes, fourth_take
    )
    in_take = swapped(in_give, "row", 1)
    out_give, out_keep = split(out_keep, out_take, 0)
    out_take = swapped(out_give, "row", 2)
    down_takes.append(swapped(follow(down_give[1], out_give), "seq", 1))
    late_give, late_keep = split(late_keep, late_take, 0)
    down_first = narrow(wide(down_keep[0], down_takes[0]))
    down_take = swapped(down_first, "seq", 4)

    (in_keep,), in_take, out_take, down_takes = together(
        pair_grads(
            follow(place, in_give, out_give, out_keep, late_give, late_keep, down_first), normed, project_grad, (1,), "in_grads_keep"
        ),
        in_take,
        out_take,
        down_takes,
    )
    half = in_keep.shape[-1] // 2
    left_give, left_keep = split(in_keep[..., :half], in_take[..., :half], 0)
    left_take = swapped(left_give, "row", 2)
    eighths = (2, 4, 2, model_width // 8, half)
    right_give, right_keep = split(in_keep[..., half:].reshape(eighths), in_take[..., half:].reshape(eighths), 2)
    right_take = swapped(right_give, "seq", 1)
    down_keep = narrow(wide(down_keep[1], down_takes[1]))

    (input_grad, small), left_take, right_take, down_take = together(
        mixer_backward(
            follow(project_grad, left_give, left_keep, right_give, right_keep, down_keep),
            in_weight, hidden, residual_grad, sums, scales,
        ),
        left_take,
        right_take,
        down_take,
    )
    left_give, left_keep = side_by_side([left_keep, out_keep], [left_take, out_take], "y_sums")
    left_take = swapped(left_give, "seq", 1)
    right_give, right_keep = split(right_keep, follow(right_take, left_give), 0)
    right_take = swapped(right_give, "row", 2)
    small_take = swapped(small, "row", 1)
    down = narrow(wide(down_keep, follow(down_take, left_give)))
    holder = [[(r & 1) == ((s >> 1) & 1) for r in range(4)] for s in range(8)]
    down_take = lax.ppermute(
        down,
        ("seq", "row"),
        [(s * 4 + r, (s ^ 2) * 4 + r) for s in range(8) for r in range(4) if not holder[s][r]],
    )
    late_take = swapped(follow(late_give, down), "seq", 4)

    (give_feed,), left_take, right_take, small_take, down_take, late_take = together(
        feed_sum(
            follow(place, left_give, left_keep, right_give, right_keep, down),
            [acts], [down_weight], False, block, "feed_out_give", (1,),
        ),
        left_take,
        right_take,
        small_take,
        down_take,
        late_take,
    )
    give, keep = side_by_side([left_keep, right_keep], [left_take, right_take], "z_sums")
    take = swapped(give, "seq", 2)
    take_feed = swapped(give_feed, "row", 1)
    small = small + small_take
    small_take = swapped(small, "row", 2)
    down = wide(down, follow(down_take, give))
    quarter = model_width // 4
    down_own = jnp.where(core == 0, down[:, :quarter], down[:, quarter:])
    down_other = narrow(jnp.where(core == 0, down[:, quarter:], down[:, :quarter]))
    down_other = lax.ppermute(
        down_other,
        ("seq", "row"),
        [(s * 4 + r, s * 4 + (r ^ 1)) for s in range(8) for r in range(4) if holder[s][r]],
    )

    (own_feed,), take, take_feed, small_take, down_other = together(
        feed_sum(
            follow(place, give, keep, small, down_own), [acts], [down_weight], False, block, "feed_out_keep", (0,)
        ),
        take,
        take_feed,
        small_take,
        down_other,
    )
    give, keep = split(keep, take, 0)
    take = swapped(give, "seq", 4)
    small = small + small_take
    small_take = swapped(small, "seq", 1)
    (gate_part, up_part), small_take = together(
        last_sums(*follow(([fourth_keep, late_keep], [fourth_take, late_take]), give)), small_take
    )
    small = small + small_take
    small_take = swapped(small, "seq", 2)
    output = narrow(residual + valid_mask * wide(own_feed, follow(take_feed, small)))
    output, small_take = together(output, small_take)
    output = output.reshape(row_count, span_length, model_width)
    small = small + small_take
    small_take = swapped(small, "seq", 4)
    down_part = jnp.where(core == seq_z0, down_own, down_other.astype(jnp.float32))
    input_grad = input_grad.reshape(row_count, span_length, model_width)
    both_part = wide(keep, take)
    past = both_part.shape[1] - half
    in_part = jnp.concatenate([both_part[:, :half], both_part[:, past:]], axis=1)
    out_part = both_part[:, half:past]
    small = small + small_take
    small = lax.dynamic_slice_in_dim(small, seq * (model_width // 8), model_width // 8, 1)
    return (
        output,
        input_grad,
        small[0],
        in_part,
        small[2:5].T,
        out_part,
        small[1],
        gate_part,
        up_part,
        down_part,
    )


def local(*args):
    hidden_in, gate_weight = args[0], args[6]
    tokens = hidden_in.shape[0] * hidden_in.shape[1]
    width, hidden = gate_weight.shape
    tiled = lax.axis_size("seq") == 8 and lax.axis_size("row") == 4 and hidden % (4 * 3 * 128) == 0
    if tiled and width % 1024 == 0 and tokens % 512 == 0:
        return fast(*args)
    return plain(*args)


def solution(mesh):
    in_specs = (
        P("row", "seq", None),
        P(),
        P(),
        P(),
        P(),
        P(),
        P(),
        P(),
        P(),
        P("row", None),
        P("row"),
        P("row", "seq", None),
    )
    out_specs = (
        P("row", "seq", None),
        P("row", "seq", None),
        P("seq"),
        P("seq", "row"),
        P("seq", None),
        P("seq", "row"),
        P("seq"),
        P("seq", "row"),
        P("seq", "row"),
        P("seq", "row"),
    )
    return jax.shard_map(local, mesh=mesh, in_specs=in_specs, out_specs=out_specs, check_vma=False)
```
